32 devices in a mesh: dp: 2 (over y), expert: 16 (over z, x, core).
Axes of the slice: x: 2, y: 2, z: 4, core: 2. Of those that a mesh axis runs over, the one named last changes fastest.
Arguments:
- out_grad: bfloat16 [3072, 2048], P('expert', 'dp'), may hold values from -6 to 6
- routes: int32 [3072, 8], P('expert'), may hold values from 0 to 15, all different within a row; in each aligned block of 192 rows (0 to 191, 192 to 383, ...) at most 144 rows name the same one
- gate_codes: int32 [3072, 8], P('expert'), may hold values from 1 to 255
- w_gate: bfloat16 [16, 2048, 384], P('expert', 'dp'), may hold values from -0.125 to 0.125
- w_up: bfloat16 [16, 2048, 384], P('expert', 'dp'), may hold values from -0.125 to 0.125
- w_down: bfloat16 [16, 384, 2048], P('expert', None, 'dp'), may hold values from -0.3125 to 0.3125
- saved_inputs: bfloat16 [16, 2304, 2048], P('expert', None, 'dp'), may hold values from -6 to 6
- saved_gate: bfloat16 [16, 2304, 384], P('expert'), may hold values from -6 to 6
- saved_up: bfloat16 [16, 2304, 384], P('expert'), may hold values from -6 to 6
Outputs:
- token_grads: bfloat16 [3072, 2048], P('expert', 'dp')
- weight_grads: bfloat16 [16, 2048, 1152], P('expert', 'dp')
The draws below stay inside these ranges and needn't reach their ends.
Inputs may be any that keep to these rules, and one draw needn't show every extreme that they name: `routes`: each token names 8 different experts; in each block of 192 tokens no expert is named by more than 144 tokens, a bound that some block reaches.
All inputs are finite; a program needn't handle non-finite values.
Results may differ from the reference program's by a relative error of at most 0.0065.
Values may be sent and summed in bfloat16 or wider, within the bound.
No kernel may reach another device: no remote copies, remote signals or barrier semaphores. Data moves between devices by JAX's collectives and lax.ppermute only.
A program may use at most 128 MiB of HBM per device.

```python
import math
import jax
import jax.numpy as jnp
import numpy as np
from jax import lax

D = 2048
HIDDEN_SIZE = 384
TOPK = 8
TOK_DEV = 192
EXPERTS = 16
CAP = 144
SLOTS = 2304
TOKENS = 3072
N_EXPERT = 16


def touch_ends(result, own_key, low, top_value):
    place = [jax.random.randint(jax.random.fold_in(own_key, axis), (), 0, length) for axis, length in enumerate(result.shape)]
    widest = result.shape.index(max(result.shape))
    neighbour = place[:widest] + [(place[widest] + 1) % result.shape[widest]] + place[widest + 1:]
    return result.at[tuple(place)].set(low).at[tuple(neighbour)].set(top_value)


def block_levels(key, shape, pieces, least, top_value):
    factor_of, own = 1.0, jax.random.fold_in(key, 6)
    for dim, shards_of in pieces:
        draws = jnp.exp(jax.random.uniform(jax.random.fold_in(own, dim), (shards_of,), jnp.float32, least / len(pieces), top_value / len(pieces)))
        factor_of = factor_of * jnp.repeat(draws, shape[dim] // shards_of).reshape([-1 if axis == dim else 1 for axis in range(len(shape))])
    return factor_of


def deal_out(key, own, number, rows, amount, top, bound, skew):
    ranking = jax.random.permutation(key, amount)
    heavy_load, ordinary = load_shares(amount, rows * top, bound, skew, True), load_shares(amount, rows * top, bound, skew, False)
    places = jnp.arange(amount)

    def named(tallies, offset_by):
        used = int((tallies > 0).sum())
        fixed = max(1, used // 4)
        moved = fixed + (places - fixed + offset_by * (used - fixed)) % max(1, amount - fixed)
        return jnp.zeros((amount,), jnp.int32).at[ranking[jnp.where(places < fixed, places, moved)]].set(jnp.asarray(tallies, jnp.int32))

    tallies = jnp.where(number % 4 == 0, named(heavy_load, number // 4), named(ordinary, number - number // 4 - 1))
    mixed = jax.random.permutation(jax.random.fold_in(own, 3), amount)
    giver, receiver = mixed[0:amount // 2 * 2:2], mixed[1:amount // 2 * 2:2]
    margin = jnp.minimum(tallies[giver] - 1, bound - tallies[receiver]) // 2
    margin = jnp.where((giver == ranking[0]) | (receiver == ranking[0]) | (tallies[receiver] == 0), 0, jnp.maximum(margin, 0))
    moved = jax.random.randint(jax.random.fold_in(own, 4), (amount // 2,), 0, 1 << 20) % (margin + 1)
    tallies = tallies.at[giver].add(-moved).at[receiver].add(moved)
    members = jnp.searchsorted(jnp.cumsum(tallies), jnp.arange(rows * top), side="right").astype(jnp.int32)
    grid = members.reshape(top, rows).T
    grid = grid[jax.random.permutation(jax.random.fold_in(own, 1), rows)]
    offset_by = jax.random.randint(jax.random.fold_in(own, 2), (rows, 1), 0, top)
    return jnp.take_along_axis(grid, (jnp.arange(top)[None, :] + offset_by) % top, axis=1)


def load_shares(count, total, reach, lean, full):
    portions = [(1 << 20) // math.isqrt(standing ** lean) + 1 for standing in range(1, count + 1)]
    largest = reach if full else min(reach, max(-(-total // count), total * portions[0] // sum(portions)))
    least = 1 if total - largest >= count - 1 else 0
    given, surplus = [largest] + [least] * (count - 1), total - largest - least * (count - 1)
    while surplus > 0:
        candidates = [i for i in range(1, count) if given[i] < largest] or [i for i in range(1, count) if given[i] < reach]
        mass, budget = sum([portions[i] for i in candidates]), surplus
        for i in candidates:
            addition = min(reach - given[i], max(1, budget * portions[i] // mass), surplus)
            given[i] = given[i] + addition
            surplus = surplus - addition
    return np.array(given)


def bell_draw(own_key, extent, spread, most, cuts=(), kind=jnp.bfloat16):
    values = spread * jax.random.normal(own_key, extent, jnp.float32)
    if cuts:
        values = values * block_levels(own_key, extent, cuts, -0.22, 0.18)
    return jnp.clip(values, -most, most).astype(kind)


def setup_inputs(seed: int = 0) -> dict:
    arg_keys = jax.random.split(jax.random.key(seed), 10)
    out_grad = bell_draw(arg_keys[0], (TOKENS, D), 1.0, 6.0, ((0, 16), (1, 2)))
    routes_keys = jax.random.split(jax.random.fold_in(arg_keys[1], 1), TOKENS // TOK_DEV)
    routes_turns = jax.random.permutation(jax.random.fold_in(arg_keys[1], 3), TOKENS // TOK_DEV)
    routes = jax.vmap(lambda own, number: deal_out(jax.random.fold_in(arg_keys[1], 2), own, number, TOK_DEV, EXPERTS, TOPK, CAP, 2))(routes_keys, routes_turns).reshape((TOKENS, TOPK))
    gate_codes = touch_ends(jax.random.randint(arg_keys[2], (TOKENS, TOPK), 1, 256), jax.random.fold_in(arg_keys[2], 1), 1, 255).astype(jnp.int32)
    w_gate = bell_draw(arg_keys[3], (EXPERTS, D, HIDDEN_SIZE), D ** -0.5, 0.125, ((0, 16), (1, 2)))
    w_up = bell_draw(arg_keys[4], (EXPERTS, D, HIDDEN_SIZE), D ** -0.5, 0.125, ((0, 16), (1, 2)))
    w_down = bell_draw(arg_keys[5], (EXPERTS, HIDDEN_SIZE, D), HIDDEN_SIZE ** -0.5, 0.3125, ((0, 16), (2, 2)))
    saved_inputs = bell_draw(arg_keys[6], (EXPERTS, SLOTS, D), 1.0, 6.0, ((0, 16), (2, 2)))
    saved_gate = bell_draw(arg_keys[7], (EXPERTS, SLOTS, HIDDEN_SIZE), 1.0, 6.0, ((0, 16),))
    saved_up = bell_draw(arg_keys[8], (EXPERTS, SLOTS, HIDDEN_SIZE), 1.0, 6.0, ((0, 16),))
    return dict(out_grad=out_grad, routes=routes, gate_codes=gate_codes, w_gate=w_gate, w_up=w_up, w_down=w_down, saved_inputs=saved_inputs, saved_gate=saved_gate, saved_up=saved_up)


gate_unit = 0.00390625
loss_scale = 0.015625


def slot_position(route_rows):
    onehot = (route_rows[:, None] == jnp.arange(EXPERTS, dtype=jnp.int32)[None, :]).astype(jnp.int32)
    earlier = jnp.cumsum(onehot, axis=0) - onehot
    return jnp.sum(earlier * onehot, axis=1).astype(jnp.int32)


def contract_rows(left, right):
    return lax.dot_general(left, right, (((0,), (0,)), ((), ())), preferred_element_type=jnp.float32)


def contract_cols(left, right):
    return lax.dot_general(left, right, (((1,), (1,)), ((), ())), preferred_element_type=jnp.float32)


def one_expert(items):
    recv, gate_weight, up_weight, down_weight, inputs, gate_saved, up_saved = items
    gate_pre = gate_saved.astype(jnp.float32)
    up_pre = up_saved.astype(jnp.float32)
    sigmoid = jax.nn.sigmoid(gate_pre)
    silu = gate_pre * sigmoid
    dsilu = sigmoid * (1.0 + gate_pre * (1.0 - sigmoid))
    hidden = (silu * up_pre).astype(jnp.bfloat16)
    grad_hidden = contract_cols(recv, down_weight)
    grad_gate_pre = (grad_hidden * up_pre * dsilu).astype(jnp.bfloat16)
    grad_up_pre = (grad_hidden * silu).astype(jnp.bfloat16)
    slot_grads = contract_cols(grad_gate_pre, gate_weight) + contract_cols(grad_up_pre, up_weight)
    slot_grads = slot_grads.astype(jnp.bfloat16)
    part = jnp.concatenate([contract_rows(inputs, grad_gate_pre), contract_rows(inputs, grad_up_pre),
                            contract_rows(recv, hidden)], axis=1)
    return slot_grads, (part * loss_scale).astype(jnp.bfloat16)


def reference(out_grad, routes, gate_codes, w_gate, w_up, w_down, saved_inputs, saved_gate, saved_up):
    routes_blocks = routes.reshape(N_EXPERT, TOK_DEV * TOPK)
    position = jax.vmap(slot_position)(routes_blocks)
    source_ids = jnp.arange(N_EXPERT, dtype=jnp.int32)
    target = (routes_blocks * SLOTS + source_ids[:, None] * CAP + position).reshape(-1).astype(jnp.int32)
    gates = (gate_codes.astype(jnp.float32) * gate_unit).reshape(TOKENS, TOPK)
    scaled = (out_grad.astype(jnp.float32)[:, None, :] * gates[:, :, None]).astype(jnp.bfloat16)
    received = jnp.zeros((EXPERTS * SLOTS, D), jnp.bfloat16).at[target].set(scaled.reshape(-1, D))
    received = received.reshape(EXPERTS, SLOTS, D)
    slot_all, weight_grads = lax.map(one_expert, (received, w_gate, w_up, w_down, saved_inputs, saved_gate, saved_up))
    picked = slot_all.reshape(EXPERTS * SLOTS, D)[target].astype(jnp.float32)
    token_grads = picked.reshape(TOKENS, TOPK, D).sum(axis=1).astype(jnp.bfloat16)
    return token_grads, weight_grads
```

```python
import jax
import jax.numpy as jnp
from jax import lax
from jax.experimental import pallas as pl
from jax.experimental.pallas import tpu as pltpu
from jax.sharding import PartitionSpec as P

gate_unit = 0.00390625
loss_scale = 0.015625
f32 = jnp.float32
bf16 = jnp.bfloat16


def contract_rows(left, right):
    return lax.dot_general(left, right, (((0,), (0,)), ((), ())), preferred_element_type=f32)


def contract_cols(left, right):
    return lax.dot_general(left, right, (((1,), (1,)), ((), ())), preferred_element_type=f32)


def activation_grads(grad_hidden, gate_pre, up_pre):
    sigmoid = jax.nn.sigmoid(gate_pre)
    silu = gate_pre * sigmoid
    dsilu = sigmoid * (1.0 + gate_pre * (1.0 - sigmoid))
    grad_gate_pre = (grad_hidden * up_pre * dsilu).astype(bf16)
    grad_up_pre = (grad_hidden * silu).astype(bf16)
    return (grad_gate_pre, grad_up_pre)


def body_any(out_grad, routes, gate_codes, w_gate, w_up, w_down, saved_inputs, saved_gate, saved_up):
    owners = lax.axis_size("expert")
    slot_count = saved_gate.shape[1]
    capacity = slot_count // owners
    token_count = routes.shape[0]
    choice_count = routes.shape[1]
    flat_routes = routes.reshape(-1)
    onehot = (flat_routes[:, None] == jnp.arange(owners, dtype=jnp.int32)[None, :]).astype(jnp.int32)
    earlier = jnp.cumsum(onehot, axis=0) - onehot
    position = jnp.sum(earlier * onehot, axis=1)
    slot_index = (flat_routes * capacity + position).reshape(token_count, choice_count)
    gate_values = gate_codes.astype(f32) * gate_unit
    rows_iota = jnp.arange(slot_count, dtype=jnp.int32)[:, None]
    weighted = jnp.zeros((slot_count, token_count), f32)
    picks = jnp.zeros((slot_count, token_count), f32)
    for pick in range(choice_count):
        hit = rows_iota == slot_index[:, pick][None, :]
        weighted = weighted + jnp.where(hit, gate_values[:, pick][None, :], 0.0)
        picks = picks + hit.astype(f32)
    outgoing = jnp.dot(weighted.astype(bf16), out_grad, preferred_element_type=f32).astype(bf16)
    received = lax.all_to_all(outgoing, "expert", split_axis=0, concat_axis=0, tiled=True)
    hidden_share = lax.psum_scatter(
        contract_cols(received, w_down[0]), "dp", scatter_dimension=0, tiled=True
    )
    gate_pre = saved_gate[0].astype(f32)
    up_pre = saved_up[0].astype(f32)
    hidden = (gate_pre * jax.nn.sigmoid(gate_pre) * up_pre).astype(bf16)
    grad_hidden = lax.all_gather(hidden_share, "dp", axis=0, tiled=True)
    grad_gate_pre, grad_up_pre = activation_grads(grad_hidden, gate_pre, up_pre)
    slot_grads = contract_cols(grad_gate_pre, w_gate[0]) + contract_cols(grad_up_pre, w_up[0])
    returned = lax.all_to_all(
        slot_grads.astype(bf16), "expert", split_axis=0, concat_axis=0, tiled=True
    )
    token_grads = contract_rows(picks.astype(bf16), returned).astype(bf16)
    inputs_here = saved_inputs[0]
    part = jnp.concatenate(
        [
            contract_rows(inputs_here, grad_gate_pre),
            contract_rows(inputs_here, grad_up_pre),
            contract_rows(received, hidden),
        ],
        axis=1,
    )
    return (token_grads, (part * loss_scale).astype(bf16)[None])


def full(shape):
    return pl.BlockSpec(shape, lambda i, sc: (0,) * len(shape))


def dispatch_kernel(sc, t0, t1, t2, t3, pos, gate, wd, rec, share, share_out):
    group, own = sc[0], sc[1]
    cap = rec.shape[0] // 4
    for rel, tok in enumerate((t0, t1, t2, t3)):
        j = jnp.bitwise_xor(own, rel)
        src = group * 4 + j
        slot = lax.broadcasted_iota(jnp.int32, (cap, tok.shape[0]), 0)
        w = jnp.where(slot == pos[pl.ds(src, 1), :], gate[pl.ds(src, 1), :], 0.0).astype(bf16)
        rows = jnp.dot(w, tok[...], preferred_element_type=f32).astype(bf16)
        rec[pl.ds(pl.multiple_of(j * cap, 16), cap), :] = rows
    gh = contract_cols(rec[...], wd[...])
    share[...] = gh
    share_out[...] = gh.astype(bf16)


def dispatch(sc, tokens, pos, gate, wd, rows):
    tok, d = tokens[0].shape
    h = wd.shape[0]
    return pl.pallas_call(
        dispatch_kernel,
        out_shape=(
            jax.ShapeDtypeStruct((rows, d), bf16),
            jax.ShapeDtypeStruct((rows, h), f32),
            jax.ShapeDtypeStruct((rows, h), bf16),
        ),
        grid_spec=pltpu.PrefetchScalarGridSpec(
            num_scalar_prefetch=1,
            grid=(1,),
            in_specs=[full((tok, d))] * 4 + [full(pos.shape)] * 2 + [full(wd.shape)],
            out_specs=(full((rows, d)), full((rows, h)), full((rows, h))),
        ),
        cost_estimate=pl.CostEstimate(
            flops=2 * rows * d * (tok + h), bytes_accessed=8 * tok * d + 2 * rows * d, transcendentals=0
        ),
        name="dispatch",
    )(sc, *tokens, pos, gate, wd)


def combine_kernel(sc, share, peer, sg, su, pos, wg, wu, gp, hid, keep, send, slots):
    group, own = sc[0], sc[1]
    cap = share.shape[0] // 4
    h = share.shape[1]
    gh = share[...] + peer[...].astype(f32)
    gate_pre = sg[...].astype(f32)
    up_pre = su[...].astype(f32)
    sigmoid = jax.nn.sigmoid(gate_pre)
    silu = gate_pre * sigmoid
    dsilu = sigmoid * (1.0 + gate_pre * (1.0 - sigmoid))
    gg = (gh * up_pre * dsilu).astype(bf16)
    gu = (gh * silu).astype(bf16)
    gp[:, :h] = gg
    gp[:, h:] = gu
    hid[...] = (silu * up_pre).astype(bf16)
    slots[...] = (contract_cols(gg, wg[...]) + contract_cols(gu, wu[...])).astype(bf16)
    for rel in range(4):
        j = jnp.bitwise_xor(own, rel)
        src = group * 4 + j
        slot = lax.broadcasted_iota(jnp.int32, (cap, pos.shape[1]), 0)
        pick = jnp.where(slot == pos[pl.ds(src, 1), :], 1.0, 0.0).astype(bf16)
        rows = slots[pl.ds(pl.multiple_of(j * cap, 16), cap), :]
        back = contract_rows(pick, rows).astype(bf16)
        (send if rel & 1 else keep)[rel >> 1] = back


def combine(sc, share, peer, sg, su, pos, wg, wu):
    rows, h = share.shape
    d = wg.shape[0]
    tok = pos.shape[1]
    part = pl.BlockSpec((rows, h), lambda i, sc: (sc[0], 0))
    return pl.pallas_call(
        combine_kernel,
        out_shape=(
            jax.ShapeDtypeStruct((rows, 2 * h), bf16),
            jax.ShapeDtypeStruct((rows, h), bf16),
            jax.ShapeDtypeStruct((2, tok, d), bf16),
            jax.ShapeDtypeStruct((2, tok, d), bf16),
        ),
        grid_spec=pltpu.PrefetchScalarGridSpec(
            num_scalar_prefetch=1,
            grid=(1,),
            in_specs=[full((rows, h)), full((rows, h)), part, part, full(pos.shape), full((d, h)), full((d, h))],
            out_specs=(full((rows, 2 * h)), full((rows, h)), full((2, tok, d)), full((2, tok, d))),
            scratch_shapes=[pltpu.VMEM((rows, d), bf16)],
        ),
        cost_estimate=pl.CostEstimate(
            flops=2 * rows * d * (tok + 2 * h), bytes_accessed=8 * tok * d + 8 * rows * h, transcendentals=rows * h
        ),
        name="combine",
    )(sc, share, peer, sg, su, pos, wg, wu)


def weights_kernel(sc, x, *refs):
    n = (len(refs) - 1) // 3
    recs, gps, hids, out = refs[:n], refs[n : 2 * n], refs[2 * n : 3 * n], refs[-1]
    rows, wide = gps[0].shape
    left = right = None
    for k in range(n):
        xs = x[pl.ds(pl.multiple_of(sc[k] * rows, 16), rows), :]
        a = contract_rows(xs, gps[k][...])
        b = contract_rows(recs[k][...], hids[k][...])
        left = a if left is None else left + a
        right = b if right is None else right + b
    out[0, :, :wide] = (left * loss_scale).astype(bf16)
    out[0, :, wide:] = (right * loss_scale).astype(bf16)


def weight_sums(groups, x, recs, gps, hids):
    slots, d = x.shape
    rows, wide = gps[0].shape
    h = hids[0].shape[1]
    tile = 256
    return pl.pallas_call(
        weights_kernel,
        out_shape=jax.ShapeDtypeStruct((1, d, wide + h), bf16),
        grid_spec=pltpu.PrefetchScalarGridSpec(
            num_scalar_prefetch=1,
            grid=(d // tile,),
            in_specs=[pl.BlockSpec((slots, tile), lambda i, sc: (0, i))]
            + [pl.BlockSpec((rows, tile), lambda i, sc: (0, i))] * len(recs)
            + [full((rows, wide))] * len(gps)
            + [full((rows, h))] * len(hids),
            out_specs=pl.BlockSpec((1, tile, wide + h), lambda i, sc: (0, i, 0)),
        ),
        cost_estimate=pl.CostEstimate(
            flops=2 * slots * d * (wide + h), bytes_accessed=4 * slots * d + 4 * d * wide, transcendentals=0
        ),
        name="weights",
    )(groups, x, *recs, *gps, *hids)


def body_grid(out_grad, routes, gate_codes, w_gate, w_up, w_down, saved_inputs, saved_gate, saved_up):
    owners = lax.axis_size("expert")
    me = lax.axis_index("expert")
    to_core = [(i, i ^ 1) for i in range(owners)]
    to_x = [(i, i ^ 2) for i in range(owners)]
    ring = [(i, (i + 4) % owners) for i in range(owners)]
    rounds = owners // 4

    def send(v, perm):
        return lax.ppermute(v, "expert", perm)

    own_col = [out_grad]
    for _ in range(rounds - 1):
        own_col.append(send(own_col[-1], ring))
    other_col = [send(v, to_x) for v in own_col]
    own_col_c = [send(v, to_core) for v in own_col]
    other_col_c = [send(v, to_core) for v in other_col]

    named = jnp.concatenate([routes.T, gate_codes.T], axis=0)
    named = lax.all_gather(named, "expert", axis=0, tiled=False)
    choices = routes.shape[1]
    hit = named[:, :choices, :] == me
    mask = jnp.any(hit, axis=1)
    gate = jnp.sum(jnp.where(hit, named[:, choices:, :], 0), axis=1).astype(f32) * gate_unit
    tok = routes.shape[0]
    tri = (jnp.arange(tok)[:, None] < jnp.arange(tok)[None, :]).astype(bf16)
    pos = jnp.dot(mask.astype(bf16), tri, preferred_element_type=f32).astype(jnp.int32)
    pos = jnp.where(mask, pos, -1)

    slots = saved_gate.shape[1]
    rows = slots // rounds
    groups = (me // 4 + rounds - jnp.arange(rounds, dtype=jnp.int32)) % rounds
    scalars = [jnp.stack([groups[k], me % 4]).astype(jnp.int32) for k in range(rounds)]
    sg, su, wg, wu, wd = saved_gate[0], saved_up[0], w_gate[0], w_up[0], w_down[0]

    recs, gps, hids, kept = [], [], [], []
    for k in range(rounds):
        rec, share, share_out = dispatch(
            scalars[k], (own_col[k], own_col_c[k], other_col[k], other_col_c[k]), pos, gate, wd, rows
        )
        peer = lax.ppermute(share_out, "dp", [(0, 1), (1, 0)])
        gp, hid, keep, away = combine(scalars[k], share, peer, sg, su, pos, wg, wu)
        pair = keep.astype(f32) + send(away, to_core).astype(f32)
        near, far = pair[0], pair[1].astype(bf16)
        kept.append((near, send(far, to_x)))
        recs.append(rec)
        gps.append(gp)
        hids.append(hid)

    run = None
    for k in [1, 2, 3, 0]:
        near, arrived = kept[k]
        total = near + arrived.astype(f32)
        if run is not None:
            total = total + run.astype(f32)
        total = total.astype(bf16)
        run = send(total, ring) if k else None
    weight_grads = weight_sums(groups, saved_inputs[0], recs, gps, hids)
    return (total, weight_grads)


def solution(mesh):
    placed = (
        P("expert", "dp"),
        P("expert", None),
        P("expert", None),
        P("expert", "dp", None),
        P("expert", "dp", None),
        P("expert", None, "dp"),
        P("expert", None, "dp"),
        P("expert", None, None),
        P("expert", None, None),
    )
    small = mesh.shape["expert"] == 16 and mesh.shape["dp"] == 2
    return jax.shard_map(
        body_grid if small else body_any,
        mesh=mesh,
        in_specs=placed,
        out_specs=(P("expert", "dp"), P("expert", "dp", None)),
        check_vma=False,
    )
```

```python
import functools

import jax
import jax.numpy as jnp
from jax import lax
from jax.experimental import pallas as pl
from jax.experimental.pallas import tpu as pltpu
from jax.sharding import PartitionSpec as P

gate_unit = 0.00390625
loss_scale = 0.015625
f32 = jnp.float32
bf16 = jnp.bfloat16


def contract_rows(left, right):
    return lax.dot_general(left, right, (((0,), (0,)), ((), ())), preferred_element_type=f32)


def contract_cols(left, right):
    return lax.dot_general(left, right, (((1,), (1,)), ((), ())), preferred_element_type=f32)


def activation_grads(grad_hidden, gate_pre, up_pre):
    sigmoid = jax.nn.sigmoid(gate_pre)
    silu = gate_pre * sigmoid
    dsilu = sigmoid * (1.0 + gate_pre * (1.0 - sigmoid))
    grad_gate_pre = (grad_hidden * up_pre * dsilu).astype(bf16)
    grad_up_pre = (grad_hidden * silu).astype(bf16)
    return (grad_gate_pre, grad_up_pre)


def body_any(out_grad, routes, gate_codes, w_gate, w_up, w_down, saved_inputs, saved_gate, saved_up):
    owners = lax.axis_size("expert")
    slot_count = saved_gate.shape[1]
    capacity = slot_count // owners
    token_count = routes.shape[0]
    choice_count = routes.shape[1]
    flat_routes = routes.reshape(-1)
    onehot = (flat_routes[:, None] == jnp.arange(owners, dtype=jnp.int32)[None, :]).astype(jnp.int32)
    earlier = jnp.cumsum(onehot, axis=0) - onehot
    position = jnp.sum(earlier * onehot, axis=1)
    slot_index = (flat_routes * capacity + position).reshape(token_count, choice_count)
    gate_values = gate_codes.astype(f32) * gate_unit
    rows_iota = jnp.arange(slot_count, dtype=jnp.int32)[:, None]
    weighted = jnp.zeros((slot_count, token_count), f32)
    picks = jnp.zeros((slot_count, token_count), f32)
    for pick in range(choice_count):
        hit = rows_iota == slot_index[:, pick][None, :]
        weighted = weighted + jnp.where(hit, gate_values[:, pick][None, :], 0.0)
        picks = picks + hit.astype(f32)
    outgoing = jnp.dot(weighted.astype(bf16), out_grad, preferred_element_type=f32).astype(bf16)
    received = lax.all_to_all(outgoing, "expert", split_axis=0, concat_axis=0, tiled=True)
    hidden_share = lax.psum_scatter(
        contract_cols(received, w_down[0]), "dp", scatter_dimension=0, tiled=True
    )
    gate_pre = saved_gate[0].astype(f32)
    up_pre = saved_up[0].astype(f32)
    hidden = (gate_pre * jax.nn.sigmoid(gate_pre) * up_pre).astype(bf16)
    grad_hidden = lax.all_gather(hidden_share, "dp", axis=0, tiled=True)
    grad_gate_pre, grad_up_pre = activation_grads(grad_hidden, gate_pre, up_pre)
    slot_grads = contract_cols(grad_gate_pre, w_gate[0]) + contract_cols(grad_up_pre, w_up[0])
    returned = lax.all_to_all(
        slot_grads.astype(bf16), "expert", split_axis=0, concat_axis=0, tiled=True
    )
    token_grads = contract_rows(picks.astype(bf16), returned).astype(bf16)
    inputs_here = saved_inputs[0]
    part = jnp.concatenate(
        [
            contract_rows(inputs_here, grad_gate_pre),
            contract_rows(inputs_here, grad_up_pre),
            contract_rows(received, hidden),
        ],
        axis=1,
    )
    return (token_grads, (part * loss_scale).astype(bf16)[None])


def whole(shape):
    return pl.BlockSpec(shape, lambda i, sc: (0,) * len(shape))


def params(mib):
    return pltpu.CompilerParams(vmem_limit_bytes=mib << 20)


def dispatch_kernel(n, cap, sc, *refs):
    toks, (wd0, wd1) = refs[:n], refs[n : n + 2]
    rec0, rec1, share, share_out, pos_out = refs[n + 2 :]
    tok = toks[0].shape[0] - 8
    line = 256 * pl.cdiv(tok, 256)
    before = lax.broadcasted_iota(jnp.int32, (tok, tok), 0) < lax.broadcasted_iota(jnp.int32, (tok, tok), 1)
    before = jnp.where(before, 1.0, 0.0).astype(bf16)
    slot = lax.broadcasted_iota(jnp.int32, (cap, tok), 0).astype(f32)
    masks, gates = [], []
    for a in range(2):
        expert = sc[a].astype(f32)
        for t in toks:
            hit = t[tok:, :tok].astype(f32) == expert
            masks.append(jnp.max(jnp.where(hit, 1.0, 0.0), axis=0, keepdims=True))
            gates.append(jnp.sum(jnp.where(hit, t[tok:, line : line + tok].astype(f32), 0.0), axis=0, keepdims=True))
    fill = [jnp.zeros((8 - 2 * n, tok), f32)] if n < 4 else []
    mask = jnp.concatenate(masks + fill, axis=0)
    pos = jnp.dot(mask.astype(bf16), before, preferred_element_type=f32)
    pos = jnp.where(mask > 0.0, pos, -1.0)
    pos_out[...] = pos
    for rel, t in enumerate(toks):
        w = [
            jnp.where(slot == pos[i : i + 1, :], gates[i] * gate_unit, 0.0).astype(bf16)
            for i in (rel, n + rel)
        ]
        rows = jnp.dot(jnp.concatenate(w, axis=0), t[:tok, :], preferred_element_type=f32).astype(bf16)
        rec0[rel * cap : (rel + 1) * cap, :] = rows[:cap]
        rec1[rel * cap : (rel + 1) * cap, :] = rows[cap:]
    for a, (rec, wd) in enumerate(((rec0, wd0), (rec1, wd1))):
        gh = contract_cols(rec[...], wd[...])
        share[a * n * cap : (a + 1) * n * cap, :] = gh
        share_out[a * n * cap : (a + 1) * n * cap, :] = gh.astype(bf16)


def dispatch(experts, toks, wd0, wd1, cap):
    n = len(toks)
    tok, d = toks[0].shape
    h = wd0.shape[0]
    outs = [((n * cap, d), bf16), ((n * cap, d), bf16), ((2 * n * cap, h), f32), ((2 * n * cap, h), bf16), ((8, tok - 8), f32)]
    return pl.pallas_call(
        functools.partial(dispatch_kernel, n, cap),
        out_shape=[jax.ShapeDtypeStruct(s, t) for s, t in outs],
        grid_spec=pltpu.PrefetchScalarGridSpec(
            num_scalar_prefetch=1,
            grid=(1,),
            in_specs=[whole((tok, d))] * n + [whole((h, d))] * 2,
            out_specs=[whole(s) for s, _ in outs],
        ),
        cost_estimate=pl.CostEstimate(
            flops=4 * n * cap * d * (tok + h), bytes_accessed=2 * n * d * (tok + 2 * cap) + 4 * h * d, transcendentals=0
        ),
        compiler_params=params(24),
        name="dispatch",
    )(experts, *toks, wd0, wd1)


def combine_kernel(n, cap, sc, share, peer, pos, *refs):
    saved, (w0, w1), (gp0, gp1), backs = refs[: 4 * n], refs[4 * n : 4 * n + 2], refs[4 * n + 2 : 4 * n + 4], refs[4 * n + 4 :]
    h = share.shape[1]
    slot = lax.broadcasted_iota(jnp.int32, (cap, pos.shape[1]), 0).astype(f32)
    sums = [None] * n
    for a, (gp, w) in enumerate(((gp0, w0), (gp1, w1))):
        for rel in range(n):
            i = a * n + rel
            gh = share[i * cap : (i + 1) * cap, :] + peer[i * cap : (i + 1) * cap, :].astype(f32)
            gate_pre = saved[2 * i][...].astype(f32)
            up_pre = saved[2 * i + 1][...].astype(f32)
            gg, gu = activation_grads(gh, gate_pre, up_pre)
            gp[rel * cap : (rel + 1) * cap, :h] = gg
            gp[rel * cap : (rel + 1) * cap, h:] = gu
        slots = contract_cols(gp[...], w[...]).astype(bf16)
        for rel in range(n):
            i = a * n + rel
            pick = jnp.where(slot == pos[i : i + 1, :], 1.0, 0.0).astype(bf16)
            part = contract_rows(pick, slots[rel * cap : (rel + 1) * cap])
            sums[rel] = part if sums[rel] is None else sums[rel] + part
    for rel in range(n):
        backs[rel][...] = sums[rel].astype(bf16)


def combine(sources, share, peer, pos, saved0, saved1, w0, w1, cap):
    n = share.shape[0] // (2 * cap)
    h = share.shape[1]
    d = w0.shape[0]
    tok = pos.shape[1]

    def piece(rel):
        return pl.BlockSpec((cap, h), lambda i, sc: (sc[rel], 0))

    saved = [v for pair in (saved0, saved1) for _ in range(n) for v in pair]
    saved_specs = [piece(rel) for _ in range(2) for rel in range(n) for _ in range(2)]
    outs = [(n * cap, 2 * h)] * 2 + [(tok, d)] * n
    return pl.pallas_call(
        functools.partial(combine_kernel, n, cap),
        out_shape=[jax.ShapeDtypeStruct(s, bf16) for s in outs],
        grid_spec=pltpu.PrefetchScalarGridSpec(
            num_scalar_prefetch=1,
            grid=(1,),
            in_specs=[whole(share.shape), whole(share.shape), whole(pos.shape)] + saved_specs + [whole((d, 2 * h))] * 2,
            out_specs=[whole(s) for s in outs],
        ),
        cost_estimate=pl.CostEstimate(
            flops=4 * n * cap * d * (tok + 2 * h),
            bytes_accessed=2 * n * tok * d + 20 * n * cap * h + 8 * d * h,
            transcendentals=2 * n * cap * h,
        ),
        compiler_params=params(28),
        name="combine",
    )(sources, share, peer, pos, *saved, w0, w1)


def weights_kernel(count, cap, sc, x, hid, *refs):
    recs, gps = refs[:count], refs[count : 2 * count]
    out, xs, rs, gs, hs, sems = refs[2 * count :]
    i = pl.program_id(0)
    tile = xs.shape[2]
    steps = pl.num_programs(0)

    def columns(at, step):
        at_col = pl.ds(pl.multiple_of(step * tile, 128), tile)
        copies = []
        base = 0
        for r in recs:
            copies.append(pltpu.make_async_copy(r.at[:, at_col], rs.at[at, pl.ds(base, r.shape[0]), :], sems.at[at, len(copies)]))
            base += r.shape[0]
        for p in range(base // cap):
            src = pl.ds(pl.multiple_of(sc[p] * cap, 16), cap)
            copies.append(pltpu.make_async_copy(x.at[src, at_col], xs.at[at, pl.ds(p * cap, cap), :], sems.at[at, len(copies)]))
        return copies

    def fixed():
        copies = []
        base = 0
        for g in gps:
            copies.append(pltpu.make_async_copy(g, gs.at[pl.ds(base, g.shape[0]), :], sems.at[2, len(copies)]))
            base += g.shape[0]
        for p in range(base // cap):
            src = pl.ds(pl.multiple_of(sc[p] * cap, 16), cap)
            copies.append(pltpu.make_async_copy(hid.at[src, :], hs.at[pl.ds(p * cap, cap), :], sems.at[2, len(copies)]))
        return copies

    @pl.when(i == 0)
    def _():
        for c in columns(0, 0) + fixed():
            c.start()

    @pl.when(i + 1 < steps)
    def _():
        for c in columns((i + 1) % 2, i + 1):
            c.start()

    for c in columns(i % 2, i):
        c.wait()

    @pl.when(i == 0)
    def _():
        for c in fixed():
            c.wait()

    wide = gs.shape[1]
    now = i % 2
    out[0, :, :wide] = (contract_rows(xs[now], gs[...]) * loss_scale).astype(bf16)
    out[0, :, wide:] = (contract_rows(rs[now], hs[...]) * loss_scale).astype(bf16)


def weight_sums(sources, x, hid, recs, gps, cap):
    slots, d = x.shape
    h = hid.shape[1]
    tile = 256
    anywhere = pl.BlockSpec(memory_space=pl.ANY)
    return pl.pallas_call(
        functools.partial(weights_kernel, len(recs), cap),
        out_shape=jax.ShapeDtypeStruct((1, d, 3 * h), bf16),
        grid_spec=pltpu.PrefetchScalarGridSpec(
            num_scalar_prefetch=1,
            grid=(d // tile,),
            in_specs=[anywhere] * (2 + 2 * len(recs)),
            out_specs=pl.BlockSpec((1, tile, 3 * h), lambda i, sc: (0, i, 0)),
            scratch_shapes=[
                pltpu.VMEM((2, slots, tile), bf16),
                pltpu.VMEM((2, slots, tile), bf16),
                pltpu.VMEM((slots, 2 * h), bf16),
                pltpu.VMEM((slots, h), bf16),
                pltpu.SemaphoreType.DMA((3, len(recs) + slots // cap)),
            ],
        ),
        cost_estimate=pl.CostEstimate(
            flops=6 * slots * d * h, bytes_accessed=4 * slots * d + 6 * d * h + 6 * slots * h, transcendentals=0
        ),
        compiler_params=params(24),
        name="weights",
    )(sources, x, hid, *recs, *gps)


def after(value, *others):
    return lax.optimization_barrier((value, *others))[0]


def body_grid(out_grad, routes, gate_codes, w_gate, w_up, w_down, saved_inputs, saved_gate, saved_up):
    owners = lax.axis_size("expert")
    me = lax.axis_index("expert")
    to_core = [(i, i ^ 1) for i in range(owners)]
    to_x = [(i, i ^ 2) for i in range(owners)]
    ring = [(i, (i + 4) % owners) for i in range(owners)]
    rounds = owners // 4
    tok, d = out_grad.shape
    choices = routes.shape[1]
    slots = saved_gate.shape[1]
    cap = slots // owners

    def send(v, perm):
        return lax.ppermute(v, "expert", perm)

    line = 256 * pl.cdiv(tok, 256)
    named = jnp.concatenate(
        [
            jnp.pad(routes.T.astype(bf16), ((0, 8 - choices), (0, line - tok)), constant_values=-1),
            jnp.pad(gate_codes.T.astype(bf16), ((0, 8 - choices), (0, d - line - tok))),
        ],
        axis=1,
    )
    block = jnp.concatenate([out_grad, named], axis=0)
    own_col = [block]
    for _ in range(rounds - 1):
        own_col.append(send(own_col[-1], ring))
    other_col = [send(v, to_x) for v in own_col]

    wd, sg, su = w_down[0], saved_gate[0], saved_up[0]
    w = jnp.concatenate([w_gate[0], w_up[0]], axis=1)
    wd_c, w_c, sg_c, su_c = [send(v, to_core) for v in (wd, w, sg, su)]
    gate_pre = sg.astype(f32)
    hid = (gate_pre * jax.nn.sigmoid(gate_pre) * su.astype(f32)).astype(bf16)

    groups = (me // 4 + rounds - jnp.arange(rounds, dtype=jnp.int32)) % rounds
    own_src = groups * 4 + me % 4
    other_src = jnp.bitwise_xor(own_src, 2)
    experts = jnp.stack([me, jnp.bitwise_xor(me, 1)]).astype(jnp.int32)

    chunks = [[(0, 0)]] + [[(1, k - 1), (0, k)] for k in range(1, rounds)] + [[(1, rounds - 1)]]
    recs, recs_c, gps, gps_c, order = [], [], [], [], []
    back = {}
    for chunk in chunks:
        toks = [(other_col if col else own_col)[k] for col, k in chunk]
        src = jnp.stack([(other_src if col else own_src)[k] for col, k in chunk])
        rec, rec_c, share, share_out, pos = dispatch(experts, toks, wd, wd_c, cap)
        peer = lax.ppermute(share_out, "dp", [(0, 1), (1, 0)])
        gp, gp_c, *sums = combine(src, share, peer, pos, (sg, su), (sg_c, su_c), w, w_c, cap)
        back.update(zip(chunk, sums))
        recs.append(rec)
        recs_c.append(send(rec_c, to_core))
        gps.append(gp)
        gps_c.append(send(gp_c, to_core))
        order.append(src)

    run = None
    arrived = {k: send(back[(1, k)], to_x) for k in [1, 2, 3, 0]}
    for k in [1, 2, 3, 0]:
        total = back[(0, k)].astype(f32) + arrived[k].astype(f32)
        if run is not None:
            total = total + run.astype(f32)
        total = total.astype(bf16)
        run = send(total, ring) if k else None
    order = jnp.concatenate(order)
    order = jnp.concatenate([order, jnp.bitwise_xor(order, 1)])
    weight_grads = weight_sums(order, saved_inputs[0], hid, recs + recs_c, gps + gps_c, cap)
    return (total, weight_grads)


def solution(mesh):
    placed = (
        P("expert", "dp"),
        P("expert", None),
        P("expert", None),
        P("expert", "dp", None),
        P("expert", "dp", None),
        P("expert", None, "dp"),
        P("expert", None, "dp"),
        P("expert", None, None),
        P("expert", None, None),
    )
    small = mesh.shape["expert"] == 16 and mesh.shape["dp"] == 2
    return jax.shard_map(
        body_grid if small else body_any,
        mesh=mesh,
        in_specs=placed,
        out_specs=(P("expert", "dp"), P("expert", "dp", None)),
        check_vma=False,
    )
```

```python
import functools

import jax
import jax.numpy as jnp
from jax import lax
from jax.experimental import pallas as pl
from jax.experimental.pallas import tpu as pltpu
from jax.sharding import PartitionSpec as P

gate_unit = 0.00390625
loss_scale = 0.015625
f32 = jnp.float32
bf16 = jnp.bfloat16


def contract_rows(left, right):
    return lax.dot_general(left, right, (((0,), (0,)), ((), ())), preferred_element_type=f32)


def contract_cols(left, right):
    return lax.dot_general(left, right, (((1,), (1,)), ((), ())), preferred_element_type=f32)


def activation_grads(grad_hidden, gate_pre, up_pre):
    sigmoid = jax.nn.sigmoid(gate_pre)
    silu = gate_pre * sigmoid
    dsilu = sigmoid * (1.0 + gate_pre * (1.0 - sigmoid))
    grad_gate_pre = (grad_hidden * up_pre * dsilu).astype(bf16)
    grad_up_pre = (grad_hidden * silu).astype(bf16)
    return (grad_gate_pre, grad_up_pre)


def body_any(out_grad, routes, gate_codes, w_gate, w_up, w_down, saved_inputs, saved_gate, saved_up):
    owners = lax.axis_size("expert")
    slot_count = saved_gate.shape[1]
    capacity = slot_count // owners
    token_count = routes.shape[0]
    choice_count = routes.shape[1]
    flat_routes = routes.reshape(-1)
    onehot = (flat_routes[:, None] == jnp.arange(owners, dtype=jnp.int32)[None, :]).astype(jnp.int32)
    earlier = jnp.cumsum(onehot, axis=0) - onehot
    position = jnp.sum(earlier * onehot, axis=1)
    slot_index = (flat_routes * capacity + position).reshape(token_count, choice_count)
    gate_values = gate_codes.astype(f32) * gate_unit
    rows_iota = jnp.arange(slot_count, dtype=jnp.int32)[:, None]
    weighted = jnp.zeros((slot_count, token_count), f32)
    picks = jnp.zeros((slot_count, token_count), f32)
    for pick in range(choice_count):
        hit = rows_iota == slot_index[:, pick][None, :]
        weighted = weighted + jnp.where(hit, gate_values[:, pick][None, :], 0.0)
        picks = picks + hit.astype(f32)
    outgoing = jnp.dot(weighted.astype(bf16), out_grad, preferred_element_type=f32).astype(bf16)
    received = lax.all_to_all(outgoing, "expert", split_axis=0, concat_axis=0, tiled=True)
    hidden_share = lax.psum_scatter(
        contract_cols(received, w_down[0]), "dp", scatter_dimension=0, tiled=True
    )
    gate_pre = saved_gate[0].astype(f32)
    up_pre = saved_up[0].astype(f32)
    hidden = (gate_pre * jax.nn.sigmoid(gate_pre) * up_pre).astype(bf16)
    grad_hidden = lax.all_gather(hidden_share, "dp", axis=0, tiled=True)
    grad_gate_pre, grad_up_pre = activation_grads(grad_hidden, gate_pre, up_pre)
    slot_grads = contract_cols(grad_gate_pre, w_gate[0]) + contract_cols(grad_up_pre, w_up[0])
    returned = lax.all_to_all(
        slot_grads.astype(bf16), "expert", split_axis=0, concat_axis=0, tiled=True
    )
    token_grads = contract_rows(picks.astype(bf16), returned).astype(bf16)
    inputs_here = saved_inputs[0]
    part = jnp.concatenate(
        [
            contract_rows(inputs_here, grad_gate_pre),
            contract_rows(inputs_here, grad_up_pre),
            contract_rows(received, hidden),
        ],
        axis=1,
    )
    return (token_grads, (part * loss_scale).astype(bf16)[None])


def whole(shape):
    return pl.BlockSpec(shape, lambda i, sc: (0,) * len(shape))


def in_hbm(v):
    return pltpu.with_memory_space_constraint(v, pltpu.HBM)


def source(here, step, other):
    group = lax.rem(here // 4 + (4 - step), 4)
    return jnp.bitwise_xor(group * 4 + lax.rem(here, 4), 2 * other)


def params(mib):
    return pltpu.CompilerParams(vmem_limit_bytes=mib << 20)


def dispatch_kernel(n, cap, here, *refs):
    toks, (wd0, wd1) = refs[:n], refs[n : n + 2]
    rec0, rec1, share, share_out, pos_out = refs[n + 2 :]
    tok = toks[0].shape[0] - 8
    line = 256 * pl.cdiv(tok, 256)
    before = lax.broadcasted_iota(jnp.int32, (tok, tok), 0) < lax.broadcasted_iota(jnp.int32, (tok, tok), 1)
    before = jnp.where(before, 1.0, 0.0).astype(bf16)
    slot = lax.broadcasted_iota(jnp.int32, (cap, tok), 0).astype(f32)
    masks, gates = [], []
    for a in range(2):
        expert = jnp.bitwise_xor(here[0], a).astype(f32)
        for t in toks:
            hit = t[tok:, :tok].astype(f32) == expert
            masks.append(jnp.max(jnp.where(hit, 1.0, 0.0), axis=0, keepdims=True))
            gates.append(jnp.sum(jnp.where(hit, t[tok:, line : line + tok].astype(f32), 0.0), axis=0, keepdims=True))
    fill = [jnp.zeros((8 - 2 * n, tok), f32)] if n < 4 else []
    mask = jnp.concatenate(masks + fill, axis=0)
    pos = jnp.dot(mask.astype(bf16), before, preferred_element_type=f32)
    pos = jnp.where(mask > 0.0, pos, -1.0)
    pos_out[...] = pos
    for rel, t in enumerate(toks):
        w = [
            jnp.where(slot == pos[i : i + 1, :], gates[i] * gate_unit, 0.0).astype(bf16)
            for i in (rel, n + rel)
        ]
        rows = jnp.dot(jnp.concatenate(w, axis=0), t[:tok, :], preferred_element_type=f32).astype(bf16)
        rec0[rel * cap : (rel + 1) * cap, :] = rows[:cap]
        rec1[rel * cap : (rel + 1) * cap, :] = rows[cap:]
    for a, (rec, wd) in enumerate(((rec0, wd0), (rec1, wd1))):
        gh = contract_cols(rec[...], wd[...])
        share[a * n * cap : (a + 1) * n * cap, :] = gh
        share_out[a * n * cap : (a + 1) * n * cap, :] = gh.astype(bf16)


def dispatch(here, toks, wd0, wd1, cap):
    n = len(toks)
    tok, d = toks[0].shape
    h = wd0.shape[0]
    outs = [((n * cap, d), bf16), ((n * cap, d), bf16), ((2 * n * cap, h), f32), ((2 * n * cap, h), bf16), ((8, tok - 8), f32)]
    return pl.pallas_call(
        functools.partial(dispatch_kernel, n, cap),
        out_shape=[pltpu.HBM(s, t) for s, t in outs],
        grid_spec=pltpu.PrefetchScalarGridSpec(
            num_scalar_prefetch=1,
            grid=(1,),
            in_specs=[whole((tok, d))] * n + [whole((h, d))] * 2,
            out_specs=[whole(s) for s, _ in outs],
        ),
        cost_estimate=pl.CostEstimate(
            flops=4 * n * cap * d * (tok + h), bytes_accessed=2 * n * d * (tok + 2 * cap) + 4 * h * d, transcendentals=0
        ),
        compiler_params=params(24),
        name="dispatch",
    )(here, *[in_hbm(t) for t in toks], wd0, wd1)


def combine_kernel(n, cap, sc, share, peer, pos, *refs):
    saved, (w0, w1), (gp0, gp1), backs = refs[: 4 * n], refs[4 * n : 4 * n + 2], refs[4 * n + 2 : 4 * n + 4], refs[4 * n + 4 :]
    h = share.shape[1]
    slot = lax.broadcasted_iota(jnp.int32, (cap, pos.shape[1]), 0).astype(f32)
    sums = [None] * n
    for a, (gp, w) in enumerate(((gp0, w0), (gp1, w1))):
        for rel in range(n):
            i = a * n + rel
            gh = share[i * cap : (i + 1) * cap, :] + peer[i * cap : (i + 1) * cap, :].astype(f32)
            gate_pre = saved[2 * i][...].astype(f32)
            up_pre = saved[2 * i + 1][...].astype(f32)
            gg, gu = activation_grads(gh, gate_pre, up_pre)
            gp[rel * cap : (rel + 1) * cap, :h] = gg
            gp[rel * cap : (rel + 1) * cap, h:] = gu
        slots = contract_cols(gp[...], w[...]).astype(bf16)
        for rel in range(n):
            i = a * n + rel
            pick = jnp.where(slot == pos[i : i + 1, :], 1.0, 0.0).astype(bf16)
            part = contract_rows(pick, slots[rel * cap : (rel + 1) * cap])
            sums[rel] = part if sums[rel] is None else sums[rel] + part
    for rel in range(n):
        backs[rel][...] = sums[rel].astype(bf16)


def combine(here, chunk, share, peer, pos, saved0, saved1, w0, w1, cap):
    n = len(chunk)
    h = share.shape[1]
    d = w0.shape[0]
    tok = pos.shape[1]

    def piece(rel):
        other, step = chunk[rel]
        return pl.BlockSpec((cap, h), lambda i, here: (source(here[0], step, other), 0))

    saved = [v for pair in (saved0, saved1) for _ in range(n) for v in pair]
    saved_specs = [piece(rel) for _ in range(2) for rel in range(n) for _ in range(2)]
    outs = [(n * cap, 2 * h)] * 2 + [(tok, d)] * n
    return pl.pallas_call(
        functools.partial(combine_kernel, n, cap),
        out_shape=[pltpu.HBM(s, bf16) for s in outs],
        grid_spec=pltpu.PrefetchScalarGridSpec(
            num_scalar_prefetch=1,
            grid=(1,),
            in_specs=[whole(share.shape), whole(share.shape), whole(pos.shape)] + saved_specs + [whole((d, 2 * h))] * 2,
            out_specs=[whole(s) for s in outs],
        ),
        cost_estimate=pl.CostEstimate(
            flops=4 * n * cap * d * (tok + 2 * h),
            bytes_accessed=2 * n * tok * d + 20 * n * cap * h + 8 * d * h,
            transcendentals=2 * n * cap * h,
        ),
        compiler_params=params(28),
        name="combine",
    )(here, in_hbm(share), in_hbm(peer), in_hbm(pos), *saved, w0, w1)


def weights_kernel(order, cap, sorted_left, here, *refs):
    by_source, pieces = refs[0], refs[1:-4]
    pieces, out = (pieces[:-1], pieces[-1])
    ls, rs, left_sems, right_sems = refs[-4:]
    i = pl.program_id(0)
    tile = ls.shape[2]
    steps = pl.num_programs(0)

    def copies_of_sorted(column, to, sems):
        made = []
        for p, (step, other, plane) in enumerate(order):
            src = jnp.bitwise_xor(source(here[0], step, other), plane)
            rows = pl.ds(pl.multiple_of(src * cap, 16), cap)
            at = by_source.at[rows, :] if column is None else by_source.at[rows, column]
            made.append(pltpu.make_async_copy(at, to.at[pl.ds(p * cap, cap), :], sems.at[len(made)]))
        return made

    def copies_of_pieces(column, to, sems):
        made, base = [], 0
        for r in pieces:
            at = r if column is None else r.at[:, column]
            made.append(pltpu.make_async_copy(at, to.at[pl.ds(base, r.shape[0]), :], sems.at[len(made)]))
            base += r.shape[0]
        return made

    left_copies, right_copies = (
        (copies_of_sorted, copies_of_pieces) if sorted_left else (copies_of_pieces, copies_of_sorted)
    )

    def left(step):
        slot = lax.rem(step, 2)
        column = pl.ds(pl.multiple_of(step * tile, 128), tile)
        return left_copies(column, ls.at[slot], left_sems.at[slot])

    @pl.when(i == 0)
    def _():
        for c in right_copies(None, rs, right_sems) + left(i):
            c.start()

    @pl.when(i + 1 < steps)
    def _():
        for c in left(i + 1):
            c.start()

    for c in left(i):
        c.wait()

    @pl.when(i == 0)
    def _():
        for c in right_copies(None, rs, right_sems):
            c.wait()

    out[0] = (contract_rows(ls[lax.rem(i, 2)], rs[...]) * loss_scale).astype(bf16)


def weight_sums(here, order, by_source, pieces, sorted_left, into, cap):
    slots = by_source.shape[0]
    d = by_source.shape[1] if sorted_left else pieces[0].shape[1]
    wide = pieces[0].shape[1] if sorted_left else by_source.shape[1]
    tile = 256
    anywhere = pl.BlockSpec(memory_space=pl.ANY)
    at = 0 if sorted_left else 2
    whole_out = jax.ShapeDtypeStruct((1, d, 3 * (wide // 2 if sorted_left else wide)), bf16)
    given = [by_source, *pieces]
    kernel = functools.partial(weights_kernel, order, cap, sorted_left)
    body = kernel if into is None else (lambda here, old, *refs: kernel(here, *refs))
    return pl.pallas_call(
        body,
        out_shape=whole_out,
        grid_spec=pltpu.PrefetchScalarGridSpec(
            num_scalar_prefetch=1,
            grid=(d // tile,),
            in_specs=[anywhere] * (len(given) + (into is not None)),
            out_specs=pl.BlockSpec((1, tile, wide), lambda i, here: (0, i, at)),
            scratch_shapes=[
                pltpu.VMEM((2, slots, tile), bf16),
                pltpu.VMEM((slots, wide), bf16),
                pltpu.SemaphoreType.DMA((2, len(order))),
                pltpu.SemaphoreType.DMA((len(order),)),
            ],
        ),
        input_output_aliases={} if into is None else {1: 0},
        cost_estimate=pl.CostEstimate(
            flops=2 * slots * d * wide, bytes_accessed=2 * slots * (d + wide) + 2 * d * wide, transcendentals=0
        ),
        compiler_params=params(20),
        name="weights",
    )(here, *([] if into is None else [into]), *[in_hbm(v) for v in given])


def together(*values):
    return lax.optimization_barrier(values)


def body_grid(out_grad, routes, gate_codes, w_gate, w_up, w_down, saved_inputs, saved_gate, saved_up):
    owners = lax.axis_size("expert")
    me = lax.axis_index("expert")
    to_core = [(i, i ^ 1) for i in range(owners)]
    to_x = [(i, i ^ 2) for i in range(owners)]
    tok, d = out_grad.shape
    choices = routes.shape[1]
    slots = saved_gate.shape[1]
    cap = slots // owners

    def send(v, perm):
        return lax.ppermute(v, "expert", perm)

    line = 256 * pl.cdiv(tok, 256)
    named = jnp.concatenate(
        [
            jnp.pad(routes.T.astype(bf16), ((0, 8 - choices), (0, line - tok)), constant_values=-1),
            jnp.pad(gate_codes.T.astype(bf16), ((0, 8 - choices), (0, d - line - tok))),
        ],
        axis=1,
    )
    block = jnp.concatenate([out_grad, named], axis=0)
    here = me.reshape(1).astype(jnp.int32)

    def ring(v, hops=1):
        return send(v, [(i, (i + 4 * hops) % owners) for i in range(owners)])

    wd, sg, su = w_down[0], saved_gate[0], saved_up[0]
    w = jnp.concatenate([w_gate[0], w_up[0]], axis=1)
    wd_c, sg_c, su_c, w_c = [send(v, to_core) for v in (wd, sg, su, w)]
    gate_pre = sg.astype(f32)
    hid = (gate_pre * jax.nn.sigmoid(gate_pre) * su.astype(f32)).astype(bf16)

    order, recs, recs_c, gps, gps_c = [], [], [], [], []

    def first(chunk, toks):
        rec, rec_c, share, share_out, pos = dispatch(here, toks, wd, wd_c, cap)
        order.extend((k, col, 0) for col, k in chunk)
        recs.append(rec)
        recs_c.append(send(rec_c, to_core))
        return chunk, share, share_out, pos

    def exchange(share_out):
        return lax.ppermute(share_out, "dp", [(0, 1), (1, 0)])

    def second(state, peer):
        chunk, share, _, pos = state
        gp, gp_c, *sums = combine(here, chunk, share, peer, pos, (sg, su), (sg_c, su_c), w, w_c, cap)
        gps.append(gp)
        gps_c.append(send(gp_c, to_core))
        return sums

    def add(*values):
        return sum(v.astype(f32) for v in values).astype(bf16)

    r1, x0 = ring(block), send(block, to_x)
    c0 = first([(0, 0)], [block])
    y0 = exchange(c0[2])
    r1, x0, _ = together(r1, x0, c0[2])
    r2, x1 = ring(r1), send(r1, to_x)
    c1 = first([(1, 0), (0, 1)], [x0, r1])
    y1 = exchange(c1[2])
    (t_r0,) = second(c0, y0)
    r2, x1, _, t_r0 = together(r2, x1, c1[2], t_r0)
    r3, x2 = ring(r2), send(r2, to_x)
    c2 = first([(1, 1), (0, 2)], [x1, r2])
    y2 = exchange(c2[2])
    t_x0, t_r1 = second(c1, y1)
    r3, x2, _, t_x0, t_r1 = together(r3, x2, c2[2], t_x0, t_r1)
    x3 = send(r3, to_x)
    c3 = first([(1, 2), (0, 3)], [x2, r3])
    y3 = exchange(c3[2])
    t_x1, t_r2 = second(c2, y2)
    x3, _, t_x1, t_r2 = together(x3, c3[2], t_x1, t_r2)
    b1 = send(t_x1, to_x)
    c4 = first([(1, 3)], [x3])
    y4 = exchange(c4[2])
    t_x2, t_r3 = second(c3, y3)
    b1, _, t_x2, t_r3 = together(b1, c4[2], t_x2, t_r3)
    b2 = send(t_x2, to_x)
    v1 = ring(add(t_r1, b1), 3)
    (t_x3,) = second(c4, y4)
    b2, t_x3 = together(b2, t_x3)
    b3 = send(t_x3, to_x)
    v2 = ring(add(t_r2, b2), 2)
    order_all = order + [(k, col, 1) for k, col, _ in order]
    part = weight_sums(here, order_all, hid, recs + recs_c, False, None, cap)
    b3, v1, part = together(b3, v1, part)
    v3 = ring(add(t_r3, b3), 1)
    b0 = send(t_x0, to_x)
    weight_grads = weight_sums(here, order_all, saved_inputs[0], gps + gps_c, True, part, cap)
    total = add(t_r0, b0, v1, v2, v3)
    return (total, weight_grads)


def solution(mesh):
    placed = (
        P("expert", "dp"),
        P("expert", None),
        P("expert", None),
        P("expert", "dp", None),
        P("expert", "dp", None),
        P("expert", None, "dp"),
        P("expert", None, "dp"),
        P("expert", None, None),
        P("expert", None, None),
    )
    small = mesh.shape["expert"] == 16 and mesh.shape["dp"] == 2
    return jax.shard_map(
        body_grid if small else body_any,
        mesh=mesh,
        in_specs=placed,
        out_specs=(P("expert", "dp"), P("expert", "dp", None)),
        check_vma=False,
    )
```

```python
import functools

import jax
import jax.numpy as jnp
from jax import lax
from jax.experimental import pallas as pl
from jax.experimental.pallas import tpu as pltpu
from jax.sharding import PartitionSpec as P

gate_unit = 0.00390625
loss_scale = 0.015625
f32 = jnp.float32
bf16 = jnp.bfloat16


def contract_rows(left, right):
    return lax.dot_general(left, right, (((0,), (0,)), ((), ())), preferred_element_type=f32)


def contract_cols(left, right):
    return lax.dot_general(left, right, (((1,), (1,)), ((), ())), preferred_element_type=f32)


def activation_grads(grad_hidden, gate_pre, up_pre):
    sigmoid = jax.nn.sigmoid(gate_pre)
    silu = gate_pre * sigmoid
    dsilu = sigmoid * (1.0 + gate_pre * (1.0 - sigmoid))
    grad_gate_pre = (grad_hidden * up_pre * dsilu).astype(bf16)
    grad_up_pre = (grad_hidden * silu).astype(bf16)
    return (grad_gate_pre, grad_up_pre)


def body_any(out_grad, routes, gate_codes, w_gate, w_up, w_down, saved_inputs, saved_gate, saved_up):
    owners = lax.axis_size("expert")
    slot_count = saved_gate.shape[1]
    capacity = slot_count // owners
    token_count = routes.shape[0]
    choice_count = routes.shape[1]
    flat_routes = routes.reshape(-1)
    onehot = (flat_routes[:, None] == jnp.arange(owners, dtype=jnp.int32)[None, :]).astype(jnp.int32)
    earlier = jnp.cumsum(onehot, axis=0) - onehot
    position = jnp.sum(earlier * onehot, axis=1)
    slot_index = (flat_routes * capacity + position).reshape(token_count, choice_count)
    gate_values = gate_codes.astype(f32) * gate_unit
    rows_iota = jnp.arange(slot_count, dtype=jnp.int32)[:, None]
    weighted = jnp.zeros((slot_count, token_count), f32)
    picks = jnp.zeros((slot_count, token_count), f32)
    for pick in range(choice_count):
        hit = rows_iota == slot_index[:, pick][None, :]
        weighted = weighted + jnp.where(hit, gate_values[:, pick][None, :], 0.0)
        picks = picks + hit.astype(f32)
    outgoing = jnp.dot(weighted.astype(bf16), out_grad, preferred_element_type=f32).astype(bf16)
    received = lax.all_to_all(outgoing, "expert", split_axis=0, concat_axis=0, tiled=True)
    hidden_share = lax.psum_scatter(
        contract_cols(received, w_down[0]), "dp", scatter_dimension=0, tiled=True
    )
    gate_pre = saved_gate[0].astype(f32)
    up_pre = saved_up[0].astype(f32)
    hidden = (gate_pre * jax.nn.sigmoid(gate_pre) * up_pre).astype(bf16)
    grad_hidden = lax.all_gather(hidden_share, "dp", axis=0, tiled=True)
    grad_gate_pre, grad_up_pre = activation_grads(grad_hidden, gate_pre, up_pre)
    slot_grads = contract_cols(grad_gate_pre, w_gate[0]) + contract_cols(grad_up_pre, w_up[0])
    returned = lax.all_to_all(
        slot_grads.astype(bf16), "expert", split_axis=0, concat_axis=0, tiled=True
    )
    token_grads = contract_rows(picks.astype(bf16), returned).astype(bf16)
    inputs_here = saved_inputs[0]
    part = jnp.concatenate(
        [
            contract_rows(inputs_here, grad_gate_pre),
            contract_rows(inputs_here, grad_up_pre),
            contract_rows(received, hidden),
        ],
        axis=1,
    )
    return (token_grads, (part * loss_scale).astype(bf16)[None])


on_chip = pl.BlockSpec(memory_space=pltpu.VMEM)
on_scalar = pl.BlockSpec(memory_space=pltpu.SMEM)
anywhere = pl.BlockSpec(memory_space=pl.ANY)
light = pl.CostEstimate(flops=1 << 20, bytes_accessed=1 << 14, transcendentals=0)


def source(here, step, other):
    group = lax.rem(here // 4 + (4 - step), 4)
    return jnp.bitwise_xor(group * 4 + lax.rem(here, 4), 2 * other)


def params(mib):
    return pltpu.CompilerParams(vmem_limit_bytes=mib << 20)


def dispatch_kernel(n, cap, here, *refs):
    toks, (wd0, wd1) = refs[:n], refs[n : n + 2]
    rec0, rec1, share, *share_out, pos_out = refs[n + 2 :]
    tok = toks[0].shape[0] - 8
    line = 256 * pl.cdiv(tok, 256)
    before = lax.broadcasted_iota(jnp.int32, (tok, tok), 0) < lax.broadcasted_iota(jnp.int32, (tok, tok), 1)
    before = jnp.where(before, 1.0, 0.0).astype(bf16)
    slot = lax.broadcasted_iota(jnp.int32, (cap, tok), 0).astype(f32)
    masks, gates = [], []
    for a in range(2):
        expert = jnp.bitwise_xor(here[0], a).astype(f32)
        for t in toks:
            hit = t[tok:, :tok].astype(f32) == expert
            masks.append(jnp.max(jnp.where(hit, 1.0, 0.0), axis=0, keepdims=True))
            gates.append(jnp.sum(jnp.where(hit, t[tok:, line : line + tok].astype(f32), 0.0), axis=0, keepdims=True))
    fill = [jnp.zeros((8 - 2 * n, tok), f32)] if n < 4 else []
    mask = jnp.concatenate(masks + fill, axis=0)
    pos = jnp.dot(mask.astype(bf16), before, preferred_element_type=f32)
    pos = jnp.where(mask > 0.0, pos, -1.0)
    pos_out[...] = pos
    for rel, t in enumerate(toks):
        w = [
            jnp.where(slot == pos[i : i + 1, :], gates[i] * gate_unit, 0.0).astype(bf16)
            for i in (rel, n + rel)
        ]
        rows = jnp.dot(jnp.concatenate(w, axis=0), t[:tok, :], preferred_element_type=f32).astype(bf16)
        rec0[rel * cap : (rel + 1) * cap, :] = rows[:cap]
        rec1[rel * cap : (rel + 1) * cap, :] = rows[cap:]
    for a, (rec, wd) in enumerate(((rec0, wd0), (rec1, wd1))):
        gh = contract_cols(rec[...], wd[...])
        share[a * n * cap : (a + 1) * n * cap, :] = gh
        share_out[a][...] = gh.astype(bf16)


def dispatch(here, toks, wd0, wd1, cap):
    n = len(toks)
    tok, d = toks[0].shape
    h = wd0.shape[0]
    outs = [((n * cap, d), bf16), ((n * cap, d), bf16), ((2 * n * cap, h), f32), ((n * cap, h), bf16), ((n * cap, h), bf16), ((8, tok - 8), f32)]
    return pl.pallas_call(
        functools.partial(dispatch_kernel, n, cap),
        out_shape=[jax.ShapeDtypeStruct(s, t) for s, t in outs],
        in_specs=[on_scalar] + [on_chip] * (n + 2),
        out_specs=[on_chip] * len(outs),
        cost_estimate=light,
        compiler_params=params(16),
        name="dispatch",
    )(here, *toks, wd0, wd1)


def combine_kernel(chunk, cap, here, share, peer0, peer1, pos, *refs):
    n = len(chunk)
    saved, (w0, w1, rec1), (gp0, both) = refs[:4], refs[4:7], refs[7:9]
    backs, (held, sems) = refs[9 : 9 + n], refs[9 + n :]
    d = rec1.shape[1]
    gp1 = both.at[:, d:]
    both[:, :d] = rec1[...]
    h = share.shape[1]
    copies = []
    for a in range(2):
        for other, step in chunk:
            rows = pl.ds(pl.multiple_of(source(here[0], step, other) * cap, 16), cap)
            for v in saved[2 * a : 2 * a + 2]:
                i = len(copies)
                copies.append(pltpu.make_async_copy(v.at[rows, :], held.at[i], sems.at[i]))
    for c in copies:
        c.start()
    slot = lax.broadcasted_iota(jnp.int32, (cap, pos.shape[1]), 0).astype(f32)
    sums = [None] * n
    for a, (gp, w, peer) in enumerate(((gp0, w0, peer0), (gp1, w1, peer1))):
        for rel in range(n):
            i = a * n + rel
            copies[2 * i].wait()
            copies[2 * i + 1].wait()
            gh = share[i * cap : (i + 1) * cap, :] + peer[rel * cap : (rel + 1) * cap, :].astype(f32)
            gg, gu = activation_grads(gh, held[2 * i].astype(f32), held[2 * i + 1].astype(f32))
            gp[rel * cap : (rel + 1) * cap, :h] = gg
            gp[rel * cap : (rel + 1) * cap, h:] = gu
        slots = contract_cols(gp[...], w[...]).astype(bf16)
        for rel in range(n):
            i = a * n + rel
            pick = jnp.where(slot == pos[i : i + 1, :], 1.0, 0.0).astype(bf16)
            part = contract_rows(pick, slots[rel * cap : (rel + 1) * cap])
            sums[rel] = part if sums[rel] is None else sums[rel] + part
    for rel in range(n):
        backs[rel][...] = sums[rel].astype(bf16)


def combine(here, chunk, share, peers, pos, saved0, saved1, w0, w1, rec1, cap):
    n = len(chunk)
    h = share.shape[1]
    d = w0.shape[0]
    tok = pos.shape[1]
    outs = [(n * cap, 2 * h), (n * cap, d + 2 * h)] + [(tok, d)] * n
    return pl.pallas_call(
        functools.partial(combine_kernel, chunk, cap),
        out_shape=[jax.ShapeDtypeStruct(s, bf16) for s in outs],
        in_specs=[on_scalar] + [on_chip] * 4 + [anywhere] * 4 + [on_chip] * 3,
        out_specs=[on_chip] * len(outs),
        scratch_shapes=[pltpu.VMEM((4 * n, cap, h), bf16), pltpu.SemaphoreType.DMA((4 * n,))],
        cost_estimate=light,
        compiler_params=params(20),
        name="combine",
    )(here, share, *peers, pos, *saved0, *saved1, w0, w1, rec1)


def join_kernel(left, right, out):
    out[:, : left.shape[1]] = left[...]
    out[:, left.shape[1] :] = right[...]


def join(left, right):
    rows, h = left.shape
    return pl.pallas_call(
        join_kernel,
        out_shape=jax.ShapeDtypeStruct((rows, 2 * h), left.dtype),
        in_specs=[on_chip] * 2,
        out_specs=on_chip,
        cost_estimate=light,
        compiler_params=params(8),
        name="join",
    )(left, right)


def add_kernel(*refs):
    total = refs[0][...].astype(f32)
    for r in refs[1:-1]:
        total = total + r[...].astype(f32)
    refs[-1][...] = total.astype(refs[-1].dtype)


def add(*values):
    return pl.pallas_call(
        add_kernel,
        out_shape=jax.ShapeDtypeStruct(values[0].shape, values[0].dtype),
        in_specs=[on_chip] * len(values),
        out_specs=on_chip,
        cost_estimate=light,
        compiler_params=params(8),
        name="add",
    )(*values)


def weights_kernel(order, cap, sorted_left, starts, here, *refs):
    count = 1 if sorted_left else 2
    by_source, pieces, out = refs[:count], refs[count:-5], refs[-5]
    ls, rs, left_sems, right_sems = refs[-4:]
    i = pl.program_id(0)
    tile = ls.shape[2]
    steps = pl.num_programs(0)

    def copies_of_sorted(v, column, to, sems):
        made = []
        for p, (step, other, plane) in enumerate(order):
            src = jnp.bitwise_xor(source(here[0], step, other), plane)
            rows = pl.ds(pl.multiple_of(src * cap, 16), cap)
            at = v.at[rows, :] if column is None else v.at[rows, pl.ds(pl.multiple_of(column * tile, 128), tile)]
            made.append(pltpu.make_async_copy(at, to.at[pl.ds(p * cap, cap), :], sems.at[len(made)]))
        return made

    def copies_of_pieces(column, to, sems):
        made, base = [], 0
        for r, first in zip(pieces, starts):
            if column is None:
                at = r.at[:, pl.ds(first, to.shape[1])]
            else:
                at = r.at[:, pl.ds(pl.multiple_of(first + column * tile, 128), tile)]
            made.append(pltpu.make_async_copy(at, to.at[pl.ds(base, r.shape[0]), :], sems.at[len(made)]))
            base += r.shape[0]
        return made

    def left(step):
        slot = lax.rem(step, 2)
        if sorted_left:
            return copies_of_sorted(by_source[0], step, ls.at[slot], left_sems.at[slot])
        return copies_of_pieces(step, ls.at[slot], left_sems.at[slot])

    def right():
        if sorted_left:
            return copies_of_pieces(None, rs.at[0], right_sems.at[0])
        return [c for k in range(2) for c in copies_of_sorted(by_source[k], None, rs.at[k], right_sems.at[k])]

    @pl.when(i == 0)
    def _():
        for c in right() + left(i):
            c.start()

    @pl.when(i + 1 < steps)
    def _():
        for c in left(i + 1):
            c.start()

    @pl.when(i == 0)
    def _():
        for c in right():
            c.wait()
        if not sorted_left:
            gate_pre = rs[0].astype(f32)
            rs[0] = (gate_pre * jax.nn.sigmoid(gate_pre) * rs[1].astype(f32)).astype(bf16)

    for c in left(i):
        c.wait()

    out[0] = (contract_rows(ls[lax.rem(i, 2)], rs[0]) * loss_scale).astype(bf16)


def weight_sums(here, order, by_source, pieces, starts, sorted_left, into, cap):
    slots, wide = by_source[0].shape
    d = pieces[0].shape[1]
    if sorted_left:
        d, wide = wide, d
    tile = 256
    at = 0 if sorted_left else 2
    whole_out = jax.ShapeDtypeStruct((1, d, 3 * (wide // 2 if sorted_left else wide)), bf16)
    given = [*by_source, *pieces]
    kernel = functools.partial(weights_kernel, order, cap, sorted_left, starts)
    body = kernel if into is None else (lambda here, old, *refs: kernel(here, *refs))
    return pl.pallas_call(
        body,
        out_shape=whole_out,
        grid_spec=pltpu.PrefetchScalarGridSpec(
            num_scalar_prefetch=1,
            grid=(d // tile,),
            in_specs=[anywhere] * (len(given) + (into is not None)),
            out_specs=pl.BlockSpec((1, tile, wide), lambda i, here: (0, i, at)),
            scratch_shapes=[
                pltpu.VMEM((2, slots, tile), bf16),
                pltpu.VMEM((len(by_source), slots, wide), bf16),
                pltpu.SemaphoreType.DMA((2, len(order))),
                pltpu.SemaphoreType.DMA((len(by_source), len(order))),
            ],
        ),
        input_output_aliases={} if into is None else {1: 0},
        cost_estimate=light,
        compiler_params=params(20),
        name="weights",
    )(here, *([] if into is None else [into]), *given)


def together(*values):
    return lax.optimization_barrier(values)


def body_grid(out_grad, routes, gate_codes, w_gate, w_up, w_down, saved_inputs, saved_gate, saved_up):
    owners = lax.axis_size("expert")
    me = lax.axis_index("expert")
    to_core = [(i, i ^ 1) for i in range(owners)]
    to_x = [(i, i ^ 2) for i in range(owners)]
    tok, d = out_grad.shape
    choices = routes.shape[1]
    slots = saved_gate.shape[1]
    cap = slots // owners

    def send(v, perm):
        return lax.ppermute(v, "expert", perm)

    line = 256 * pl.cdiv(tok, 256)
    named = jnp.concatenate(
        [
            jnp.pad(routes.T.astype(bf16), ((0, 8 - choices), (0, line - tok)), constant_values=-1),
            jnp.pad(gate_codes.T.astype(bf16), ((0, 8 - choices), (0, d - line - tok))),
        ],
        axis=1,
    )
    block = jnp.concatenate([out_grad, named], axis=0)
    here = me.reshape(1).astype(jnp.int32)

    def ring(v, hops=1):
        return send(v, [(i, (i + 4 * hops) % owners) for i in range(owners)])

    wd, sg, su = w_down[0], saved_gate[0], saved_up[0]
    wd_c, sg_c, su_c = [send(v, to_core) for v in (wd, sg, su)]

    order, recs, gps = [], [], []

    def first(chunk, toks):
        rec, rec_c, share, share0, share1, pos = dispatch(here, toks, wd, wd_c, cap)
        order.extend((k, col, 0) for col, k in chunk)
        recs.append(rec)
        return (chunk, share, pos, rec_c), share0, share1

    def exchange(v):
        return lax.ppermute(v, "dp", [(0, 1), (1, 0)])

    def second(state, *peers):
        chunk, share, pos, rec_c = state
        gp, both, *sums = combine(here, chunk, share, peers, pos, (sg, su), (sg_c, su_c), w, w_c, rec_c, cap)
        gps.append(gp)
        return both, *sums

    r1, x0 = ring(block), send(block, to_x)
    c0, h0, g0 = first([(0, 0)], [block])
    w = join(w_gate[0], w_up[0])
    r1, x0, h0, g0, w, sg_c, su_c = together(r1, x0, h0, g0, w, sg_c, su_c)
    r2, x1 = ring(r1), send(r1, to_x)
    h0, g0, w_c = exchange(h0), exchange(g0), send(w, to_core)
    c1, h1, g1 = first([(1, 0), (0, 1)], [x0, r1])
    h1 = exchange(h1)
    both0, t_r0 = second(c0, h0, g0)
    r2, x1, h1, g1, t_r0, both0 = together(r2, x1, h1, g1, t_r0, both0)
    r3, x2 = ring(r2), send(r2, to_x)
    g1, p0 = exchange(g1), send(both0, to_core)
    c2, h2, g2 = first([(1, 1), (0, 2)], [x1, r2])
    h2 = exchange(h2)
    both1, t_x0, t_r1 = second(c1, h1, g1)
    r3, x2, p0, h2, g2, t_x0, t_r1, both1 = together(r3, x2, p0, h2, g2, t_x0, t_r1, both1)
    x3 = send(r3, to_x)
    g2, p1 = exchange(g2), send(both1, to_core)
    c3, h3, g3 = first([(1, 2), (0, 3)], [x2, r3])
    h3 = exchange(h3)
    both2, t_x1, t_r2 = second(c2, h2, g2)
    x3, p1, h3, g3, t_x1, t_r2, both2 = together(x3, p1, h3, g3, t_x1, t_r2, both2)
    b1 = send(t_x1, to_x)
    g3, p2 = exchange(g3), send(both2, to_core)
    c4, h4, g4 = first([(1, 3)], [x3])
    h4, g4 = exchange(h4), exchange(g4)
    both3, t_x2, t_r3 = second(c3, h3, g3)
    b1, p2, h4, g4, t_x2, t_r3, both3 = together(b1, p2, h4, g4, t_x2, t_r3, both3)
    b2 = send(t_x2, to_x)
    p3 = send(both3, to_core)
    w1 = ring(add(t_r1, b1))
    both4, t_x3 = second(c4, h4, g4)
    b3, p4 = send(t_x3, to_x), send(both4, to_core)
    b2, p3, w1, _ = together(b2, p3, w1, t_x3)
    w2 = ring(add(t_r2, b2, w1))
    away = [p0, p1, p2, p3, p4]
    order_all = order + [(k, col, 1) for k, col, _ in order]
    zeros = [0] * len(recs)
    part = weight_sums(here, order_all, [sg, su], recs + away, zeros + zeros, False, None, cap)
    b3, w2, part, t_x0 = together(b3, w2, part, t_x0)
    w3 = ring(add(t_r3, b3, w2))
    b0 = send(t_x0, to_x)
    skip = [d] * len(recs)
    weight_grads = weight_sums(here, order_all, [saved_inputs[0]], gps + away, zeros + skip, True, part, cap)
    total = add(t_r0, b0, w3)
    return (total, weight_grads)


def solution(mesh):
    placed = (
        P("expert", "dp"),
        P("expert", None),
        P("expert", None),
        P("expert", "dp", None),
        P("expert", "dp", None),
        P("expert", None, "dp"),
        P("expert", None, "dp"),
        P("expert", None, None),
        P("expert", None, None),
    )
    small = mesh.shape["expert"] == 16 and mesh.shape["dp"] == 2
    return jax.shard_map(
        body_grid if small else body_any,
        mesh=mesh,
        in_specs=placed,
        out_specs=(P("expert", "dp"), P("expert", "dp", None)),
        check_vma=False,
    )
```

```python
import functools

import jax
import jax.numpy as jnp
from jax import lax
from jax.experimental import pallas as pl
from jax.experimental.pallas import tpu as pltpu
from jax.sharding import PartitionSpec as P

gate_unit = 0.00390625
loss_scale = 0.015625
f32 = jnp.float32
bf16 = jnp.bfloat16


def contract_rows(left, right):
    return lax.dot_general(left, right, (((0,), (0,)), ((), ())), preferred_element_type=f32)


def contract_cols(left, right):
    return lax.dot_general(left, right, (((1,), (1,)), ((), ())), preferred_element_type=f32)


def activation_grads(grad_hidden, gate_pre, up_pre):
    sigmoid = jax.nn.sigmoid(gate_pre)
    silu = gate_pre * sigmoid
    dsilu = sigmoid * (1.0 + gate_pre * (1.0 - sigmoid))
    grad_gate_pre = (grad_hidden * up_pre * dsilu).astype(bf16)
    grad_up_pre = (grad_hidden * silu).astype(bf16)
    return (grad_gate_pre, grad_up_pre)


def body_any(out_grad, routes, gate_codes, w_gate, w_up, w_down, saved_inputs, saved_gate, saved_up):
    owners = lax.axis_size("expert")
    slot_count = saved_gate.shape[1]
    capacity = slot_count // owners
    token_count = routes.shape[0]
    choice_count = routes.shape[1]
    flat_routes = routes.reshape(-1)
    onehot = (flat_routes[:, None] == jnp.arange(owners, dtype=jnp.int32)[None, :]).astype(jnp.int32)
    earlier = jnp.cumsum(onehot, axis=0) - onehot
    position = jnp.sum(earlier * onehot, axis=1)
    slot_index = (flat_routes * capacity + position).reshape(token_count, choice_count)
    gate_values = gate_codes.astype(f32) * gate_unit
    rows_iota = jnp.arange(slot_count, dtype=jnp.int32)[:, None]
    weighted = jnp.zeros((slot_count, token_count), f32)
    picks = jnp.zeros((slot_count, token_count), f32)
    for pick in range(choice_count):
        hit = rows_iota == slot_index[:, pick][None, :]
        weighted = weighted + jnp.where(hit, gate_values[:, pick][None, :], 0.0)
        picks = picks + hit.astype(f32)
    outgoing = jnp.dot(weighted.astype(bf16), out_grad, preferred_element_type=f32).astype(bf16)
    received = lax.all_to_all(outgoing, "expert", split_axis=0, concat_axis=0, tiled=True)
    hidden_share = lax.psum_scatter(
        contract_cols(received, w_down[0]), "dp", scatter_dimension=0, tiled=True
    )
    gate_pre = saved_gate[0].astype(f32)
    up_pre = saved_up[0].astype(f32)
    hidden = (gate_pre * jax.nn.sigmoid(gate_pre) * up_pre).astype(bf16)
    grad_hidden = lax.all_gather(hidden_share, "dp", axis=0, tiled=True)
    grad_gate_pre, grad_up_pre = activation_grads(grad_hidden, gate_pre, up_pre)
    slot_grads = contract_cols(grad_gate_pre, w_gate[0]) + contract_cols(grad_up_pre, w_up[0])
    returned = lax.all_to_all(
        slot_grads.astype(bf16), "expert", split_axis=0, concat_axis=0, tiled=True
    )
    token_grads = contract_rows(picks.astype(bf16), returned).astype(bf16)
    inputs_here = saved_inputs[0]
    part = jnp.concatenate(
        [
            contract_rows(inputs_here, grad_gate_pre),
            contract_rows(inputs_here, grad_up_pre),
            contract_rows(received, hidden),
        ],
        axis=1,
    )
    return (token_grads, (part * loss_scale).astype(bf16)[None])


on_chip = pl.BlockSpec(memory_space=pltpu.VMEM)
on_scalar = pl.BlockSpec(memory_space=pltpu.SMEM)
anywhere = pl.BlockSpec(memory_space=pl.ANY)
light = pl.CostEstimate(flops=1 << 20, bytes_accessed=1 << 14, transcendentals=0)


def source(here, step, other):
    group = lax.rem(here // 4 + (4 - step), 4)
    return jnp.bitwise_xor(group * 4 + lax.rem(here, 4), 2 * other)


def params(mib):
    return pltpu.CompilerParams(vmem_limit_bytes=mib << 20)


def dispatch_kernel(n, cap, here, *refs):
    toks, (wd0, wd1) = refs[:n], refs[n : n + 2]
    rec0, rec1, share, *share_out, pos_out = refs[n + 2 :]
    tok = toks[0].shape[0] - 8
    line = 256 * pl.cdiv(tok, 256)
    before = lax.broadcasted_iota(jnp.int32, (tok, tok), 0) < lax.broadcasted_iota(jnp.int32, (tok, tok), 1)
    before = jnp.where(before, 1.0, 0.0).astype(bf16)
    slot = lax.broadcasted_iota(jnp.int32, (cap, tok), 0).astype(f32)
    masks, gates = [], []
    for a in range(2):
        expert = jnp.bitwise_xor(here[0], a).astype(f32)
        for t in toks:
            hit = t[tok:, :tok].astype(f32) == expert
            masks.append(jnp.max(jnp.where(hit, 1.0, 0.0), axis=0, keepdims=True))
            gates.append(jnp.sum(jnp.where(hit, t[tok:, line : line + tok].astype(f32), 0.0), axis=0, keepdims=True))
    fill = [jnp.zeros((8 - 2 * n, tok), f32)] if n < 4 else []
    mask = jnp.concatenate(masks + fill, axis=0)
    pos = jnp.dot(mask.astype(bf16), before, preferred_element_type=f32)
    pos = jnp.where(mask > 0.0, pos, -1.0)
    pos_out[...] = pos
    for rel, t in enumerate(toks):
        w = [
            jnp.where(slot == pos[i : i + 1, :], gates[i] * gate_unit, 0.0).astype(bf16)
            for i in (rel, n + rel)
        ]
        rows = jnp.dot(jnp.concatenate(w, axis=0), t[:tok, :], preferred_element_type=f32).astype(bf16)
        rec0[rel * cap : (rel + 1) * cap, :] = rows[:cap]
        rec1[rel * cap : (rel + 1) * cap, :] = rows[cap:]
    for a, (rec, wd) in enumerate(((rec0, wd0), (rec1, wd1))):
        gh = contract_cols(rec[...], wd[...])
        share[a * n * cap : (a + 1) * n * cap, :] = gh
        if n == 1:
            share_out[0][a * cap : (a + 1) * cap, :] = gh.astype(bf16)
        else:
            share_out[a][...] = gh.astype(bf16)


def dispatch(here, toks, wd0, wd1, cap):
    n = len(toks)
    tok, d = toks[0].shape
    h = wd0.shape[0]
    outs = [((n * cap, d), bf16), ((n * cap, d), bf16), ((2 * n * cap, h), f32)]
    outs += [((2 * cap, h), bf16)] if n == 1 else [((n * cap, h), bf16)] * 2
    outs += [((8, tok - 8), f32)]
    return pl.pallas_call(
        functools.partial(dispatch_kernel, n, cap),
        out_shape=[jax.ShapeDtypeStruct(s, t) for s, t in outs],
        in_specs=[on_scalar] + [on_chip] * (n + 2),
        out_specs=[on_chip] * len(outs),
        cost_estimate=light,
        compiler_params=params(16),
        name="dispatch",
    )(here, *toks, wd0, wd1)


def combine_kernel(chunk, cap, here, share, *refs):
    n = len(chunk)
    if n == 1:
        peer0, peer1 = refs[0].at[:cap, :], refs[0].at[cap:, :]
        pos, *refs = refs[1:]
    else:
        peer0, peer1, pos, *refs = refs
    saved, (w0, w1, rec1), (gp0, both) = refs[:4], refs[4:7], refs[7:9]
    backs, (held, sems) = refs[9:-2], refs[-2:]
    d = rec1.shape[1]
    gp1 = both.at[:, d:]
    both[:, :d] = rec1[...]
    h = share.shape[1]
    copies = []
    for a in range(2):
        for other, step in chunk:
            rows = pl.ds(pl.multiple_of(source(here[0], step, other) * cap, 16), cap)
            for v in saved[2 * a : 2 * a + 2]:
                i = len(copies)
                copies.append(pltpu.make_async_copy(v.at[rows, :], held.at[i], sems.at[i]))
    for c in copies:
        c.start()
    slot = lax.broadcasted_iota(jnp.int32, (cap, pos.shape[1]), 0).astype(f32)
    sums = [None] * n
    for a, (gp, w, peer) in enumerate(((gp0, w0, peer0), (gp1, w1, peer1))):
        for rel in range(n):
            i = a * n + rel
            copies[2 * i].wait()
            copies[2 * i + 1].wait()
            gh = share[i * cap : (i + 1) * cap, :] + peer[rel * cap : (rel + 1) * cap, :].astype(f32)
            gg, gu = activation_grads(gh, held[2 * i].astype(f32), held[2 * i + 1].astype(f32))
            gp[rel * cap : (rel + 1) * cap, :h] = gg
            gp[rel * cap : (rel + 1) * cap, h:] = gu
        slots = contract_cols(gp[...], w[...]).astype(bf16)
        for rel in range(n):
            i = a * n + rel
            pick = jnp.where(slot == pos[i : i + 1, :], 1.0, 0.0).astype(bf16)
            part = contract_rows(pick, slots[rel * cap : (rel + 1) * cap])
            sums[rel] = part if sums[rel] is None else sums[rel] + part
    if len(backs) > n:
        half = backs[0].shape[1]
        for k, back in enumerate(backs):
            back[...] = sums[0][:, k * half : (k + 1) * half].astype(bf16)
    else:
        for rel in range(n):
            backs[rel][...] = sums[rel].astype(bf16)


def combine(here, chunk, share, peers, pos, saved0, saved1, w0, w1, rec1, cap, halves=False):
    n = len(chunk)
    h = share.shape[1]
    d = w0.shape[0]
    tok = pos.shape[1]
    outs = [(n * cap, 2 * h), (n * cap, d + 2 * h)] + ([(tok, d // 2)] * 2 if halves else [(tok, d)] * n)
    return pl.pallas_call(
        functools.partial(combine_kernel, chunk, cap),
        out_shape=[jax.ShapeDtypeStruct(s, bf16) for s in outs],
        in_specs=[on_scalar] + [on_chip] * (2 + len(peers)) + [anywhere] * 4 + [on_chip] * 3,
        out_specs=[on_chip] * len(outs),
        scratch_shapes=[pltpu.VMEM((4 * n, cap, h), bf16), pltpu.SemaphoreType.DMA((4 * n,))],
        cost_estimate=light,
        compiler_params=params(20),
        name="combine",
    )(here, share, *peers, pos, *saved0, *saved1, w0, w1, rec1)


def join_kernel(left, right, out):
    out[:, : left.shape[1]] = left[...]
    out[:, left.shape[1] :] = right[...]


def join(left, right):
    rows, h = left.shape
    return pl.pallas_call(
        join_kernel,
        out_shape=jax.ShapeDtypeStruct((rows, 2 * h), left.dtype),
        in_specs=[on_chip] * 2,
        out_specs=on_chip,
        cost_estimate=light,
        compiler_params=params(8),
        name="join",
    )(left, right)


def add_kernel(part, *refs):
    wide = refs[-1].shape[1]
    total = None
    for r in refs[:-1]:
        v = r[...] if part is None or r.shape[1] == wide else r[:, part * wide : (part + 1) * wide]
        total = v.astype(f32) if total is None else total + v.astype(f32)
    refs[-1][...] = total.astype(bf16)


def add(values, part=None):
    rows, wide = values[0].shape
    return pl.pallas_call(
        functools.partial(add_kernel, part),
        out_shape=jax.ShapeDtypeStruct((rows, wide if part is None else wide // 2), bf16),
        in_specs=[on_chip] * len(values),
        out_specs=on_chip,
        cost_estimate=light,
        compiler_params=params(8),
        name="add",
    )(*values)


def finish_kernel(a, b, left, right, out):
    half = left.shape[1]
    for at, v in ((0, left), (half, right)):
        total = a[:, at : at + half].astype(f32) + b[:, at : at + half].astype(f32) + v[...].astype(f32)
        out[:, at : at + half] = total.astype(bf16)


def finish(a, b, left, right):
    return pl.pallas_call(
        finish_kernel,
        out_shape=jax.ShapeDtypeStruct(a.shape, bf16),
        in_specs=[on_chip] * 4,
        out_specs=on_chip,
        cost_estimate=light,
        compiler_params=params(8),
        name="finish",
    )(a, b, left, right)


def hidden_kernel(gate, up, out):
    gate_pre = gate[...].astype(f32)
    out[...] = (gate_pre * jax.nn.sigmoid(gate_pre) * up[...].astype(f32)).astype(bf16)


def hidden(gate, up):
    rows, h = gate.shape
    tile = rows // 4
    spec = pl.BlockSpec((tile, h), lambda i: (i, 0))
    return pl.pallas_call(
        hidden_kernel,
        out_shape=jax.ShapeDtypeStruct((rows, h), bf16),
        grid=(rows // tile,),
        in_specs=[spec, spec],
        out_specs=spec,
        cost_estimate=light,
        compiler_params=params(8),
        name="hidden",
    )(gate, up)


def pack_kernel(line, tokens, routes, codes, out):
    tok = tokens.shape[0]
    out[:tok, :] = tokens[...]
    same = lax.broadcasted_iota(jnp.int32, (tok, tok), 0) == lax.broadcasted_iota(jnp.int32, (tok, tok), 1)
    same = jnp.where(same, 1.0, 0.0).astype(bf16)
    out[tok:, :] = jnp.zeros((8, out.shape[1]), bf16)
    for at, v in ((0, routes), (line, codes)):
        out[tok:, at : at + tok] = contract_rows(v[...].astype(f32).astype(bf16), same).astype(bf16)


def pack(tokens, routes, codes, line):
    tok, d = tokens.shape
    return pl.pallas_call(
        functools.partial(pack_kernel, line),
        out_shape=jax.ShapeDtypeStruct((tok + 8, d), bf16),
        in_specs=[on_chip] * 3,
        out_specs=on_chip,
        cost_estimate=light,
        compiler_params=params(8),
        name="pack",
    )(tokens, routes, codes)


def weights_kernel(order, cap, sorted_left, starts, base_tile, here, *refs):
    count = 1
    by_source, pieces, out = refs[:count], refs[count:-5], refs[-5]
    ls, rs, left_sems, right_sems = refs[-4:]
    i = pl.program_id(0)
    tile = ls.shape[2]
    steps = pl.num_programs(0)

    def copies_of_sorted(v, column, to, sems):
        made = []
        for p, (step, other, plane) in enumerate(order):
            src = jnp.bitwise_xor(source(here[0], step, other), plane)
            rows = pl.ds(pl.multiple_of(src * cap, 16), cap)
            at = v.at[rows, :] if column is None else v.at[rows, pl.ds(pl.multiple_of(column * tile, 128), tile)]
            made.append(pltpu.make_async_copy(at, to.at[pl.ds(p * cap, cap), :], sems.at[len(made)]))
        return made

    def copies_of_pieces(column, to, sems):
        made, base = [], 0
        for r, first in zip(pieces, starts):
            if column is None:
                at = r.at[:, pl.ds(first, to.shape[1])]
            else:
                at = r.at[:, pl.ds(pl.multiple_of(first + column * tile, 128), tile)]
            made.append(pltpu.make_async_copy(at, to.at[pl.ds(base, r.shape[0]), :], sems.at[len(made)]))
            base += r.shape[0]
        return made

    def left(step):
        slot = lax.rem(step, 2)
        if sorted_left:
            return copies_of_sorted(by_source[0], base_tile + step, ls.at[slot], left_sems.at[slot])
        return copies_of_pieces(base_tile + step, ls.at[slot], left_sems.at[slot])

    def right():
        if sorted_left:
            return copies_of_pieces(None, rs.at[0], right_sems.at[0])
        return copies_of_sorted(by_source[0], None, rs.at[0], right_sems.at[0])

    @pl.when(i == 0)
    def _():
        for c in right() + left(i):
            c.start()

    @pl.when(i + 1 < steps)
    def _():
        for c in left(i + 1):
            c.start()

    @pl.when(i == 0)
    def _():
        for c in right():
            c.wait()

    for c in left(i):
        c.wait()

    out[0] = (contract_rows(ls[lax.rem(i, 2)], rs[0]) * loss_scale).astype(bf16)


def weight_sums(here, order, by_source, pieces, starts, sorted_left, tiles, into, cap):
    slots, wide = by_source[0].shape
    d = pieces[0].shape[1]
    if sorted_left:
        d, wide = wide, d
    tile = 256
    at = 0 if sorted_left else 2
    whole_out = jax.ShapeDtypeStruct((1, d, 3 * (wide // 2 if sorted_left else wide)), bf16)
    given = [*by_source, *pieces]
    kernel = functools.partial(weights_kernel, order, cap, sorted_left, starts, tiles[0])
    body = kernel if into is None else (lambda here, old, *refs: kernel(here, *refs))
    return pl.pallas_call(
        body,
        out_shape=whole_out,
        grid_spec=pltpu.PrefetchScalarGridSpec(
            num_scalar_prefetch=1,
            grid=(tiles[1],),
            in_specs=[anywhere] * (len(given) + (into is not None)),
            out_specs=pl.BlockSpec((1, tile, wide), lambda i, here: (0, tiles[0] + i, at)),
            scratch_shapes=[
                pltpu.VMEM((2, slots, tile), bf16),
                pltpu.VMEM((len(by_source), slots, wide), bf16),
                pltpu.SemaphoreType.DMA((2, len(order))),
                pltpu.SemaphoreType.DMA((len(by_source), len(order))),
            ],
        ),
        input_output_aliases={} if into is None else {1: 0},
        cost_estimate=light,
        compiler_params=params(20),
        name="weights",
    )(here, *([] if into is None else [into]), *given)


def together(*values):
    return lax.optimization_barrier(values)


def body_grid(out_grad, routes, gate_codes, w_gate, w_up, w_down, saved_inputs, saved_gate, saved_up):
    owners = lax.axis_size("expert")
    me = lax.axis_index("expert")
    to_core = [(i, i ^ 1) for i in range(owners)]
    to_x = [(i, i ^ 2) for i in range(owners)]
    tok, d = out_grad.shape
    choices = routes.shape[1]
    slots = saved_gate.shape[1]
    cap = slots // owners

    def send(v, perm):
        return lax.ppermute(v, "expert", perm)

    line = 256 * pl.cdiv(tok, 256)
    block = pack(out_grad, routes, gate_codes, line)
    here = me.reshape(1).astype(jnp.int32)

    def ring(v, hops=1):
        return send(v, [(i, (i + 4 * hops) % owners) for i in range(owners)])

    wd, sg, su = w_down[0], saved_gate[0], saved_up[0]
    wd_c, sg_c, su_c = [send(v, to_core) for v in (wd, sg, su)]

    order, recs, gps = [], [], []

    def first(chunk, toks):
        rec, rec_c, share, *shares, pos = dispatch(here, toks, wd, wd_c, cap)
        order.extend((k, col, 0) for col, k in chunk)
        recs.append(rec)
        return (chunk, share, pos, rec_c), *shares

    def exchange(v):
        return lax.ppermute(v, "dp", [(0, 1), (1, 0)])

    def second(state, *peers, halves=False):
        chunk, share, pos, rec_c = state
        gp, both, *sums = combine(here, chunk, share, peers, pos, (sg, su), (sg_c, su_c), w, w_c, rec_c, cap, halves)
        gps.append(gp)
        return both, *sums

    r1, x0 = ring(block), send(block, to_x)
    c0, h0 = first([(0, 0)], [block])
    w = join(w_gate[0], w_up[0])
    hid = hidden(sg, su)
    r1, x0, h0, w, hid, sg_c, su_c = together(r1, x0, h0, w, hid, sg_c, su_c)
    r2, x1 = ring(r1), send(r1, to_x)
    h0, w_c = exchange(h0), send(w, to_core)
    c1, h1, g1 = first([(1, 0), (0, 1)], [x0, r1])
    h1 = exchange(h1)
    both0, t_r0 = second(c0, h0)
    r2, x1, h1, g1, t_r0, both0 = together(r2, x1, h1, g1, t_r0, both0)
    r3, x2 = ring(r2), send(r2, to_x)
    g1 = exchange(g1)
    c2, h2, g2 = first([(1, 1), (0, 2)], [x1, r2])
    h2, p0 = exchange(h2), send(both0, to_core)
    both1, t_x0, t_r1 = second(c1, h1, g1)
    r3, x2, p0, h2, g2, t_x0, t_r1, both1 = together(r3, x2, p0, h2, g2, t_x0, t_r1, both1)
    x3, w1 = send(r3, to_x), ring(t_r1)
    g2 = exchange(g2)
    c3, h3, g3 = first([(1, 2), (0, 3)], [x2, r3])
    h3, p1 = exchange(h3), send(both1, to_core)
    both2, t_x1, t_r2 = second(c2, h2, g2)
    x3, w1, p1, h3, g3, t_x1, t_r2, both2 = together(x3, w1, p1, h3, g3, t_x1, t_r2, both2)
    u1, b0 = ring(t_x1), send(t_x0, to_x)
    g3 = exchange(g3)
    c4, h4 = first([(1, 3)], [x3])
    h4, p2 = exchange(h4), send(both2, to_core)
    both3, t_x2, t_r3 = second(c3, h3, g3)
    u1, b0, p2, h4, t_x2, t_r3, both3 = together(u1, b0, p2, h4, t_x2, t_r3, both3)
    a0, a1, h4 = together(add([t_x2, u1], 0), add([t_x2, u1], 1), h4)
    b2 = [send(a0, to_x), send(a1, to_x)]
    p3 = send(both3, to_core)
    both4, *t_x3 = second(c4, h4, halves=True)
    b3 = [send(t, to_x) for t in t_x3]
    b2[0], p3, both4, _ = together(b2[0], p3, both4, t_x3[0])
    p4 = send(both4, to_core)
    away = [p0, p1, p2, p3, p4]
    order_all = order + [(k, col, 1) for k, col, _ in order]
    zeros, skip = [0] * len(recs), [d] * len(recs)

    def received_part(tiles, into):
        return weight_sums(here, order_all, [hid], recs + away, zeros + zeros, False, tiles, into, cap)

    def inputs_part(tiles, into):
        return weight_sums(here, order_all, [saved_inputs[0]], gps + away, zeros + skip, True, tiles, into, cap)

    tiles = d // 256
    low, high = (0, tiles // 2), (tiles // 2, tiles - tiles // 2)
    w2 = [ring(add([t_r2, w1, b2[0]], 0))]
    part = received_part(low, None)
    b2[1], part = together(b2[1], part)
    w2.append(ring(add([t_r2, w1, b2[1]], 1)))
    part = received_part(high, part)
    b3[0], w2[0], part = together(b3[0], w2[0], part)
    w3 = [ring(add([t_r3, b3[0], w2[0]], 0))]
    part = inputs_part(low, part)
    b3[1], w2[1], part = together(b3[1], w2[1], part)
    w3.append(ring(add([t_r3, b3[1], w2[1]], 1)))
    weight_grads = inputs_part(high, part)
    return (finish(t_r0, b0, *w3), weight_grads)


def solution(mesh):
    placed = (
        P("expert", "dp"),
        P("expert", None),
        P("expert", None),
        P("expert", "dp", None),
        P("expert", "dp", None),
        P("expert", None, "dp"),
        P("expert", None, "dp"),
        P("expert", None, None),
        P("expert", None, None),
    )
    small = mesh.shape["expert"] == 16 and mesh.shape["dp"] == 2
    return jax.shard_map(
        body_grid if small else body_any,
        mesh=mesh,
        in_specs=placed,
        out_specs=(P("expert", "dp"), P("expert", "dp", None)),
        check_vma=False,
    )
```

```python
import functools

import jax
import jax.numpy as jnp
from jax import lax
from jax.experimental import pallas as pl
from jax.experimental.pallas import tpu as pltpu
from jax.sharding import PartitionSpec as P

gate_unit = 0.00390625
loss_scale = 0.015625
f32 = jnp.float32
bf16 = jnp.bfloat16


def contract_rows(left, right):
    return lax.dot_general(left, right, (((0,), (0,)), ((), ())), preferred_element_type=f32)


def contract_cols(left, right):
    return lax.dot_general(left, right, (((1,), (1,)), ((), ())), preferred_element_type=f32)


def activation_grads(grad_hidden, gate_pre, up_pre):
    sigmoid = jax.nn.sigmoid(gate_pre)
    silu = gate_pre * sigmoid
    dsilu = sigmoid * (1.0 + gate_pre * (1.0 - sigmoid))
    grad_gate_pre = (grad_hidden * up_pre * dsilu).astype(bf16)
    grad_up_pre = (grad_hidden * silu).astype(bf16)
    return (grad_gate_pre, grad_up_pre)


def body_any(out_grad, routes, gate_codes, w_gate, w_up, w_down, saved_inputs, saved_gate, saved_up):
    owners = lax.axis_size("expert")
    slot_count = saved_gate.shape[1]
    capacity = slot_count // owners
    token_count = routes.shape[0]
    choice_count = routes.shape[1]
    flat_routes = routes.reshape(-1)
    onehot = (flat_routes[:, None] == jnp.arange(owners, dtype=jnp.int32)[None, :]).astype(jnp.int32)
    earlier = jnp.cumsum(onehot, axis=0) - onehot
    position = jnp.sum(earlier * onehot, axis=1)
    slot_index = (flat_routes * capacity + position).reshape(token_count, choice_count)
    gate_values = gate_codes.astype(f32) * gate_unit
    rows_iota = jnp.arange(slot_count, dtype=jnp.int32)[:, None]
    weighted = jnp.zeros((slot_count, token_count), f32)
    picks = jnp.zeros((slot_count, token_count), f32)
    for pick in range(choice_count):
        hit = rows_iota == slot_index[:, pick][None, :]
        weighted = weighted + jnp.where(hit, gate_values[:, pick][None, :], 0.0)
        picks = picks + hit.astype(f32)
    outgoing = jnp.dot(weighted.astype(bf16), out_grad, preferred_element_type=f32).astype(bf16)
    received = lax.all_to_all(outgoing, "expert", split_axis=0, concat_axis=0, tiled=True)
    hidden_share = lax.psum_scatter(
        contract_cols(received, w_down[0]), "dp", scatter_dimension=0, tiled=True
    )
    gate_pre = saved_gate[0].astype(f32)
    up_pre = saved_up[0].astype(f32)
    hidden = (gate_pre * jax.nn.sigmoid(gate_pre) * up_pre).astype(bf16)
    grad_hidden = lax.all_gather(hidden_share, "dp", axis=0, tiled=True)
    grad_gate_pre, grad_up_pre = activation_grads(grad_hidden, gate_pre, up_pre)
    slot_grads = contract_cols(grad_gate_pre, w_gate[0]) + contract_cols(grad_up_pre, w_up[0])
    returned = lax.all_to_all(
        slot_grads.astype(bf16), "expert", split_axis=0, concat_axis=0, tiled=True
    )
    token_grads = contract_rows(picks.astype(bf16), returned).astype(bf16)
    inputs_here = saved_inputs[0]
    part = jnp.concatenate(
        [
            contract_rows(inputs_here, grad_gate_pre),
            contract_rows(inputs_here, grad_up_pre),
            contract_rows(received, hidden),
        ],
        axis=1,
    )
    return (token_grads, (part * loss_scale).astype(bf16)[None])


on_chip = pl.BlockSpec(memory_space=pltpu.VMEM)
on_scalar = pl.BlockSpec(memory_space=pltpu.SMEM)
anywhere = pl.BlockSpec(memory_space=pl.ANY)
light = pl.CostEstimate(flops=1 << 20, bytes_accessed=1 << 14, transcendentals=0)


def source(here, step, other):
    group = lax.rem(here // 4 + (4 - step), 4)
    return jnp.bitwise_xor(group * 4 + lax.rem(here, 4), 2 * other)


def params(mib):
    return pltpu.CompilerParams(vmem_limit_bytes=mib << 20)


def dispatch_kernel(n, cap, here, *refs):
    toks, (wd0, wd1) = refs[:n], refs[n : n + 2]
    rec0, rec1, share, *share_out, pos_out = refs[n + 2 :]
    tok = toks[0].shape[0] - 8
    line = 256 * pl.cdiv(tok, 256)
    before = lax.broadcasted_iota(jnp.int32, (tok, tok), 0) < lax.broadcasted_iota(jnp.int32, (tok, tok), 1)
    before = jnp.where(before, 1.0, 0.0).astype(bf16)
    slot = lax.broadcasted_iota(jnp.int32, (cap, tok), 0).astype(f32)
    masks, gates = [], []
    for a in range(2):
        expert = jnp.bitwise_xor(here[0], a).astype(f32)
        for t in toks:
            hit = t[tok:, :tok].astype(f32) == expert
            masks.append(jnp.max(jnp.where(hit, 1.0, 0.0), axis=0, keepdims=True))
            gates.append(jnp.sum(jnp.where(hit, t[tok:, line : line + tok].astype(f32), 0.0), axis=0, keepdims=True))
    fill = [jnp.zeros((8 - 2 * n, tok), f32)] if n < 4 else []
    mask = jnp.concatenate(masks + fill, axis=0)
    pos = jnp.dot(mask.astype(bf16), before, preferred_element_type=f32)
    pos = jnp.where(mask > 0.0, pos, -1.0)
    pos_out[...] = pos
    for rel, t in enumerate(toks):
        w = [
            jnp.where(slot == pos[i : i + 1, :], gates[i] * gate_unit, 0.0).astype(bf16)
            for i in (rel, n + rel)
        ]
        rows = jnp.dot(jnp.concatenate(w, axis=0), t[:tok, :], preferred_element_type=f32).astype(bf16)
        rec0[rel * cap : (rel + 1) * cap, :] = rows[:cap]
        rec1[rel * cap : (rel + 1) * cap, :] = rows[cap:]
    for a, (rec, wd) in enumerate(((rec0, wd0), (rec1, wd1))):
        gh = contract_cols(rec[...], wd[...])
        share[a * n * cap : (a + 1) * n * cap, :] = gh
        if n == 1:
            share_out[0][a * cap : (a + 1) * cap, :] = gh.astype(bf16)
        else:
            share_out[a][...] = gh.astype(bf16)


def dispatch(here, toks, wd0, wd1, cap):
    n = len(toks)
    tok, d = toks[0].shape
    h = wd0.shape[0]
    outs = [((n * cap, d), bf16), ((n * cap, d), bf16), ((2 * n * cap, h), f32)]
    outs += [((2 * cap, h), bf16)] if n == 1 else [((n * cap, h), bf16)] * 2
    outs += [((8, tok - 8), f32)]
    return pl.pallas_call(
        functools.partial(dispatch_kernel, n, cap),
        out_shape=[jax.ShapeDtypeStruct(s, t) for s, t in outs],
        in_specs=[on_scalar] + [on_chip] * (n + 2),
        out_specs=[on_chip] * len(outs),
        cost_estimate=light,
        compiler_params=params(16),
        name="dispatch",
    )(here, *toks, wd0, wd1)


def combine_kernel(chunk, cap, here, share, *refs):
    n = len(chunk)
    if n == 1:
        peer0, peer1 = refs[0].at[:cap, :], refs[0].at[cap:, :]
        pos, *refs = refs[1:]
    else:
        peer0, peer1, pos, *refs = refs
    saved, (w0, w1, rec1), (gp0, both) = refs[:4], refs[4:7], refs[7:9]
    backs, (held, sems) = refs[9:-2], refs[-2:]
    d = rec1.shape[1]
    gp1 = both.at[:, d:]
    both[:, :d] = rec1[...]
    h = share.shape[1]
    copies = []
    for a in range(2):
        for other, step in chunk:
            rows = pl.ds(pl.multiple_of(source(here[0], step, other) * cap, 16), cap)
            for v in saved[2 * a : 2 * a + 2]:
                i = len(copies)
                copies.append(pltpu.make_async_copy(v.at[rows, :], held.at[i], sems.at[i]))
    for c in copies:
        c.start()
    slot = lax.broadcasted_iota(jnp.int32, (cap, pos.shape[1]), 0).astype(f32)
    sums = [None] * n
    for a, (gp, w, peer) in enumerate(((gp0, w0, peer0), (gp1, w1, peer1))):
        for rel in range(n):
            i = a * n + rel
            copies[2 * i].wait()
            copies[2 * i + 1].wait()
            gh = share[i * cap : (i + 1) * cap, :] + peer[rel * cap : (rel + 1) * cap, :].astype(f32)
            gg, gu = activation_grads(gh, held[2 * i].astype(f32), held[2 * i + 1].astype(f32))
            gp[rel * cap : (rel + 1) * cap, :h] = gg
            gp[rel * cap : (rel + 1) * cap, h:] = gu
        slots = contract_cols(gp[...], w[...]).astype(bf16)
        for rel in range(n):
            i = a * n + rel
            pick = jnp.where(slot == pos[i : i + 1, :], 1.0, 0.0).astype(bf16)
            part = contract_rows(pick, slots[rel * cap : (rel + 1) * cap])
            sums[rel] = part if sums[rel] is None else sums[rel] + part
    if len(backs) > n:
        half = backs[0].shape[1]
        for k, back in enumerate(backs):
            back[...] = sums[0][:, k * half : (k + 1) * half].astype(bf16)
    else:
        for rel in range(n):
            backs[rel][...] = sums[rel].astype(bf16)


def combine(here, chunk, share, peers, pos, saved0, saved1, w0, w1, rec1, cap, halves=False):
    n = len(chunk)
    h = share.shape[1]
    d = w0.shape[0]
    tok = pos.shape[1]
    outs = [(n * cap, 2 * h), (n * cap, d + 2 * h)] + ([(tok, d // 2)] * 2 if halves else [(tok, d)] * n)
    return pl.pallas_call(
        functools.partial(combine_kernel, chunk, cap),
        out_shape=[jax.ShapeDtypeStruct(s, bf16) for s in outs],
        in_specs=[on_scalar] + [on_chip] * (2 + len(peers)) + [anywhere] * 4 + [on_chip] * 3,
        out_specs=[on_chip] * len(outs),
        scratch_shapes=[pltpu.VMEM((4 * n, cap, h), bf16), pltpu.SemaphoreType.DMA((4 * n,))],
        cost_estimate=light,
        compiler_params=params(20),
        name="combine",
    )(here, share, *peers, pos, *saved0, *saved1, w0, w1, rec1)


def join_kernel(left, right, out):
    out[:, : left.shape[1]] = left[...]
    out[:, left.shape[1] :] = right[...]


def join(left, right):
    rows, h = left.shape
    return pl.pallas_call(
        join_kernel,
        out_shape=jax.ShapeDtypeStruct((rows, 2 * h), left.dtype),
        in_specs=[on_chip] * 2,
        out_specs=on_chip,
        cost_estimate=light,
        compiler_params=params(8),
        name="join",
    )(left, right)


def add_kernel(part, *refs):
    wide = refs[-1].shape[1]
    total = None
    for r in refs[:-1]:
        v = r[...] if part is None or r.shape[1] == wide else r[:, part * wide : (part + 1) * wide]
        total = v.astype(f32) if total is None else total + v.astype(f32)
    refs[-1][...] = total.astype(bf16)


def add(values, part=None):
    rows, wide = values[0].shape
    return pl.pallas_call(
        functools.partial(add_kernel, part),
        out_shape=jax.ShapeDtypeStruct((rows, wide if part is None else wide // 2), bf16),
        in_specs=[on_chip] * len(values),
        out_specs=on_chip,
        cost_estimate=light,
        compiler_params=params(8),
        name="add",
    )(*values)


def finish_kernel(a, b, left, right, out):
    half = left.shape[1]
    for at, v in ((0, left), (half, right)):
        total = a[:, at : at + half].astype(f32) + b[:, at : at + half].astype(f32) + v[...].astype(f32)
        out[:, at : at + half] = total.astype(bf16)


def finish(a, b, left, right):
    return pl.pallas_call(
        finish_kernel,
        out_shape=jax.ShapeDtypeStruct(a.shape, bf16),
        in_specs=[on_chip] * 4,
        out_specs=on_chip,
        cost_estimate=light,
        compiler_params=params(8),
        name="finish",
    )(a, b, left, right)


def in_hbm(v):
    return pltpu.with_memory_space_constraint(v, pltpu.HBM)


def hidden_kernel(gate, up, out):
    gate_pre = gate[...].astype(f32)
    out[...] = (gate_pre * jax.nn.sigmoid(gate_pre) * up[...].astype(f32)).astype(bf16).T


def hidden(gate, up):
    rows, h = gate.shape
    tile = 768
    spec = pl.BlockSpec((tile, h), lambda i: (i, 0))
    return pl.pallas_call(
        hidden_kernel,
        out_shape=jax.ShapeDtypeStruct((h, rows), bf16),
        grid=(rows // tile,),
        in_specs=[spec, spec],
        out_specs=pl.BlockSpec((h, tile), lambda i: (0, i)),
        cost_estimate=light,
        compiler_params=params(12),
        name="hidden",
    )(in_hbm(gate), in_hbm(up))


def turn_kernel(v, out):
    out[...] = v[...].T


def turn(v):
    rows, d = v.shape
    tile = 256
    return pl.pallas_call(
        turn_kernel,
        out_shape=jax.ShapeDtypeStruct((d, rows), v.dtype),
        grid=(d // tile,),
        in_specs=[pl.BlockSpec((rows, tile), lambda i: (0, i))],
        out_specs=pl.BlockSpec((tile, rows), lambda i: (i, 0)),
        cost_estimate=light,
        compiler_params=params(12),
        name="turn",
    )(in_hbm(v))


def pack_kernel(line, tokens, routes, codes, out, named, sems):
    tok = tokens.shape[0]
    copies = [
        pltpu.make_async_copy(tokens, out.at[:tok, :], sems.at[0]),
        pltpu.make_async_copy(routes, named.at[0], sems.at[1]),
        pltpu.make_async_copy(codes, named.at[1], sems.at[2]),
    ]
    for c in copies:
        c.start()
    out[tok:, :] = jnp.zeros((8, out.shape[1]), bf16)
    for k, at in enumerate((0, line)):
        copies[1 + k].wait()
        out[tok:, at : at + tok] = named[k].astype(f32).astype(bf16)
    copies[0].wait()


def pack(tokens, routes, codes, line):
    tok, d = tokens.shape
    return pl.pallas_call(
        functools.partial(pack_kernel, line),
        out_shape=jax.ShapeDtypeStruct((tok + 8, d), bf16),
        in_specs=[anywhere] * 3,
        out_specs=on_chip,
        scratch_shapes=[pltpu.VMEM((2, *routes.shape), jnp.int32), pltpu.SemaphoreType.DMA((3,))],
        cost_estimate=light,
        compiler_params=params(8),
        name="pack",
    )(in_hbm(tokens), in_hbm(routes), in_hbm(codes))


def weights_kernel(order, cap, starts, left_whole, here, left, *refs):
    pieces, out, held, sems = refs[:-3], refs[-3], refs[-2], refs[-1]
    i = pl.program_id(0)
    wide = held.shape[2]

    def copies(step):
        slot = lax.rem(step, 2) if left_whole else 0
        made = []
        for r, first in zip(pieces, starts):
            column = pl.ds(pl.multiple_of(first + step * wide, 128), wide) if left_whole else pl.ds(first, wide)
            for at in range(0, r.shape[0], cap):
                k, other, plane = order[len(made)]
                src = jnp.bitwise_xor(source(here[0], k, other), plane)
                to = held.at[slot, pl.ds(pl.multiple_of(src * cap, 16), cap), :]
                made.append(pltpu.make_async_copy(r.at[pl.ds(at, cap), column], to, sems.at[slot, len(made)]))
        return made

    @pl.when(i == 0)
    def _():
        for c in copies(i):
            c.start()

    if left_whole:
        @pl.when(i + 1 < pl.num_programs(0))
        def _():
            for c in copies(i + 1):
                c.start()

        for c in copies(i):
            c.wait()
        part = jnp.dot(left[...], held[lax.rem(i, 2)], preferred_element_type=f32)
        out[0] = (part * loss_scale).astype(bf16).T
    else:
        @pl.when(i == 0)
        def _():
            for c in copies(i):
                c.wait()

        part = jnp.dot(left[...], held[0], preferred_element_type=f32)
        out[0] = (part * loss_scale).astype(bf16)


def weight_sums(here, order, left, pieces, starts, left_whole, into, cap, d):
    rows, slots = left.shape
    tile = 256
    h = rows if left_whole else (pieces[0].shape[1] // 2)
    wide, at = (h, 2) if left_whole else (2 * h, 0)
    kernel = functools.partial(weights_kernel, order, cap, starts, left_whole)
    body = kernel if into is None else (lambda here, old, *refs: kernel(here, *refs))
    left_spec = pl.BlockSpec((rows, slots), lambda i, here: (0, 0))
    if not left_whole:
        left_spec = pl.BlockSpec((tile, slots), lambda i, here: (i, 0))
    held = (2, slots, tile) if left_whole else (1, slots, wide)
    return pl.pallas_call(
        body,
        out_shape=jax.ShapeDtypeStruct((1, d, 3 * h), bf16),
        grid_spec=pltpu.PrefetchScalarGridSpec(
            num_scalar_prefetch=1,
            grid=(d // tile,),
            in_specs=[anywhere] * (into is not None) + [left_spec] + [anywhere] * len(pieces),
            out_specs=pl.BlockSpec((1, tile, wide), lambda i, here: (0, i, at)),
            scratch_shapes=[pltpu.VMEM(held, bf16), pltpu.SemaphoreType.DMA((2, len(order)))],
        ),
        input_output_aliases={} if into is None else {1: 0},
        cost_estimate=light,
        compiler_params=params(20),
        name="weights",
    )(here, *([] if into is None else [into]), left, *pieces)


def together(*values):
    return lax.optimization_barrier(values)


def body_grid(out_grad, routes, gate_codes, w_gate, w_up, w_down, saved_inputs, saved_gate, saved_up):
    owners = lax.axis_size("expert")
    me = lax.axis_index("expert")
    to_core = [(i, i ^ 1) for i in range(owners)]
    to_x = [(i, i ^ 2) for i in range(owners)]
    tok, d = out_grad.shape
    choices = routes.shape[1]
    slots = saved_gate.shape[1]
    cap = slots // owners

    def send(v, perm):
        return lax.ppermute(v, "expert", perm)

    line = 256 * pl.cdiv(tok, 256)
    block = pack(out_grad, routes.T, gate_codes.T, line)
    here = me.reshape(1).astype(jnp.int32)

    def ring(v, hops=1):
        return send(v, [(i, (i + 4 * hops) % owners) for i in range(owners)])

    wd, sg, su = w_down[0], saved_gate[0], saved_up[0]
    wd_c, sg_c, su_c = [send(v, to_core) for v in (wd, sg, su)]

    order, recs, gps = [], [], []

    def first(chunk, toks):
        rec, rec_c, share, *shares, pos = dispatch(here, toks, wd, wd_c, cap)
        order.extend((k, col, 0) for col, k in chunk)
        recs.append(rec)
        return (chunk, share, pos, rec_c), *shares

    def exchange(v):
        return lax.ppermute(v, "dp", [(0, 1), (1, 0)])

    def second(state, *peers, halves=False):
        chunk, share, pos, rec_c = state
        gp, both, *sums = combine(here, chunk, share, peers, pos, (sg, su), (sg_c, su_c), w, w_c, rec_c, cap, halves)
        gps.append(gp)
        return both, *sums

    r1, x0 = ring(block), send(block, to_x)
    c0, h0 = first([(0, 0)], [block])
    w = join(w_gate[0], w_up[0])
    hid, inputs = hidden(sg, su), turn(saved_inputs[0])
    r1, x0, h0, w, hid, inputs, sg_c, su_c = together(r1, x0, h0, w, hid, inputs, sg_c, su_c)
    r2, x1 = ring(r1), send(r1, to_x)
    h0, w_c = exchange(h0), send(w, to_core)
    c1, h1, g1 = first([(1, 0), (0, 1)], [x0, r1])
    h1 = exchange(h1)
    both0, t_r0 = second(c0, h0)
    r2, x1, h1, g1, t_r0, both0 = together(r2, x1, h1, g1, t_r0, both0)
    r3, x2 = ring(r2), send(r2, to_x)
    g1 = exchange(g1)
    c2, h2, g2 = first([(1, 1), (0, 2)], [x1, r2])
    h2, p0 = exchange(h2), send(both0, to_core)
    both1, t_x0, t_r1 = second(c1, h1, g1)
    r3, x2, p0, h2, g2, t_x0, t_r1, both1 = together(r3, x2, p0, h2, g2, t_x0, t_r1, both1)
    x3, w1 = send(r3, to_x), ring(t_r1)
    g2 = exchange(g2)
    c3, h3, g3 = first([(1, 2), (0, 3)], [x2, r3])
    h3, p1 = exchange(h3), send(both1, to_core)
    both2, t_x1, t_r2 = second(c2, h2, g2)
    x3, w1, p1, h3, g3, t_x1, t_r2, both2 = together(x3, w1, p1, h3, g3, t_x1, t_r2, both2)
    u1, b0 = ring(t_x1), send(t_x0, to_x)
    g3 = exchange(g3)
    c4, h4 = first([(1, 3)], [x3])
    h4, p2 = exchange(h4), send(both2, to_core)
    both3, t_x2, t_r3 = second(c3, h3, g3)
    u1, b0, p2, h4, t_x2, t_r3, both3 = together(u1, b0, p2, h4, t_x2, t_r3, both3)
    a0, a1, h4 = together(add([t_x2, u1], 0), add([t_x2, u1], 1), h4)
    b2 = [send(a0, to_x), send(a1, to_x)]
    p3 = send(both3, to_core)
    both4, *t_x3 = second(c4, h4, halves=True)
    b3 = [send(t, to_x) for t in t_x3]
    b2[0], p3, both4, _ = together(b2[0], p3, both4, t_x3[0])
    p4 = send(both4, to_core)
    away = [p0, p1, p2, p3, p4]
    order_all = order + [(k, col, 1) for k, col, _ in order]
    zeros, skip = [0] * len(recs), [d] * len(recs)

    w2 = [ring(add([t_r2, w1, b2[0]], 0))]
    part = weight_sums(here, order_all, hid, recs + away, zeros + zeros, True, None, cap, d)
    b2[1], part = together(b2[1], part)
    w2.append(ring(add([t_r2, w1, b2[1]], 1)))
    weight_grads = weight_sums(here, order_all, inputs, gps + away, zeros + skip, False, part, cap, d)
    b3[0], w2[0], weight_grads = together(b3[0], w2[0], weight_grads)
    w3 = [ring(add([t_r3, b3[0], w2[0]], 0)), ring(add([t_r3, b3[1], w2[1]], 1))]
    return (finish(t_r0, b0, *w3), weight_grads)


def solution(mesh):
    placed = (
        P("expert", "dp"),
        P("expert", None),
        P("expert", None),
        P("expert", "dp", None),
        P("expert", "dp", None),
        P("expert", None, "dp"),
        P("expert", None, "dp"),
        P("expert", None, None),
        P("expert", None, None),
    )
    small = mesh.shape["expert"] == 16 and mesh.shape["dp"] == 2
    return jax.shard_map(
        body_grid if small else body_any,
        mesh=mesh,
        in_specs=placed,
        out_specs=(P("expert", "dp"), P("expert", "dp", None)),
        check_vma=False,
    )
```

```python
import functools

import jax
import jax.numpy as jnp
from jax import lax
from jax.experimental import pallas as pl
from jax.experimental.pallas import tpu as pltpu
from jax.sharding import PartitionSpec as P

gate_unit = 0.00390625
loss_scale = 0.015625
f32 = jnp.float32
bf16 = jnp.bfloat16


def contract_rows(left, right):
    return lax.dot_general(left, right, (((0,), (0,)), ((), ())), preferred_element_type=f32)


def contract_cols(left, right):
    return lax.dot_general(left, right, (((1,), (1,)), ((), ())), preferred_element_type=f32)


def activation_grads(grad_hidden, gate_pre, up_pre):
    sigmoid = jax.nn.sigmoid(gate_pre)
    silu = gate_pre * sigmoid
    dsilu = sigmoid * (1.0 + gate_pre * (1.0 - sigmoid))
    grad_gate_pre = (grad_hidden * up_pre * dsilu).astype(bf16)
    grad_up_pre = (grad_hidden * silu).astype(bf16)
    return (grad_gate_pre, grad_up_pre)


def body_any(out_grad, routes, gate_codes, w_gate, w_up, w_down, saved_inputs, saved_gate, saved_up):
    owners = lax.axis_size("expert")
    slot_count = saved_gate.shape[1]
    capacity = slot_count // owners
    token_count = routes.shape[0]
    choice_count = routes.shape[1]
    flat_routes = routes.reshape(-1)
    onehot = (flat_routes[:, None] == jnp.arange(owners, dtype=jnp.int32)[None, :]).astype(jnp.int32)
    earlier = jnp.cumsum(onehot, axis=0) - onehot
    position = jnp.sum(earlier * onehot, axis=1)
    slot_index = (flat_routes * capacity + position).reshape(token_count, choice_count)
    gate_values = gate_codes.astype(f32) * gate_unit
    rows_iota = jnp.arange(slot_count, dtype=jnp.int32)[:, None]
    weighted = jnp.zeros((slot_count, token_count), f32)
    picks = jnp.zeros((slot_count, token_count), f32)
    for pick in range(choice_count):
        hit = rows_iota == slot_index[:, pick][None, :]
        weighted = weighted + jnp.where(hit, gate_values[:, pick][None, :], 0.0)
        picks = picks + hit.astype(f32)
    outgoing = jnp.dot(weighted.astype(bf16), out_grad, preferred_element_type=f32).astype(bf16)
    received = lax.all_to_all(outgoing, "expert", split_axis=0, concat_axis=0, tiled=True)
    hidden_share = lax.psum_scatter(
        contract_cols(received, w_down[0]), "dp", scatter_dimension=0, tiled=True
    )
    gate_pre = saved_gate[0].astype(f32)
    up_pre = saved_up[0].astype(f32)
    hidden = (gate_pre * jax.nn.sigmoid(gate_pre) * up_pre).astype(bf16)
    grad_hidden = lax.all_gather(hidden_share, "dp", axis=0, tiled=True)
    grad_gate_pre, grad_up_pre = activation_grads(grad_hidden, gate_pre, up_pre)
    slot_grads = contract_cols(grad_gate_pre, w_gate[0]) + contract_cols(grad_up_pre, w_up[0])
    returned = lax.all_to_all(
        slot_grads.astype(bf16), "expert", split_axis=0, concat_axis=0, tiled=True
    )
    token_grads = contract_rows(picks.astype(bf16), returned).astype(bf16)
    inputs_here = saved_inputs[0]
    part = jnp.concatenate(
        [
            contract_rows(inputs_here, grad_gate_pre),
            contract_rows(inputs_here, grad_up_pre),
            contract_rows(received, hidden),
        ],
        axis=1,
    )
    return (token_grads, (part * loss_scale).astype(bf16)[None])


on_chip = pl.BlockSpec(memory_space=pltpu.VMEM)
on_scalar = pl.BlockSpec(memory_space=pltpu.SMEM)
anywhere = pl.BlockSpec(memory_space=pl.ANY)
light = pl.CostEstimate(flops=1 << 20, bytes_accessed=1 << 14, transcendentals=0)


def source(here, step, other):
    group = lax.rem(here // 4 + (4 - step), 4)
    return jnp.bitwise_xor(group * 4 + lax.rem(here, 4), 2 * other)


def params(mib):
    return pltpu.CompilerParams(vmem_limit_bytes=mib << 20)


def dispatch_kernel(n, cap, here, *refs):
    toks, (wd0, wd1) = refs[:n], refs[n : n + 2]
    rec0, rec1, share, *share_out, pos_out = refs[n + 2 :]
    tok = toks[0].shape[0] - 8
    line = 256 * pl.cdiv(tok, 256)
    before = lax.broadcasted_iota(jnp.int32, (tok, tok), 0) < lax.broadcasted_iota(jnp.int32, (tok, tok), 1)
    before = jnp.where(before, 1.0, 0.0).astype(bf16)
    slot = lax.broadcasted_iota(jnp.int32, (cap, tok), 0).astype(f32)
    masks, gates = [], []
    for a in range(2):
        expert = jnp.bitwise_xor(here[0], a).astype(f32)
        for t in toks:
            hit = t[tok:, :tok].astype(f32) == expert
            masks.append(jnp.max(jnp.where(hit, 1.0, 0.0), axis=0, keepdims=True))
            gates.append(jnp.sum(jnp.where(hit, t[tok:, line : line + tok].astype(f32), 0.0), axis=0, keepdims=True))
    fill = [jnp.zeros((8 - 2 * n, tok), f32)] if n < 4 else []
    mask = jnp.concatenate(masks + fill, axis=0)
    pos = jnp.dot(mask.astype(bf16), before, preferred_element_type=f32)
    pos = jnp.where(mask > 0.0, pos, -1.0)
    pos_out[...] = pos
    for rel, t in enumerate(toks):
        w = [
            jnp.where(slot == pos[i : i + 1, :], gates[i] * gate_unit, 0.0).astype(bf16)
            for i in (rel, n + rel)
        ]
        rows = jnp.dot(jnp.concatenate(w, axis=0), t[:tok, :], preferred_element_type=f32).astype(bf16)
        rec0[rel * cap : (rel + 1) * cap, :] = rows[:cap]
        rec1[rel * cap : (rel + 1) * cap, :] = rows[cap:]
    for a, (rec, wd) in enumerate(((rec0, wd0), (rec1, wd1))):
        gh = contract_cols(rec[...], wd[...])
        share[a * n * cap : (a + 1) * n * cap, :] = gh
        if n == 1:
            share_out[0][a * cap : (a + 1) * cap, :] = gh.astype(bf16)
        else:
            share_out[a][...] = gh.astype(bf16)


def dispatch(here, toks, wd0, wd1, cap):
    n = len(toks)
    tok, d = toks[0].shape
    h = wd0.shape[0]
    outs = [((n * cap, d), bf16), ((n * cap, d), bf16), ((2 * n * cap, h), f32)]
    outs += [((2 * cap, h), bf16)] if n == 1 else [((n * cap, h), bf16)] * 2
    outs += [((8, tok - 8), f32)]
    return pl.pallas_call(
        functools.partial(dispatch_kernel, n, cap),
        out_shape=[jax.ShapeDtypeStruct(s, t) for s, t in outs],
        in_specs=[on_scalar] + [on_chip] * (n + 2),
        out_specs=[on_chip] * len(outs),
        cost_estimate=light,
        compiler_params=params(16),
        name="dispatch",
    )(here, *toks, wd0, wd1)


def combine_kernel(chunk, cap, here, share, *refs):
    n = len(chunk)
    if n == 1:
        peer0, peer1 = refs[0].at[:cap, :], refs[0].at[cap:, :]
        pos, *refs = refs[1:]
    else:
        peer0, peer1, pos, *refs = refs
    saved, (w0, w1), (gp0, gp1) = refs[:4], refs[4:6], refs[6:8]
    backs, (held, sems) = refs[8:-2], refs[-2:]
    h = share.shape[1]
    copies = []
    for a in range(2):
        for other, step in chunk:
            rows = pl.ds(pl.multiple_of(source(here[0], step, other) * cap, 16), cap)
            for v in saved[2 * a : 2 * a + 2]:
                i = len(copies)
                copies.append(pltpu.make_async_copy(v.at[rows, :], held.at[i], sems.at[i]))
    for c in copies:
        c.start()
    slot = lax.broadcasted_iota(jnp.int32, (cap, pos.shape[1]), 0).astype(f32)
    sums = [None] * n
    for a, (gp, w, peer) in enumerate(((gp0, w0, peer0), (gp1, w1, peer1))):
        for rel in range(n):
            i = a * n + rel
            copies[2 * i].wait()
            copies[2 * i + 1].wait()
            gh = share[i * cap : (i + 1) * cap, :] + peer[rel * cap : (rel + 1) * cap, :].astype(f32)
            gg, gu = activation_grads(gh, held[2 * i].astype(f32), held[2 * i + 1].astype(f32))
            gp[rel * cap : (rel + 1) * cap, :h] = gg
            gp[rel * cap : (rel + 1) * cap, h:] = gu
        slots = contract_cols(gp[...], w[...]).astype(bf16)
        for rel in range(n):
            i = a * n + rel
            pick = jnp.where(slot == pos[i : i + 1, :], 1.0, 0.0).astype(bf16)
            part = contract_rows(pick, slots[rel * cap : (rel + 1) * cap])
            sums[rel] = part if sums[rel] is None else sums[rel] + part
    if len(backs) > n:
        half = backs[0].shape[1]
        for k, back in enumerate(backs):
            back[...] = sums[0][:, k * half : (k + 1) * half].astype(bf16)
    else:
        for rel in range(n):
            backs[rel][...] = sums[rel].astype(bf16)


def combine(here, chunk, share, peers, pos, saved0, saved1, w0, w1, cap, halves=False):
    n = len(chunk)
    h = share.shape[1]
    d = w0.shape[0]
    tok = pos.shape[1]
    outs = [(n * cap, 2 * h)] * 2 + ([(tok, d // 2)] * 2 if halves else [(tok, d)] * n)
    return pl.pallas_call(
        functools.partial(combine_kernel, chunk, cap),
        out_shape=[jax.ShapeDtypeStruct(s, bf16) for s in outs],
        in_specs=[on_scalar] + [on_chip] * (2 + len(peers)) + [anywhere] * 4 + [on_chip] * 2,
        out_specs=[on_chip] * len(outs),
        scratch_shapes=[pltpu.VMEM((4 * n, cap, h), bf16), pltpu.SemaphoreType.DMA((4 * n,))],
        cost_estimate=light,
        compiler_params=params(20),
        name="combine",
    )(here, share, *peers, pos, *saved0, *saved1, w0, w1)


def join_kernel(left, right, out):
    out[:, : left.shape[1]] = left[...]
    out[:, left.shape[1] :] = right[...]


def join(left, right):
    rows, h = left.shape
    return pl.pallas_call(
        join_kernel,
        out_shape=jax.ShapeDtypeStruct((rows, 2 * h), left.dtype),
        in_specs=[on_chip] * 2,
        out_specs=on_chip,
        cost_estimate=light,
        compiler_params=params(8),
        name="join",
    )(left, right)


def add_kernel(part, *refs):
    wide = refs[-1].shape[1]
    total = None
    for r in refs[:-1]:
        v = r[...] if part is None or r.shape[1] == wide else r[:, part * wide : (part + 1) * wide]
        total = v.astype(f32) if total is None else total + v.astype(f32)
    refs[-1][...] = total.astype(bf16)


def add(values, part=None):
    rows, wide = values[0].shape
    return pl.pallas_call(
        functools.partial(add_kernel, part),
        out_shape=jax.ShapeDtypeStruct((rows, wide if part is None else wide // 2), bf16),
        in_specs=[on_chip] * len(values),
        out_specs=on_chip,
        cost_estimate=light,
        compiler_params=params(8),
        name="add",
    )(*values)


def finish_kernel(a, b, left, right, out):
    half = left.shape[1]
    for at, v in ((0, left), (half, right)):
        total = a[:, at : at + half].astype(f32) + b[:, at : at + half].astype(f32) + v[...].astype(f32)
        out[:, at : at + half] = total.astype(bf16)


def finish(a, b, left, right):
    return pl.pallas_call(
        finish_kernel,
        out_shape=jax.ShapeDtypeStruct(a.shape, bf16),
        in_specs=[on_chip] * 4,
        out_specs=on_chip,
        cost_estimate=light,
        compiler_params=params(8),
        name="finish",
    )(a, b, left, right)


def in_hbm(v):
    return pltpu.with_memory_space_constraint(v, pltpu.HBM)


def hidden_kernel(cap, here, gate, up, out, held, sems):
    copies = []
    for k, v in enumerate((gate, up)):
        for q in range(held.shape[1] // cap):
            rows = pl.ds(pl.multiple_of((2 * q + lax.rem(here[0], 2)) * cap, 16), cap)
            to = held.at[k, pl.ds(q * cap, cap), :]
            copies.append(pltpu.make_async_copy(v.at[rows, :], to, sems.at[len(copies)]))
    for c in copies:
        c.start()
    for c in copies:
        c.wait()
    gate_pre = held[0].astype(f32)
    out[...] = (gate_pre * jax.nn.sigmoid(gate_pre) * held[1].astype(f32)).astype(bf16).T


def hidden(here, gate, up, cap):
    rows, h = gate.shape
    rows = rows // 2
    return pl.pallas_call(
        functools.partial(hidden_kernel, cap),
        out_shape=jax.ShapeDtypeStruct((h, rows), bf16),
        in_specs=[on_scalar, anywhere, anywhere],
        out_specs=on_chip,
        scratch_shapes=[pltpu.VMEM((2, rows, h), bf16), pltpu.SemaphoreType.DMA((2 * rows // cap,))],
        cost_estimate=light,
        compiler_params=params(16),
        name="hidden",
    )(here, gate, up)


def turn_kernel(cap, here, v, own, other, held):
    for k, out in enumerate((own, other)):
        plane = lax.rem(here[0] + k, 2)
        for q in range(held.shape[0] // cap):
            held[q * cap : (q + 1) * cap, :] = v[pl.ds(pl.multiple_of((2 * q + plane) * cap, 16), cap), :]
        out[...] = held[...].T


def turn(here, v, cap):
    slots, d = v.shape
    rows = slots // 2
    tile = 256
    out = pl.BlockSpec((tile, rows), lambda i, here: (i, 0))
    return pl.pallas_call(
        functools.partial(turn_kernel, cap),
        out_shape=[jax.ShapeDtypeStruct((d, rows), v.dtype)] * 2,
        grid_spec=pltpu.PrefetchScalarGridSpec(
            num_scalar_prefetch=1,
            grid=(d // tile,),
            in_specs=[pl.BlockSpec((slots, tile), lambda i, here: (0, i))],
            out_specs=[out, out],
            scratch_shapes=[pltpu.VMEM((rows, tile), v.dtype)],
        ),
        cost_estimate=light,
        compiler_params=params(12),
        name="turn",
    )(here, in_hbm(v))


def pack_kernel(line, tokens, routes, codes, out, named, sems):
    tok = tokens.shape[0]
    copies = [
        pltpu.make_async_copy(tokens, out.at[:tok, :], sems.at[0]),
        pltpu.make_async_copy(routes, named.at[0], sems.at[1]),
        pltpu.make_async_copy(codes, named.at[1], sems.at[2]),
    ]
    for c in copies:
        c.start()
    out[tok:, :] = jnp.zeros((8, out.shape[1]), bf16)
    for k, at in enumerate((0, line)):
        copies[1 + k].wait()
        out[tok:, at : at + tok] = named[k].astype(f32).astype(bf16)
    copies[0].wait()


def pack(tokens, routes, codes, line):
    tok, d = tokens.shape
    return pl.pallas_call(
        functools.partial(pack_kernel, line),
        out_shape=jax.ShapeDtypeStruct((tok + 8, d), bf16),
        in_specs=[anywhere] * 3,
        out_specs=on_chip,
        scratch_shapes=[pltpu.VMEM((2, *routes.shape), jnp.int32), pltpu.SemaphoreType.DMA((3,))],
        cost_estimate=light,
        compiler_params=params(8),
        name="pack",
    )(in_hbm(tokens), in_hbm(routes), in_hbm(codes))


def weights_kernel(order, cap, count, here, inputs, hid, *refs):
    recs, gps, refs = refs[:count], refs[count : 2 * count], refs[2 * count :]
    summed, (out, rs, gs, rec_sems, gp_sems) = refs[:-5], refs[-5:]
    i = pl.program_id(0)
    tile = rs.shape[2]

    def copies(pieces, column, to, sems):
        made = []
        for r in pieces:
            for at in range(0, r.shape[0], cap):
                src = source(here[0], *order[len(made)])
                rows = pl.ds(pl.multiple_of((src // 2) * cap, 16), cap)
                made.append(pltpu.make_async_copy(r.at[pl.ds(at, cap), column], to.at[rows, :], sems.at[len(made)]))
        return made

    def received(step):
        slot = lax.rem(step, 2)
        return copies(recs, pl.ds(pl.multiple_of(step * tile, 128), tile), rs.at[slot], rec_sems.at[slot])

    fixed = copies(gps, pl.ds(0, gs.shape[1]), gs, gp_sems)

    @pl.when(i == 0)
    def _():
        for c in fixed + received(i):
            c.start()

    @pl.when(i + 1 < pl.num_programs(0))
    def _():
        for c in received(i + 1):
            c.start()

    @pl.when(i == 0)
    def _():
        for c in fixed:
            c.wait()

    wide = gs.shape[1]
    left = jnp.dot(inputs[...], gs[...], preferred_element_type=f32)
    for c in received(i):
        c.wait()
    right = jnp.dot(hid[...], rs[lax.rem(i, 2)], preferred_element_type=f32)
    if summed:
        other = summed[0]
        out[0, :, :wide] = ((left + other[:, :wide].astype(f32)) * loss_scale).astype(bf16)
        out[0, :, wide:] = ((right.T + other[:, wide:].astype(f32)) * loss_scale).astype(bf16)
    else:
        out[:, :wide] = left.astype(bf16)
        out[:, wide:] = right.astype(bf16).T


def weight_sums(here, order, inputs, hid, recs, gps, cap, summed=None):
    d, slots = inputs.shape
    h = hid.shape[0]
    tile = 512
    block = pl.BlockSpec((tile, 3 * h), lambda i, here: (i, 0))
    given = [] if summed is None else [summed]
    last = summed is not None
    return pl.pallas_call(
        functools.partial(weights_kernel, order, cap, len(recs)),
        out_shape=jax.ShapeDtypeStruct((1, d, 3 * h) if last else (d, 3 * h), bf16),
        grid_spec=pltpu.PrefetchScalarGridSpec(
            num_scalar_prefetch=1,
            grid=(d // tile,),
            in_specs=[
                pl.BlockSpec((tile, slots), lambda i, here: (i, 0)),
                pl.BlockSpec((h, slots), lambda i, here: (0, 0)),
            ]
            + [anywhere] * (2 * len(recs))
            + [block] * len(given),
            out_specs=pl.BlockSpec((1, tile, 3 * h), lambda i, here: (0, i, 0)) if last else block,
            scratch_shapes=[
                pltpu.VMEM((2, slots, tile), bf16),
                pltpu.VMEM((slots, 2 * h), bf16),
                pltpu.SemaphoreType.DMA((2, len(order))),
                pltpu.SemaphoreType.DMA((len(order),)),
            ],
        ),
        cost_estimate=light,
        compiler_params=params(28),
        name="weights",
    )(here, inputs, hid, *recs, *gps, *given)


def together(*values):
    return lax.optimization_barrier(values)


def body_grid(out_grad, routes, gate_codes, w_gate, w_up, w_down, saved_inputs, saved_gate, saved_up):
    owners = lax.axis_size("expert")
    me = lax.axis_index("expert")
    to_core = [(i, i ^ 1) for i in range(owners)]
    to_x = [(i, i ^ 2) for i in range(owners)]
    tok, d = out_grad.shape
    choices = routes.shape[1]
    slots = saved_gate.shape[1]
    cap = slots // owners

    def send(v, perm):
        return lax.ppermute(v, "expert", perm)

    line = 256 * pl.cdiv(tok, 256)
    block = pack(out_grad, routes.T, gate_codes.T, line)
    here = me.reshape(1).astype(jnp.int32)

    def ring(v, hops=1):
        return send(v, [(i, (i + 4 * hops) % owners) for i in range(owners)])

    wd, sg, su = w_down[0], saved_gate[0], saved_up[0]
    wd_c, sg_c, su_c = [send(v, to_core) for v in (wd, sg, su)]

    order, recs, recs_c, gps, gps_c = [], [], [], [], []

    def first(chunk, toks):
        rec, rec_c, share, *shares, pos = dispatch(here, toks, wd, wd_c, cap)
        order.extend((k, col) for col, k in chunk)
        recs.append(rec)
        recs_c.append(rec_c)
        return (chunk, share, pos), *shares

    def exchange(v):
        return lax.ppermute(v, "dp", [(0, 1), (1, 0)])

    def second(state, *peers, halves=False):
        chunk, share, pos = state
        gp, gp_c, *sums = combine(here, chunk, share, peers, pos, (sg, su), (sg_c, su_c), w, w_c, cap, halves)
        gps.append(gp)
        gps_c.append(gp_c)
        return sums

    r1, x0 = ring(block), send(block, to_x)
    c0, h0 = first([(0, 0)], [block])
    w = join(w_gate[0], w_up[0])
    inputs, inputs_away = turn(here, saved_inputs[0], cap)
    r1, x0, h0, w, inputs, inputs_away, sg_c, su_c = together(r1, x0, h0, w, inputs, inputs_away, sg_c, su_c)
    r2, x1 = ring(r1), send(r1, to_x)
    h0, w_c = exchange(h0), send(w, to_core)
    c1, h1, g1 = first([(1, 0), (0, 1)], [x0, r1])
    h1 = exchange(h1)
    (t_r0,) = second(c0, h0)
    r2, x1, h1, g1, t_r0 = together(r2, x1, h1, g1, t_r0)
    r3, x2 = ring(r2), send(r2, to_x)
    g1, inputs_c = exchange(g1), send(inputs_away, to_core)
    c2, h2, g2 = first([(1, 1), (0, 2)], [x1, r2])
    h2 = exchange(h2)
    t_x0, t_r1 = second(c1, h1, g1)
    hid = hidden(here, sg, su, cap)
    r3, x2, h2, g2, t_x0, t_r1, inputs_c, hid = together(r3, x2, h2, g2, t_x0, t_r1, inputs_c, hid)
    x3, w1 = send(r3, to_x), ring(t_r1)
    g2 = exchange(g2)
    c3, h3, g3 = first([(1, 2), (0, 3)], [x2, r3])
    h3 = exchange(h3)
    t_x1, t_r2 = second(c2, h2, g2)
    hid_c = hidden(here, sg_c, su_c, cap)
    x3, w1, h3, g3, t_x0, t_x1, t_r2, hid_c = together(x3, w1, h3, g3, t_x0, t_x1, t_r2, hid_c)
    u1, b0 = ring(t_x1), send(t_x0, to_x)
    g3 = exchange(g3)
    c4, h4 = first([(1, 3)], [x3])
    h4 = exchange(h4)
    t_x2, t_r3 = second(c3, h3, g3)
    u1, b0, h4, t_x2, t_r3 = together(u1, b0, h4, t_x2, t_r3)
    a0, a1, h4 = together(add([t_x2, u1], 0), add([t_x2, u1], 1), h4)
    b2 = [send(a0, to_x), send(a1, to_x)]
    t_x3 = second(c4, h4, halves=True)
    b3 = [send(t, to_x) for t in t_x3]
    away = weight_sums(here, order, inputs_c, hid_c, recs_c, gps_c, cap)
    b2[0], away = together(b2[0], away)
    summed = send(away, to_core)
    w2 = [ring(add([t_r2, w1, b2[k]], k)) for k in range(2)]
    w3 = [ring(add([t_r3, b3[k], w2[k]], k)) for k in range(2)]
    weight_grads = weight_sums(here, order, inputs, hid, recs, gps, cap, summed)
    w3[1], weight_grads = together(w3[1], weight_grads)
    return (finish(t_r0, b0, *w3), weight_grads)


def solution(mesh):
    placed = (
        P("expert", "dp"),
        P("expert", None),
        P("expert", None),
        P("expert", "dp", None),
        P("expert", "dp", None),
        P("expert", None, "dp"),
        P("expert", None, "dp"),
        P("expert", None, None),
        P("expert", None, None),
    )
    small = mesh.shape["expert"] == 16 and mesh.shape["dp"] == 2
    return jax.shard_map(
        body_grid if small else body_any,
        mesh=mesh,
        in_specs=placed,
        out_specs=(P("expert", "dp"), P("expert", "dp", None)),
        check_vma=False,
    )
```

```python
import functools

import jax
import jax.numpy as jnp
from jax import lax
from jax.experimental import pallas as pl
from jax.experimental.pallas import tpu as pltpu
from jax.sharding import PartitionSpec as P

gate_unit = 0.00390625
loss_scale = 0.015625
f32 = jnp.float32
bf16 = jnp.bfloat16


def contract_rows(left, right):
    return lax.dot_general(left, right, (((0,), (0,)), ((), ())), preferred_element_type=f32)


def contract_cols(left, right):
    return lax.dot_general(left, right, (((1,), (1,)), ((), ())), preferred_element_type=f32)


def activation_grads(grad_hidden, gate_pre, up_pre):
    sigmoid = jax.nn.sigmoid(gate_pre)
    silu = gate_pre * sigmoid
    dsilu = sigmoid * (1.0 + gate_pre * (1.0 - sigmoid))
    grad_gate_pre = (grad_hidden * up_pre * dsilu).astype(bf16)
    grad_up_pre = (grad_hidden * silu).astype(bf16)
    return (grad_gate_pre, grad_up_pre)


def body_any(out_grad, routes, gate_codes, w_gate, w_up, w_down, saved_inputs, saved_gate, saved_up):
    owners = lax.axis_size("expert")
    slot_count = saved_gate.shape[1]
    capacity = slot_count // owners
    token_count = routes.shape[0]
    choice_count = routes.shape[1]
    flat_routes = routes.reshape(-1)
    onehot = (flat_routes[:, None] == jnp.arange(owners, dtype=jnp.int32)[None, :]).astype(jnp.int32)
    earlier = jnp.cumsum(onehot, axis=0) - onehot
    position = jnp.sum(earlier * onehot, axis=1)
    slot_index = (flat_routes * capacity + position).reshape(token_count, choice_count)
    gate_values = gate_codes.astype(f32) * gate_unit
    rows_iota = jnp.arange(slot_count, dtype=jnp.int32)[:, None]
    weighted = jnp.zeros((slot_count, token_count), f32)
    picks = jnp.zeros((slot_count, token_count), f32)
    for pick in range(choice_count):
        hit = rows_iota == slot_index[:, pick][None, :]
        weighted = weighted + jnp.where(hit, gate_values[:, pick][None, :], 0.0)
        picks = picks + hit.astype(f32)
    outgoing = jnp.dot(weighted.astype(bf16), out_grad, preferred_element_type=f32).astype(bf16)
    received = lax.all_to_all(outgoing, "expert", split_axis=0, concat_axis=0, tiled=True)
    hidden_share = lax.psum_scatter(
        contract_cols(received, w_down[0]), "dp", scatter_dimension=0, tiled=True
    )
    gate_pre = saved_gate[0].astype(f32)
    up_pre = saved_up[0].astype(f32)
    hidden = (gate_pre * jax.nn.sigmoid(gate_pre) * up_pre).astype(bf16)
    grad_hidden = lax.all_gather(hidden_share, "dp", axis=0, tiled=True)
    grad_gate_pre, grad_up_pre = activation_grads(grad_hidden, gate_pre, up_pre)
    slot_grads = contract_cols(grad_gate_pre, w_gate[0]) + contract_cols(grad_up_pre, w_up[0])
    returned = lax.all_to_all(
        slot_grads.astype(bf16), "expert", split_axis=0, concat_axis=0, tiled=True
    )
    token_grads = contract_rows(picks.astype(bf16), returned).astype(bf16)
    inputs_here = saved_inputs[0]
    part = jnp.concatenate(
        [
            contract_rows(inputs_here, grad_gate_pre),
            contract_rows(inputs_here, grad_up_pre),
            contract_rows(received, hidden),
        ],
        axis=1,
    )
    return (token_grads, (part * loss_scale).astype(bf16)[None])


on_chip = pl.BlockSpec(memory_space=pltpu.VMEM)
on_scalar = pl.BlockSpec(memory_space=pltpu.SMEM)
anywhere = pl.BlockSpec(memory_space=pl.ANY)
light = pl.CostEstimate(flops=1 << 20, bytes_accessed=1 << 14, transcendentals=0)


def source(here, step, other):
    group = lax.rem(here // 4 + (4 - step), 4)
    return jnp.bitwise_xor(group * 4 + lax.rem(here, 4), 2 * other)


def params(mib):
    return pltpu.CompilerParams(vmem_limit_bytes=mib << 20)


def plane_rows(here, other, step, cap):
    return pl.ds(pl.multiple_of((source(here, step, other) // 2) * cap, 16), cap)


def dispatch_kernel(chunk, cap, begun, here, *refs):
    n = len(chunk)
    toks, (wd0, wd1) = refs[:n], refs[n : n + 2]
    buf0, buf1, share, *share_out, pos_out, rec, sems = refs[n + 2 + 2 * begun :]
    tok = toks[0].shape[0] - 8
    line = 256 * pl.cdiv(tok, 256)
    before = lax.broadcasted_iota(jnp.int32, (tok, tok), 0) < lax.broadcasted_iota(jnp.int32, (tok, tok), 1)
    before = jnp.where(before, 1.0, 0.0).astype(bf16)
    slot = lax.broadcasted_iota(jnp.int32, (cap, tok), 0).astype(f32)
    masks, gates = [], []
    for a in range(2):
        expert = jnp.bitwise_xor(here[0], a).astype(f32)
        for t in toks:
            hit = t[tok:, :tok].astype(f32) == expert
            masks.append(jnp.max(jnp.where(hit, 1.0, 0.0), axis=0, keepdims=True))
            gates.append(jnp.sum(jnp.where(hit, t[tok:, line : line + tok].astype(f32), 0.0), axis=0, keepdims=True))
    fill = [jnp.zeros((8 - 2 * n, tok), f32)] if n < 4 else []
    mask = jnp.concatenate(masks + fill, axis=0)
    pos = jnp.dot(mask.astype(bf16), before, preferred_element_type=f32)
    pos = jnp.where(mask > 0.0, pos, -1.0)
    pos_out[...] = pos
    copies = []
    for rel, t in enumerate(toks):
        w = [
            jnp.where(slot == pos[i : i + 1, :], gates[i] * gate_unit, 0.0).astype(bf16)
            for i in (rel, n + rel)
        ]
        rows = jnp.dot(jnp.concatenate(w, axis=0), t[:tok, :], preferred_element_type=f32).astype(bf16)
        at = pl.ds(rel * cap, cap)
        for a, buf in enumerate((buf0, buf1)):
            rec[a, at, :] = rows[a * cap : (a + 1) * cap]
            to = plane_rows(here[0], *chunk[rel], cap)
            copies.append(pltpu.make_async_copy(rec.at[a, at, :], buf.at[to, :], sems.at[len(copies)]))
            copies[-1].start()
    for a, wd in enumerate((wd0, wd1)):
        gh = contract_cols(rec[a], wd[...])
        share[a * n * cap : (a + 1) * n * cap, :] = gh
        if n == 1:
            share_out[0][a * cap : (a + 1) * cap, :] = gh.astype(bf16)
        else:
            share_out[a][...] = gh.astype(bf16)
    for c in copies:
        c.wait()


def dispatch(here, chunk, toks, wd0, wd1, cap, rows, old):
    n = len(toks)
    tok, d = toks[0].shape
    h = wd0.shape[0]
    outs = [((rows, d), bf16)] * 2 + [((2 * n * cap, h), f32)]
    outs += [((2 * cap, h), bf16)] if n == 1 else [((n * cap, h), bf16)] * 2
    outs += [((8, tok - 8), f32)]
    return pl.pallas_call(
        functools.partial(dispatch_kernel, chunk, cap, len(old) // 2),
        out_shape=[jax.ShapeDtypeStruct(s, t) for s, t in outs],
        in_specs=[on_scalar] + [on_chip] * (n + 2) + [anywhere] * len(old),
        out_specs=[anywhere] * 2 + [on_chip] * (len(outs) - 2),
        scratch_shapes=[pltpu.VMEM((2, n * cap, d), bf16), pltpu.SemaphoreType.DMA((2 * n,))],
        input_output_aliases={n + 3 + k: k for k in range(len(old))},
        cost_estimate=light,
        compiler_params=params(16),
        name="dispatch",
    )(here, *toks, wd0, wd1, *old)


def combine_kernel(chunk, cap, begun, last, here, share, *refs):
    n = len(chunk)
    if n == 1:
        peer0, peer1 = refs[0].at[:cap, :], refs[0].at[cap:, :]
        pos, *refs = refs[1:]
    else:
        peer0, peer1, pos, *refs = refs
    saved, ws, refs = refs[:4], refs[4:6], refs[6 + begun * (1 if last else 2) :]
    buffers, backs, (held, gps, sems, out_sems) = refs[:2], refs[2:-4], refs[-4:]
    h = share.shape[1]
    copies = []
    for a in range(2):
        for other, step in chunk:
            rows = pl.ds(pl.multiple_of(source(here[0], step, other) * cap, 16), cap)
            for v in saved[2 * a : 2 * a + 2]:
                i = len(copies)
                copies.append(pltpu.make_async_copy(v.at[rows, :], held.at[i], sems.at[i]))
    for c in copies:
        c.start()
    slot = lax.broadcasted_iota(jnp.int32, (cap, pos.shape[1]), 0).astype(f32)
    sums, leaving = [None] * n, []
    for a, (w, peer) in enumerate(zip(ws, (peer0, peer1))):
        gp = gps.at[a]
        for rel in range(n):
            i = a * n + rel
            copies[2 * i].wait()
            copies[2 * i + 1].wait()
            gh = share[i * cap : (i + 1) * cap, :] + peer[rel * cap : (rel + 1) * cap, :].astype(f32)
            gg, gu = activation_grads(gh, held[2 * i].astype(f32), held[2 * i + 1].astype(f32))
            gp[rel * cap : (rel + 1) * cap, :h] = gg
            gp[rel * cap : (rel + 1) * cap, h:] = gu
            if a == 0 or not last:
                to = buffers[a].at[plane_rows(here[0], *chunk[rel], cap), :]
                leaving.append(pltpu.make_async_copy(gp.at[rel * cap : (rel + 1) * cap, :], to, out_sems.at[i]))
                leaving[-1].start()
        if a == 1 and last:
            buffers[1][...] = gp[...]
        slots = contract_cols(gp[...], w[...]).astype(bf16)
        for rel in range(n):
            i = a * n + rel
            pick = jnp.where(slot == pos[i : i + 1, :], 1.0, 0.0).astype(bf16)
            part = contract_rows(pick, slots[rel * cap : (rel + 1) * cap])
            sums[rel] = part if sums[rel] is None else sums[rel] + part
    if len(backs) > n:
        half = backs[0].shape[1]
        for k, back in enumerate(backs):
            back[...] = sums[0][:, k * half : (k + 1) * half].astype(bf16)
    else:
        for rel in range(n):
            backs[rel][...] = sums[rel].astype(bf16)
    for c in leaving:
        c.wait()


def combine(here, chunk, share, peers, pos, saved0, saved1, w0, w1, cap, rows, old, last=False):
    n = len(chunk)
    h = share.shape[1]
    d = w0.shape[0]
    tok = pos.shape[1]
    old = old[:1] if last else old
    outs = [(rows, 2 * h), (n * cap if last else rows, 2 * h)] + ([(tok, d // 2)] * 2 if last else [(tok, d)] * n)
    first_old = 2 + len(peers) + 1 + 4 + 2
    return pl.pallas_call(
        functools.partial(combine_kernel, chunk, cap, 1 if old else 0, last),
        out_shape=[jax.ShapeDtypeStruct(s, bf16) for s in outs],
        in_specs=[on_scalar] + [on_chip] * (2 + len(peers)) + [anywhere] * 4 + [on_chip] * 2 + [anywhere] * len(old),
        out_specs=[anywhere, on_chip if last else anywhere] + [on_chip] * (len(outs) - 2),
        scratch_shapes=[
            pltpu.VMEM((4 * n, cap, h), bf16),
            pltpu.VMEM((2, n * cap, 2 * h), bf16),
            pltpu.SemaphoreType.DMA((4 * n,)),
            pltpu.SemaphoreType.DMA((2 * n,)),
        ],
        input_output_aliases={first_old + k: k for k in range(len(old))},
        cost_estimate=light,
        compiler_params=params(20),
        name="combine",
    )(here, share, *peers, pos, *saved0, *saved1, w0, w1, *old)


def join_kernel(left, right, out):
    out[:, : left.shape[1]] = left[...]
    out[:, left.shape[1] :] = right[...]


def join(left, right):
    rows, h = left.shape
    return pl.pallas_call(
        join_kernel,
        out_shape=jax.ShapeDtypeStruct((rows, 2 * h), left.dtype),
        in_specs=[on_chip] * 2,
        out_specs=on_chip,
        cost_estimate=light,
        compiler_params=params(8),
        name="join",
    )(left, right)


def add_kernel(part, *refs):
    wide = refs[-1].shape[1]
    total = None
    for r in refs[:-1]:
        v = r[...] if part is None or r.shape[1] == wide else r[:, part * wide : (part + 1) * wide]
        total = v.astype(f32) if total is None else total + v.astype(f32)
    refs[-1][...] = total.astype(bf16)


def add(values, part=None):
    rows, wide = values[0].shape
    return pl.pallas_call(
        functools.partial(add_kernel, part),
        out_shape=jax.ShapeDtypeStruct((rows, wide if part is None else wide // 2), bf16),
        in_specs=[on_chip] * len(values),
        out_specs=on_chip,
        cost_estimate=light,
        compiler_params=params(8),
        name="add",
    )(*values)


def finish_kernel(a, b, left, right, out):
    half = left.shape[1]
    for at, v in ((0, left), (half, right)):
        total = a[:, at : at + half].astype(f32) + b[:, at : at + half].astype(f32) + v[...].astype(f32)
        out[:, at : at + half] = total.astype(bf16)


def finish(a, b, left, right):
    return pl.pallas_call(
        finish_kernel,
        out_shape=jax.ShapeDtypeStruct(a.shape, bf16),
        in_specs=[on_chip] * 4,
        out_specs=on_chip,
        cost_estimate=light,
        compiler_params=params(8),
        name="finish",
    )(a, b, left, right)


def in_hbm(v):
    return pltpu.with_memory_space_constraint(v, pltpu.HBM)


def hidden_kernel(cap, here, gate, up, out, held, sems):
    rows = held.shape[2]
    copies = []
    for k in range(2):
        plane = lax.rem(here[0] + k, 2)
        for i, v in enumerate((gate, up)):
            for q in range(rows // cap):
                at = pl.ds(pl.multiple_of((2 * q + plane) * cap, 16), cap)
                to = held.at[k, i, pl.ds(q * cap, cap), :]
                copies.append(pltpu.make_async_copy(v.at[at, :], to, sems.at[len(copies)]))
    for c in copies:
        c.start()
    for k in range(2):
        for c in copies[k * len(copies) // 2 : (k + 1) * len(copies) // 2]:
            c.wait()
        gate_pre = held[k, 0].astype(f32)
        out[:, k * rows : (k + 1) * rows] = (
            (gate_pre * jax.nn.sigmoid(gate_pre) * held[k, 1].astype(f32)).astype(bf16).T
        )


def hidden(here, gate, up, cap):
    slots, h = gate.shape
    return pl.pallas_call(
        functools.partial(hidden_kernel, cap),
        out_shape=jax.ShapeDtypeStruct((h, slots), bf16),
        in_specs=[on_scalar, anywhere, anywhere],
        out_specs=on_chip,
        scratch_shapes=[pltpu.VMEM((2, 2, slots // 2, h), bf16), pltpu.SemaphoreType.DMA((2 * slots // cap,))],
        cost_estimate=light,
        compiler_params=params(24),
        name="hidden",
    )(here, gate, up)


def turn_kernel(cap, here, v, out, held):
    rows = held.shape[0]
    for k in range(2):
        plane = lax.rem(here[0] + k, 2)
        for q in range(rows // cap):
            held[q * cap : (q + 1) * cap, :] = v[pl.ds(pl.multiple_of((2 * q + plane) * cap, 16), cap), :]
        out[:, k * rows : (k + 1) * rows] = held[...].T


def turn(here, v, cap):
    slots, d = v.shape
    tile = 256
    return pl.pallas_call(
        functools.partial(turn_kernel, cap),
        out_shape=jax.ShapeDtypeStruct((d, slots), v.dtype),
        grid_spec=pltpu.PrefetchScalarGridSpec(
            num_scalar_prefetch=1,
            grid=(d // tile,),
            in_specs=[pl.BlockSpec((slots, tile), lambda i, here: (0, i))],
            out_specs=pl.BlockSpec((tile, slots), lambda i, here: (i, 0)),
            scratch_shapes=[pltpu.VMEM((slots // 2, tile), v.dtype)],
        ),
        cost_estimate=light,
        compiler_params=params(12),
        name="turn",
    )(here, in_hbm(v))


def pack_kernel(line, tokens, routes, codes, out, named, sems):
    tok = tokens.shape[0]
    copies = [
        pltpu.make_async_copy(tokens, out.at[:tok, :], sems.at[0]),
        pltpu.make_async_copy(routes, named.at[0], sems.at[1]),
        pltpu.make_async_copy(codes, named.at[1], sems.at[2]),
    ]
    for c in copies:
        c.start()
    out[tok:, :] = jnp.zeros((8, out.shape[1]), bf16)
    for k, at in enumerate((0, line)):
        copies[1 + k].wait()
        out[tok:, at : at + tok] = named[k].astype(f32).astype(bf16)
    copies[0].wait()


def pack(tokens, routes, codes, line):
    tok, d = tokens.shape
    return pl.pallas_call(
        functools.partial(pack_kernel, line),
        out_shape=jax.ShapeDtypeStruct((tok + 8, d), bf16),
        in_specs=[anywhere] * 3,
        out_specs=on_chip,
        scratch_shapes=[pltpu.VMEM((2, *routes.shape), jnp.int32), pltpu.SemaphoreType.DMA((3,))],
        cost_estimate=light,
        compiler_params=params(8),
        name="pack",
    )(in_hbm(tokens), in_hbm(routes), in_hbm(codes))


def received_kernel(hid, own, other, out):
    rows = own.shape[0]
    part = jnp.dot(hid[:, :rows], own[...], preferred_element_type=f32)
    part = part + jnp.dot(hid[:, rows:], other[...], preferred_element_type=f32)
    out[0] = (part * loss_scale).astype(bf16).T


def received_part(hid, own, other):
    h, slots = hid.shape
    rows, d = own.shape
    tile = 256
    return pl.pallas_call(
        received_kernel,
        out_shape=jax.ShapeDtypeStruct((1, d, 3 * h), bf16),
        grid=(d // tile,),
        in_specs=[pl.BlockSpec((h, slots), lambda i: (0, 0))] + [pl.BlockSpec((rows, tile), lambda i: (0, i))] * 2,
        out_specs=pl.BlockSpec((1, tile, h), lambda i: (0, i, 2)),
        cost_estimate=light,
        compiler_params=params(20),
        name="received_part",
    )(hid, own, other)


def inputs_kernel(cap, last, here, old, inputs, own, other, late, out, held):
    rows = own.shape[0]

    @pl.when(pl.program_id(0) == 0)
    def _():
        held[...] = other[...]
        held[plane_rows(here[0], *last, cap), :] = late[...]

    part = jnp.dot(inputs[:, :rows], own[...], preferred_element_type=f32)
    part = part + jnp.dot(inputs[:, rows:], held[...], preferred_element_type=f32)
    out[0] = (part * loss_scale).astype(bf16)


def inputs_part(here, last, old, inputs, own, other, late, cap):
    d, slots = inputs.shape
    rows, wide = own.shape
    tile = 256

    def fixed(v):
        return pl.BlockSpec(v.shape, lambda i, here: (0, 0))

    return pl.pallas_call(
        functools.partial(inputs_kernel, cap, last),
        out_shape=jax.ShapeDtypeStruct(old.shape, bf16),
        grid_spec=pltpu.PrefetchScalarGridSpec(
            num_scalar_prefetch=1,
            grid=(d // tile,),
            in_specs=[anywhere, pl.BlockSpec((tile, slots), lambda i, here: (i, 0)), fixed(own), fixed(other), fixed(late)],
            out_specs=pl.BlockSpec((1, tile, wide), lambda i, here: (0, i, 0)),
            scratch_shapes=[pltpu.VMEM((rows, wide), bf16)],
        ),
        input_output_aliases={1: 0},
        cost_estimate=light,
        compiler_params=params(24),
        name="inputs_part",
    )(here, old, inputs, own, other, late)


def together(*values):
    return lax.optimization_barrier(values)


def body_grid(out_grad, routes, gate_codes, w_gate, w_up, w_down, saved_inputs, saved_gate, saved_up):
    owners = lax.axis_size("expert")
    me = lax.axis_index("expert")
    to_core = [(i, i ^ 1) for i in range(owners)]
    to_x = [(i, i ^ 2) for i in range(owners)]
    tok, d = out_grad.shape
    choices = routes.shape[1]
    slots = saved_gate.shape[1]
    cap = slots // owners

    def send(v, perm):
        return lax.ppermute(v, "expert", perm)

    line = 256 * pl.cdiv(tok, 256)
    block = pack(out_grad, routes.T, gate_codes.T, line)
    here = me.reshape(1).astype(jnp.int32)

    def ring(v, hops=1):
        return send(v, [(i, (i + 4 * hops) % owners) for i in range(owners)])

    wd, sg, su = w_down[0], saved_gate[0], saved_up[0]
    wd_c, sg_c, su_c = [send(v, to_core) for v in (wd, sg, su)]

    half = slots // 2
    recs, gps = [], []

    def first(chunk, toks):
        recs[:], (share, *shares, pos) = (lambda a, b, *rest: ([a, b], rest))(
            *dispatch(here, chunk, toks, wd, wd_c, cap, half, recs)
        )
        return (chunk, share, pos), *shares

    def exchange(v):
        return lax.ppermute(v, "dp", [(0, 1), (1, 0)])

    def second(state, *peers, last=False):
        chunk, share, pos = state
        gps[:], sums = (lambda a, b, *rest: ([a, b], rest))(
            *combine(here, chunk, share, peers, pos, (sg, su), (sg_c, su_c), w, w_c, cap, half, gps, last)
        )
        return sums

    r1, x0 = ring(block), send(block, to_x)
    c0, h0 = first([(0, 0)], [block])
    w = join(w_gate[0], w_up[0])
    inputs = turn(here, saved_inputs[0], cap)
    r1, x0, h0, w, inputs, sg_c, su_c = together(r1, x0, h0, w, inputs, sg_c, su_c)
    r2, x1 = ring(r1), send(r1, to_x)
    h0, w_c = exchange(h0), send(w, to_core)
    c1, h1, g1 = first([(1, 0), (0, 1)], [x0, r1])
    h1 = exchange(h1)
    (t_r0,) = second(c0, h0)
    hid = hidden(here, sg, su, cap)
    r2, x1, h1, g1, t_r0, hid = together(r2, x1, h1, g1, t_r0, hid)
    r3, x2 = ring(r2), send(r2, to_x)
    g1 = exchange(g1)
    c2, h2, g2 = first([(1, 1), (0, 2)], [x1, r2])
    h2 = exchange(h2)
    t_x0, t_r1 = second(c1, h1, g1)
    r3, x2, h2, g2, t_x0, t_r1 = together(r3, x2, h2, g2, t_x0, t_r1)
    x3, w1 = send(r3, to_x), ring(t_r1)
    g2 = exchange(g2)
    c3, h3, g3 = first([(1, 2), (0, 3)], [x2, r3])
    h3 = exchange(h3)
    t_x1, t_r2 = second(c2, h2, g2)
    x3, w1, h3, g3, t_x0, t_x1, t_r2 = together(x3, w1, h3, g3, t_x0, t_x1, t_r2)
    u1, b0 = ring(t_x1), send(t_x0, to_x)
    g3 = exchange(g3)
    c4, h4 = first([(1, 3)], [x3])
    h4 = exchange(h4)
    t_x2, t_r3 = second(c3, h3, g3)
    u1, b0, h4, t_x2, t_r3, rec_away, gp_away = together(u1, b0, h4, t_x2, t_r3, recs[1], gps[1])
    rec_c, gp_c = send(rec_away, to_core), send(gp_away, to_core)
    a0, a1, h4 = together(add([t_x2, u1], 0), add([t_x2, u1], 1), h4)
    b2 = [send(a0, to_x), send(a1, to_x)]
    t_x3 = second(c4, h4, last=True)
    b3 = [send(t, to_x) for t in t_x3]
    late = send(gps[1], to_core)
    w2 = [ring(add([t_r2, w1, b2[0]], 0))]
    part = received_part(hid, recs[0], rec_c)
    b2[1], part = together(b2[1], part)
    w2.append(ring(add([t_r2, w1, b2[1]], 1)))
    w3 = [ring(add([t_r3, b3[k], w2[k]], k)) for k in range(2)]
    weight_grads = inputs_part(here, (1, 3), part, inputs, gps[0], gp_c, late, cap)
    w3[1], weight_grads = together(w3[1], weight_grads)
    return (finish(t_r0, b0, *w3), weight_grads)


def solution(mesh):
    placed = (
        P("expert", "dp"),
        P("expert", None),
        P("expert", None),
        P("expert", "dp", None),
        P("expert", "dp", None),
        P("expert", None, "dp"),
        P("expert", None, "dp"),
        P("expert", None, None),
        P("expert", None, None),
    )
    small = mesh.shape["expert"] == 16 and mesh.shape["dp"] == 2
    return jax.shard_map(
        body_grid if small else body_any,
        mesh=mesh,
        in_specs=placed,
        out_specs=(P("expert", "dp"), P("expert", "dp", None)),
        check_vma=False,
    )
```

```python
import functools

import jax
import jax.numpy as jnp
from jax import lax
from jax.experimental import pallas as pl
from jax.experimental.pallas import tpu as pltpu
from jax.sharding import PartitionSpec as P

gate_unit = 0.00390625
loss_scale = 0.015625
f32 = jnp.float32
bf16 = jnp.bfloat16


def contract_rows(left, right):
    return lax.dot_general(left, right, (((0,), (0,)), ((), ())), preferred_element_type=f32)


def contract_cols(left, right):
    return lax.dot_general(left, right, (((1,), (1,)), ((), ())), preferred_element_type=f32)


def activation_grads(grad_hidden, gate_pre, up_pre):
    sigmoid = jax.nn.sigmoid(gate_pre)
    silu = gate_pre * sigmoid
    dsilu = sigmoid * (1.0 + gate_pre * (1.0 - sigmoid))
    grad_gate_pre = (grad_hidden * up_pre * dsilu).astype(bf16)
    grad_up_pre = (grad_hidden * silu).astype(bf16)
    return (grad_gate_pre, grad_up_pre)


def sigmoid_of(x):
    return 0.5 * jnp.tanh(0.5 * x) + 0.5


def kernel_grads(grad_hidden, gate_pre, up_pre):
    sigmoid = sigmoid_of(gate_pre)
    silu = gate_pre * sigmoid
    dsilu = sigmoid + silu * (1.0 - sigmoid)
    return ((grad_hidden * up_pre * dsilu).astype(bf16), (grad_hidden * silu).astype(bf16))


def body_any(out_grad, routes, gate_codes, w_gate, w_up, w_down, saved_inputs, saved_gate, saved_up):
    owners = lax.axis_size("expert")
    slot_count = saved_gate.shape[1]
    capacity = slot_count // owners
    token_count = routes.shape[0]
    choice_count = routes.shape[1]
    flat_routes = routes.reshape(-1)
    onehot = (flat_routes[:, None] == jnp.arange(owners, dtype=jnp.int32)[None, :]).astype(jnp.int32)
    earlier = jnp.cumsum(onehot, axis=0) - onehot
    position = jnp.sum(earlier * onehot, axis=1)
    slot_index = (flat_routes * capacity + position).reshape(token_count, choice_count)
    gate_values = gate_codes.astype(f32) * gate_unit
    rows_iota = jnp.arange(slot_count, dtype=jnp.int32)[:, None]
    weighted = jnp.zeros((slot_count, token_count), f32)
    picks = jnp.zeros((slot_count, token_count), f32)
    for pick in range(choice_count):
        hit = rows_iota == slot_index[:, pick][None, :]
        weighted = weighted + jnp.where(hit, gate_values[:, pick][None, :], 0.0)
        picks = picks + hit.astype(f32)
    outgoing = jnp.dot(weighted.astype(bf16), out_grad, preferred_element_type=f32).astype(bf16)
    received = lax.all_to_all(outgoing, "expert", split_axis=0, concat_axis=0, tiled=True)
    hidden_share = lax.psum_scatter(
        contract_cols(received, w_down[0]), "dp", scatter_dimension=0, tiled=True
    )
    gate_pre = saved_gate[0].astype(f32)
    up_pre = saved_up[0].astype(f32)
    hidden = (gate_pre * jax.nn.sigmoid(gate_pre) * up_pre).astype(bf16)
    grad_hidden = lax.all_gather(hidden_share, "dp", axis=0, tiled=True)
    grad_gate_pre, grad_up_pre = activation_grads(grad_hidden, gate_pre, up_pre)
    slot_grads = contract_cols(grad_gate_pre, w_gate[0]) + contract_cols(grad_up_pre, w_up[0])
    returned = lax.all_to_all(
        slot_grads.astype(bf16), "expert", split_axis=0, concat_axis=0, tiled=True
    )
    token_grads = contract_rows(picks.astype(bf16), returned).astype(bf16)
    inputs_here = saved_inputs[0]
    part = jnp.concatenate(
        [
            contract_rows(inputs_here, grad_gate_pre),
            contract_rows(inputs_here, grad_up_pre),
            contract_rows(received, hidden),
        ],
        axis=1,
    )
    return (token_grads, (part * loss_scale).astype(bf16)[None])


on_chip = pl.BlockSpec(memory_space=pltpu.VMEM)
on_scalar = pl.BlockSpec(memory_space=pltpu.SMEM)
anywhere = pl.BlockSpec(memory_space=pl.ANY)
light = pl.CostEstimate(flops=1 << 20, bytes_accessed=1 << 14, transcendentals=0)


def source(here, step, other):
    group = lax.rem(here // 4 + (4 - step), 4)
    return jnp.bitwise_xor(group * 4 + lax.rem(here, 4), 2 * other)


def params(mib):
    return pltpu.CompilerParams(vmem_limit_bytes=mib << 20)


def plane_rows(here, other, step, cap):
    return pl.ds(pl.multiple_of((source(here, step, other) // 2) * cap, 16), cap)


def dispatch_kernel(chunk, cap, begun, here, *refs):
    n = len(chunk)
    toks, (wd0, wd1) = refs[:n], refs[n : n + 2]
    buf0, buf1, share, *share_out, pos_out, rec, sems = refs[n + 2 + 2 * begun :]
    tok = toks[0].shape[0] - 8
    line = 256 * pl.cdiv(tok, 256)
    before = lax.broadcasted_iota(jnp.int32, (tok, tok), 0) < lax.broadcasted_iota(jnp.int32, (tok, tok), 1)
    before = jnp.where(before, 1.0, 0.0).astype(bf16)
    slot = lax.broadcasted_iota(jnp.int32, (cap, tok), 0).astype(f32)
    masks, gates = [], []
    for a in range(2):
        expert = jnp.bitwise_xor(here[0], a).astype(f32)
        for t in toks:
            hit = t[tok:, :tok].astype(f32) == expert
            masks.append(jnp.max(jnp.where(hit, 1.0, 0.0), axis=0, keepdims=True))
            gates.append(jnp.sum(jnp.where(hit, t[tok:, line : line + tok].astype(f32), 0.0), axis=0, keepdims=True))
    fill = [jnp.zeros((8 - 2 * n, tok), f32)] if n < 4 else []
    mask = jnp.concatenate(masks + fill, axis=0)
    pos = jnp.dot(mask.astype(bf16), before, preferred_element_type=f32)
    pos = jnp.where(mask > 0.0, pos, -1.0)
    pos_out[...] = pos
    copies = []
    for rel, t in enumerate(toks):
        w = [
            jnp.where(slot == pos[i : i + 1, :], gates[i] * gate_unit, 0.0).astype(bf16)
            for i in (rel, n + rel)
        ]
        rows = jnp.dot(jnp.concatenate(w, axis=0), t[:tok, :], preferred_element_type=f32).astype(bf16)
        at = pl.ds(rel * cap, cap)
        for a, buf in enumerate((buf0, buf1)):
            rec[a, at, :] = rows[a * cap : (a + 1) * cap]
            to = plane_rows(here[0], *chunk[rel], cap)
            copies.append(pltpu.make_async_copy(rec.at[a, at, :], buf.at[to, :], sems.at[len(copies)]))
    for c in copies:
        c.start()
    for a, wd in enumerate((wd0, wd1)):
        gh = contract_cols(rec[a], wd[...])
        share[a * n * cap : (a + 1) * n * cap, :] = gh
        if n == 1:
            share_out[0][a * cap : (a + 1) * cap, :] = gh.astype(bf16)
        else:
            share_out[a][...] = gh.astype(bf16)
    for c in copies:
        c.wait()


def dispatch(here, chunk, toks, wd0, wd1, cap, rows, old):
    n = len(toks)
    tok, d = toks[0].shape
    h = wd0.shape[0]
    outs = [((rows, d), bf16)] * 2 + [((2 * n * cap, h), f32)]
    outs += [((2 * cap, h), bf16)] if n == 1 else [((n * cap, h), bf16)] * 2
    outs += [((8, tok - 8), f32)]
    return pl.pallas_call(
        functools.partial(dispatch_kernel, chunk, cap, len(old) // 2),
        out_shape=[jax.ShapeDtypeStruct(s, t) for s, t in outs],
        in_specs=[on_scalar] + [on_chip] * (n + 2) + [anywhere] * len(old),
        out_specs=[anywhere] * 2 + [on_chip] * (len(outs) - 2),
        scratch_shapes=[pltpu.VMEM((2, n * cap, d), bf16), pltpu.SemaphoreType.DMA((2 * n,))],
        input_output_aliases={n + 3 + k: k for k in range(len(old))},
        cost_estimate=light,
        compiler_params=params(16),
        name="dispatch",
    )(here, *toks, wd0, wd1, *old)


def combine_kernel(chunk, cap, begun, last, here, share, *refs):
    n = len(chunk)
    if n == 1:
        peer0, peer1 = refs[0].at[:cap, :], refs[0].at[cap:, :]
        pos, *refs = refs[1:]
    else:
        peer0, peer1, pos, *refs = refs
    saved, ws, refs = refs[:4], refs[4:6], refs[6 + begun :]
    buffers, backs, (held, gps, sems, out_sems) = refs[:2], refs[2:-4], refs[-4:]
    h = share.shape[1]
    copies = []
    for a in range(2):
        for other, step in chunk:
            rows = pl.ds(pl.multiple_of(source(here[0], step, other) * cap, 16), cap)
            for v in saved[2 * a : 2 * a + 2]:
                i = len(copies)
                copies.append(pltpu.make_async_copy(v.at[rows, :], held.at[i], sems.at[i]))
    for c in copies:
        c.start()
    slot = lax.broadcasted_iota(jnp.int32, (cap, pos.shape[1]), 0).astype(f32)
    leaving = []
    for c in copies:
        c.wait()
    for a, peer in enumerate((peer0, peer1)):
        for rel in range(n):
            i = a * n + rel
            at = slice(rel * cap, (rel + 1) * cap)
            gh = share[i * cap : (i + 1) * cap, :] + peer[at, :].astype(f32)
            gg, gu = kernel_grads(gh, held[2 * i].astype(f32), held[2 * i + 1].astype(f32))
            gps[a, at, :h] = gg
            gps[a, at, h:] = gu
            if a == 0 or not last:
                to = buffers[a].at[plane_rows(here[0], *chunk[rel], cap), :]
                leaving.append(pltpu.make_async_copy(gps.at[a, at, :], to, out_sems.at[i]))
    for c in leaving:
        c.start()
    if last:
        buffers[1][...] = gps[1]
    sums = [None] * n
    for a, w in enumerate(ws):
        slots = contract_cols(gps[a], w[...]).astype(bf16)
        for rel in range(n):
            i = a * n + rel
            pick = jnp.where(slot == pos[i : i + 1, :], 1.0, 0.0).astype(bf16)
            part = contract_rows(pick, slots[rel * cap : (rel + 1) * cap])
            sums[rel] = part if sums[rel] is None else sums[rel] + part
    if len(backs) > n:
        half = backs[0].shape[1]
        for k, back in enumerate(backs):
            back[...] = sums[0][:, k * half : (k + 1) * half].astype(bf16)
    else:
        for rel in range(n):
            backs[rel][...] = sums[rel].astype(bf16)
    for c in leaving:
        c.wait()


def combine(here, chunk, share, peers, pos, saved0, saved1, w0, w1, cap, rows, old, last=False):
    n = len(chunk)
    h = share.shape[1]
    d = w0.shape[0]
    tok = pos.shape[1]
    old = old[:1] if last else old
    outs = [(rows, 2 * h), (n * cap if last else rows, 2 * h)] + ([(tok, d // 2)] * 2 if last else [(tok, d)] * n)
    first_old = 2 + len(peers) + 1 + 4 + 2
    return pl.pallas_call(
        functools.partial(combine_kernel, chunk, cap, len(old), last),
        out_shape=[jax.ShapeDtypeStruct(s, bf16) for s in outs],
        in_specs=[on_scalar] + [on_chip] * (2 + len(peers)) + [anywhere] * 4 + [on_chip] * 2 + [anywhere] * len(old),
        out_specs=[anywhere, on_chip if last else anywhere] + [on_chip] * (len(outs) - 2),
        scratch_shapes=[
            pltpu.VMEM((4 * n, cap, h), bf16),
            pltpu.VMEM((2, n * cap, 2 * h), bf16),
            pltpu.SemaphoreType.DMA((4 * n,)),
            pltpu.SemaphoreType.DMA((2 * n,)),
        ],
        input_output_aliases={first_old + k: k for k in range(len(old))},
        cost_estimate=light,
        compiler_params=params(20),
        name="combine",
    )(here, share, *peers, pos, *saved0, *saved1, w0, w1, *old)


def join_kernel(left, right, out):
    out[:, : left.shape[1]] = left[...]
    out[:, left.shape[1] :] = right[...]


def join(left, right):
    rows, h = left.shape
    return pl.pallas_call(
        join_kernel,
        out_shape=jax.ShapeDtypeStruct((rows, 2 * h), left.dtype),
        in_specs=[on_chip] * 2,
        out_specs=on_chip,
        cost_estimate=light,
        compiler_params=params(8),
        name="join",
    )(left, right)


def add_kernel(part, *refs):
    wide = refs[-1].shape[1]
    total = None
    for r in refs[:-1]:
        v = r[...] if part is None or r.shape[1] == wide else r[:, part * wide : (part + 1) * wide]
        total = v.astype(f32) if total is None else total + v.astype(f32)
    refs[-1][...] = total.astype(bf16)


def add(values, part=None):
    rows, wide = values[0].shape
    return pl.pallas_call(
        functools.partial(add_kernel, part),
        out_shape=jax.ShapeDtypeStruct((rows, wide if part is None else wide // 2), bf16),
        in_specs=[on_chip] * len(values),
        out_specs=on_chip,
        cost_estimate=light,
        compiler_params=params(8),
        name="add",
    )(*values)


def finish_kernel(a, b, left, right, out):
    half = left.shape[1]
    for at, v in ((0, left), (half, right)):
        total = a[:, at : at + half].astype(f32) + b[:, at : at + half].astype(f32) + v[...].astype(f32)
        out[:, at : at + half] = total.astype(bf16)


def finish(a, b, left, right):
    return pl.pallas_call(
        finish_kernel,
        out_shape=jax.ShapeDtypeStruct(a.shape, bf16),
        in_specs=[on_chip] * 4,
        out_specs=on_chip,
        cost_estimate=light,
        compiler_params=params(8),
        name="finish",
    )(a, b, left, right)


def in_hbm(v):
    return pltpu.with_memory_space_constraint(v, pltpu.HBM)


def hidden_kernel(cap, k, here, gate, up, out, held, sems):
    plane = lax.rem(here[0] + k, 2)
    copies = []
    for i, v in enumerate((gate, up)):
        for q in range(held.shape[1] // cap):
            at = pl.ds(pl.multiple_of((2 * q + plane) * cap, 16), cap)
            to = held.at[i, pl.ds(q * cap, cap), :]
            copies.append(pltpu.make_async_copy(v.at[at, :], to, sems.at[len(copies)]))
    for c in copies:
        c.start()
    for c in copies:
        c.wait()
    gate_pre = held[0].astype(f32)
    out[...] = (gate_pre * sigmoid_of(gate_pre) * held[1].astype(f32)).astype(bf16).T


def hidden(here, gate, up, cap, k):
    slots, h = gate.shape
    return pl.pallas_call(
        functools.partial(hidden_kernel, cap, k),
        out_shape=jax.ShapeDtypeStruct((h, slots // 2), bf16),
        in_specs=[on_scalar, anywhere, anywhere],
        out_specs=on_chip,
        scratch_shapes=[pltpu.VMEM((2, slots // 2, h), bf16), pltpu.SemaphoreType.DMA((slots // cap,))],
        cost_estimate=light,
        compiler_params=params(16),
        name="hidden",
    )(here, in_hbm(gate), in_hbm(up))


def turn_kernel(cap, here, v, out, held):
    rows = held.shape[0]
    for k in range(2):
        plane = lax.rem(here[0] + k, 2)
        for q in range(rows // cap):
            held[q * cap : (q + 1) * cap, :] = v[pl.ds(pl.multiple_of((2 * q + plane) * cap, 16), cap), :]
        out[:, k * rows : (k + 1) * rows] = held[...].T


def turn(here, v, cap):
    slots, d = v.shape
    tile = 256
    return pl.pallas_call(
        functools.partial(turn_kernel, cap),
        out_shape=jax.ShapeDtypeStruct((d, slots), v.dtype),
        grid_spec=pltpu.PrefetchScalarGridSpec(
            num_scalar_prefetch=1,
            grid=(d // tile,),
            in_specs=[pl.BlockSpec((slots, tile), lambda i, here: (0, i))],
            out_specs=pl.BlockSpec((tile, slots), lambda i, here: (i, 0)),
            scratch_shapes=[pltpu.VMEM((slots // 2, tile), v.dtype)],
        ),
        cost_estimate=light,
        compiler_params=params(12),
        name="turn",
    )(here, in_hbm(v))


def pack_kernel(line, tokens, routes, codes, out, named, sems):
    tok = tokens.shape[0]
    copies = [
        pltpu.make_async_copy(tokens, out.at[:tok, :], sems.at[0]),
        pltpu.make_async_copy(routes, named.at[0], sems.at[1]),
        pltpu.make_async_copy(codes, named.at[1], sems.at[2]),
    ]
    for c in copies:
        c.start()
    out[tok:, :] = jnp.zeros((8, out.shape[1]), bf16)
    for k, at in enumerate((0, line)):
        copies[1 + k].wait()
        out[tok:, at : at + tok] = named[k].astype(f32).astype(bf16)
    copies[0].wait()


def pack(tokens, routes, codes, line):
    tok, d = tokens.shape
    return pl.pallas_call(
        functools.partial(pack_kernel, line),
        out_shape=jax.ShapeDtypeStruct((tok + 8, d), bf16),
        in_specs=[anywhere] * 3,
        out_specs=on_chip,
        scratch_shapes=[pltpu.VMEM((2, *routes.shape), jnp.int32), pltpu.SemaphoreType.DMA((3,))],
        cost_estimate=light,
        compiler_params=params(8),
        name="pack",
    )(in_hbm(tokens), in_hbm(routes), in_hbm(codes))


def received_kernel(hid, hid_c, own, other, out):
    part = jnp.dot(hid[...], own[...], preferred_element_type=f32)
    part = part + jnp.dot(hid_c[...], other[...], preferred_element_type=f32)
    out[0] = (part * loss_scale).astype(bf16).T


def received_part(hid, hid_c, own, other):
    h = hid.shape[0]
    rows, d = own.shape
    tile = 256
    return pl.pallas_call(
        received_kernel,
        out_shape=jax.ShapeDtypeStruct((1, d, 3 * h), bf16),
        grid=(d // tile,),
        in_specs=[pl.BlockSpec((h, rows), lambda i: (0, 0))] * 2 + [pl.BlockSpec((rows, tile), lambda i: (0, i))] * 2,
        out_specs=pl.BlockSpec((1, tile, h), lambda i: (0, i, 2)),
        cost_estimate=light,
        compiler_params=params(20),
        name="received_part",
    )(hid, hid_c, own, other)


def inputs_kernel(cap, last, here, old, inputs, own, other, late, out, held):
    rows = own.shape[0]

    @pl.when(pl.program_id(0) == 0)
    def _():
        held[...] = other[...]
        held[plane_rows(here[0], *last, cap), :] = late[...]

    part = jnp.dot(inputs[:, :rows], own[...], preferred_element_type=f32)
    part = part + jnp.dot(inputs[:, rows:], held[...], preferred_element_type=f32)
    out[0] = (part * loss_scale).astype(bf16)


def inputs_part(here, last, old, inputs, own, other, late, cap):
    d, slots = inputs.shape
    rows, wide = own.shape
    tile = 256

    def fixed(v):
        return pl.BlockSpec(v.shape, lambda i, here: (0, 0))

    return pl.pallas_call(
        functools.partial(inputs_kernel, cap, last),
        out_shape=jax.ShapeDtypeStruct(old.shape, bf16),
        grid_spec=pltpu.PrefetchScalarGridSpec(
            num_scalar_prefetch=1,
            grid=(d // tile,),
            in_specs=[anywhere, pl.BlockSpec((tile, slots), lambda i, here: (i, 0)), fixed(own), fixed(other), fixed(late)],
            out_specs=pl.BlockSpec((1, tile, wide), lambda i, here: (0, i, 0)),
            scratch_shapes=[pltpu.VMEM((rows, wide), bf16)],
        ),
        input_output_aliases={1: 0},
        cost_estimate=light,
        compiler_params=params(24),
        name="inputs_part",
    )(here, old, inputs, own, other, late)


def together(*values):
    return lax.optimization_barrier(values)


def body_grid(out_grad, routes, gate_codes, w_gate, w_up, w_down, saved_inputs, saved_gate, saved_up):
    owners = lax.axis_size("expert")
    me = lax.axis_index("expert")
    to_core = [(i, i ^ 1) for i in range(owners)]
    to_x = [(i, i ^ 2) for i in range(owners)]
    tok, d = out_grad.shape
    choices = routes.shape[1]
    slots = saved_gate.shape[1]
    cap = slots // owners

    def send(v, perm):
        return lax.ppermute(v, "expert", perm)

    line = 256 * pl.cdiv(tok, 256)
    block = pack(out_grad, routes.T, gate_codes.T, line)
    here = me.reshape(1).astype(jnp.int32)

    def ring(v, hops=1):
        return send(v, [(i, (i + 4 * hops) % owners) for i in range(owners)])

    wd, sg, su = w_down[0], saved_gate[0], saved_up[0]
    wd_c, sg_c, su_c = [send(v, to_core) for v in (wd, sg, su)]

    half = slots // 2
    recs, gps = [], []

    def first(chunk, toks):
        recs[:], (share, *shares, pos) = (lambda a, b, *rest: ([a, b], rest))(
            *dispatch(here, chunk, toks, wd, wd_c, cap, half, recs)
        )
        return (chunk, share, pos), *shares

    def exchange(v):
        return lax.ppermute(v, "dp", [(0, 1), (1, 0)])

    def second(state, *peers, last=False):
        chunk, share, pos = state
        gps[:], sums = (lambda a, b, *rest: ([a, b], rest))(
            *combine(here, chunk, share, peers, pos, (sg, su), (sg_c, su_c), w, w_c, cap, half, gps, last)
        )
        return sums

    r1, x0 = ring(block), send(block, to_x)
    c0, h0 = first([(0, 0)], [block])
    w = join(w_gate[0], w_up[0])
    inputs = turn(here, saved_inputs[0], cap)
    hid = hidden(here, sg, su, cap, 0)
    r1, x0, h0, w, inputs, hid, sg_c, su_c = together(r1, x0, h0, w, inputs, hid, sg_c, su_c)
    r2, x1 = ring(r1), send(r1, to_x)
    h0, w_c = exchange(h0), send(w, to_core)
    c1, h1, g1 = first([(1, 0), (0, 1)], [x0, r1])
    h1 = exchange(h1)
    (t_r0,) = second(c0, h0)
    r2, x1, h1, g1, t_r0 = together(r2, x1, h1, g1, t_r0)
    r3, x2 = ring(r2), send(r2, to_x)
    g1 = exchange(g1)
    c2, h2, g2 = first([(1, 1), (0, 2)], [x1, r2])
    h2 = exchange(h2)
    t_x0, t_r1 = second(c1, h1, g1)
    r3, x2, h2, g2, t_x0, t_r1 = together(r3, x2, h2, g2, t_x0, t_r1)
    x3, w1 = send(r3, to_x), ring(t_r1)
    g2 = exchange(g2)
    c3, h3, g3 = first([(1, 2), (0, 3)], [x2, r3])
    h3 = exchange(h3)
    t_x1, t_r2 = second(c2, h2, g2)
    x3, w1, h3, g3, t_x0, t_x1, t_r2 = together(x3, w1, h3, g3, t_x0, t_x1, t_r2)
    u1, b0 = ring(t_x1), send(t_x0, to_x)
    g3 = exchange(g3)
    c4, h4 = first([(1, 3)], [x3])
    h4 = exchange(h4)
    t_x2, t_r3 = second(c3, h3, g3)
    hid_c = hidden(here, sg, su, cap, 1)
    u1, b0, h4, t_x2, t_r3, hid_c, rec_away, gp_away = together(u1, b0, h4, t_x2, t_r3, hid_c, recs[1], gps[1])
    rec_c, gp_c = send(rec_away, to_core), send(gp_away, to_core)
    a0, a1, h4 = together(add([t_x2, u1], 0), add([t_x2, u1], 1), h4)
    b2 = [send(a0, to_x), send(a1, to_x)]
    left, right = second(c4, h4, last=True)
    left, rec_c = together(left, rec_c)
    b3 = [send(left, to_x), send(right, to_x)]
    late = send(gps[1], to_core)
    w2 = [ring(add([t_r2, w1, b2[k]], k)) for k in range(2)]
    part = received_part(hid, hid_c, recs[0], rec_c)
    w2[0], part = together(w2[0], part)
    w3 = [ring(add([t_r3, b3[k], w2[k]], k)) for k in range(2)]
    weight_grads = inputs_part(here, (1, 3), part, inputs, gps[0], gp_c, late, cap)
    w3[1], weight_grads = together(w3[1], weight_grads)
    return (finish(t_r0, b0, *w3), weight_grads)


def solution(mesh):
    placed = (
        P("expert", "dp"),
        P("expert", None),
        P("expert", None),
        P("expert", "dp", None),
        P("expert", "dp", None),
        P("expert", None, "dp"),
        P("expert", None, "dp"),
        P("expert", None, None),
        P("expert", None, None),
    )
    small = mesh.shape["expert"] == 16 and mesh.shape["dp"] == 2
    return jax.shard_map(
        body_grid if small else body_any,
        mesh=mesh,
        in_specs=placed,
        out_specs=(P("expert", "dp"), P("expert", "dp", None)),
        check_vma=False,
    )
```

```python
import functools

import jax
import jax.numpy as jnp
from jax import lax
from jax.experimental import pallas as pl
from jax.experimental.pallas import tpu as pltpu
from jax.sharding import PartitionSpec as P

gate_unit = 0.00390625
loss_scale = 0.015625
f32 = jnp.float32
bf16 = jnp.bfloat16


def contract_rows(left, right):
    return lax.dot_general(left, right, (((0,), (0,)), ((), ())), preferred_element_type=f32)


def contract_cols(left, right):
    return lax.dot_general(left, right, (((1,), (1,)), ((), ())), preferred_element_type=f32)


def activation_grads(grad_hidden, gate_pre, up_pre):
    sigmoid = jax.nn.sigmoid(gate_pre)
    silu = gate_pre * sigmoid
    dsilu = sigmoid * (1.0 + gate_pre * (1.0 - sigmoid))
    grad_gate_pre = (grad_hidden * up_pre * dsilu).astype(bf16)
    grad_up_pre = (grad_hidden * silu).astype(bf16)
    return (grad_gate_pre, grad_up_pre)


def sigmoid_of(x):
    return 0.5 * jnp.tanh(0.5 * x) + 0.5


def kernel_grads(grad_hidden, gate_pre, up_pre):
    sigmoid = sigmoid_of(gate_pre)
    silu = gate_pre * sigmoid
    dsilu = sigmoid + silu * (1.0 - sigmoid)
    return ((grad_hidden * up_pre * dsilu).astype(bf16), (grad_hidden * silu).astype(bf16))


def body_any(out_grad, routes, gate_codes, w_gate, w_up, w_down, saved_inputs, saved_gate, saved_up):
    owners = lax.axis_size("expert")
    slot_count = saved_gate.shape[1]
    capacity = slot_count // owners
    token_count = routes.shape[0]
    choice_count = routes.shape[1]
    flat_routes = routes.reshape(-1)
    onehot = (flat_routes[:, None] == jnp.arange(owners, dtype=jnp.int32)[None, :]).astype(jnp.int32)
    earlier = jnp.cumsum(onehot, axis=0) - onehot
    position = jnp.sum(earlier * onehot, axis=1)
    slot_index = (flat_routes * capacity + position).reshape(token_count, choice_count)
    gate_values = gate_codes.astype(f32) * gate_unit
    rows_iota = jnp.arange(slot_count, dtype=jnp.int32)[:, None]
    weighted = jnp.zeros((slot_count, token_count), f32)
    picks = jnp.zeros((slot_count, token_count), f32)
    for pick in range(choice_count):
        hit = rows_iota == slot_index[:, pick][None, :]
        weighted = weighted + jnp.where(hit, gate_values[:, pick][None, :], 0.0)
        picks = picks + hit.astype(f32)
    outgoing = jnp.dot(weighted.astype(bf16), out_grad, preferred_element_type=f32).astype(bf16)
    received = lax.all_to_all(outgoing, "expert", split_axis=0, concat_axis=0, tiled=True)
    hidden_share = lax.psum_scatter(
        contract_cols(received, w_down[0]), "dp", scatter_dimension=0, tiled=True
    )
    gate_pre = saved_gate[0].astype(f32)
    up_pre = saved_up[0].astype(f32)
    hidden = (gate_pre * jax.nn.sigmoid(gate_pre) * up_pre).astype(bf16)
    grad_hidden = lax.all_gather(hidden_share, "dp", axis=0, tiled=True)
    grad_gate_pre, grad_up_pre = activation_grads(grad_hidden, gate_pre, up_pre)
    slot_grads = contract_cols(grad_gate_pre, w_gate[0]) + contract_cols(grad_up_pre, w_up[0])
    returned = lax.all_to_all(
        slot_grads.astype(bf16), "expert", split_axis=0, concat_axis=0, tiled=True
    )
    token_grads = contract_rows(picks.astype(bf16), returned).astype(bf16)
    inputs_here = saved_inputs[0]
    part = jnp.concatenate(
        [
            contract_rows(inputs_here, grad_gate_pre),
            contract_rows(inputs_here, grad_up_pre),
            contract_rows(received, hidden),
        ],
        axis=1,
    )
    return (token_grads, (part * loss_scale).astype(bf16)[None])


on_chip = pl.BlockSpec(memory_space=pltpu.VMEM)
on_scalar = pl.BlockSpec(memory_space=pltpu.SMEM)
anywhere = pl.BlockSpec(memory_space=pl.ANY)
light = pl.CostEstimate(flops=1 << 20, bytes_accessed=1 << 14, transcendentals=0)


def source(here, step, other):
    group = lax.rem(here // 4 + (4 - step), 4)
    return jnp.bitwise_xor(group * 4 + lax.rem(here, 4), 2 * other)


def params(mib):
    return pltpu.CompilerParams(vmem_limit_bytes=mib << 20)


def plane_rows(here, other, step, cap):
    return pl.ds(pl.multiple_of((source(here, step, other) // 2) * cap, 16), cap)


def dispatch_kernel(chunk, cap, begun, here, *refs):
    n = len(chunk)
    toks, (wd0, wd1) = refs[:n], refs[n : n + 2]
    buf0, buf1, share, *share_out, pos_out, rec, sems = refs[n + 2 + 2 * begun :]
    tok = toks[0].shape[0] - 8
    line = 256 * pl.cdiv(tok, 256)
    before = lax.broadcasted_iota(jnp.int32, (tok, tok), 0) < lax.broadcasted_iota(jnp.int32, (tok, tok), 1)
    before = jnp.where(before, 1.0, 0.0).astype(bf16)
    slot = lax.broadcasted_iota(jnp.int32, (cap, tok), 0).astype(f32)
    masks, gates = [], []
    for a in range(2):
        expert = jnp.bitwise_xor(here[0], a).astype(f32)
        for t in toks:
            hit = t[tok:, :tok].astype(f32) == expert
            masks.append(jnp.max(jnp.where(hit, 1.0, 0.0), axis=0, keepdims=True))
            gates.append(jnp.sum(jnp.where(hit, t[tok:, line : line + tok].astype(f32), 0.0), axis=0, keepdims=True))
    fill = [jnp.zeros((8 - 2 * n, tok), f32)] if n < 4 else []
    mask = jnp.concatenate(masks + fill, axis=0)
    pos = jnp.dot(mask.astype(bf16), before, preferred_element_type=f32)
    pos = jnp.where(mask > 0.0, pos, -1.0)
    pos_out[...] = pos
    copies = []
    for rel, t in enumerate(toks):
        w = [
            jnp.where(slot == pos[i : i + 1, :], gates[i] * gate_unit, 0.0).astype(bf16)
            for i in (rel, n + rel)
        ]
        rows = jnp.dot(jnp.concatenate(w, axis=0), t[:tok, :], preferred_element_type=f32).astype(bf16)
        at = pl.ds(rel * cap, cap)
        for a, buf in enumerate((buf0, buf1)):
            rec[a, at, :] = rows[a * cap : (a + 1) * cap]
            to = plane_rows(here[0], *chunk[rel], cap)
            copies.append(pltpu.make_async_copy(rec.at[a, at, :], buf.at[to, :], sems.at[len(copies)]))
    for c in copies:
        c.start()
    for a, wd in enumerate((wd0, wd1)):
        gh = contract_cols(rec[a], wd[...])
        share[a * n * cap : (a + 1) * n * cap, :] = gh
        if n == 1:
            share_out[0][a * cap : (a + 1) * cap, :] = gh.astype(bf16)
        else:
            share_out[a][...] = gh.astype(bf16)
    for c in copies:
        c.wait()


def dispatch(here, chunk, toks, wd0, wd1, cap, rows, old):
    n = len(toks)
    tok, d = toks[0].shape
    h = wd0.shape[0]
    outs = [((rows, d), bf16)] * 2 + [((2 * n * cap, h), f32)]
    outs += [((2 * cap, h), bf16)] if n == 1 else [((n * cap, h), bf16)] * 2
    outs += [((8, tok - 8), f32)]
    return pl.pallas_call(
        functools.partial(dispatch_kernel, chunk, cap, len(old) // 2),
        out_shape=[jax.ShapeDtypeStruct(s, t) for s, t in outs],
        in_specs=[on_scalar] + [on_chip] * (n + 2) + [anywhere] * len(old),
        out_specs=[anywhere] * 2 + [on_chip] * (len(outs) - 2),
        scratch_shapes=[pltpu.VMEM((2, n * cap, d), bf16), pltpu.SemaphoreType.DMA((2 * n,))],
        input_output_aliases={n + 3 + k: k for k in range(len(old))},
        cost_estimate=light,
        compiler_params=params(16),
        name="dispatch",
    )(here, *toks, wd0, wd1, *old)


def combine_kernel(chunk, cap, begun, last, here, share, *refs):
    n = len(chunk)
    if n == 1:
        peer0, peer1 = refs[0].at[:cap, :], refs[0].at[cap:, :]
        pos, *refs = refs[1:]
    else:
        peer0, peer1, pos, *refs = refs
    saved, ws, refs = refs[:4], refs[4:6], refs[6 + begun :]
    buffers, backs, (gps, out_sems) = refs[:2], refs[2:-2], refs[-2:]
    h = share.shape[1]
    slot = lax.broadcasted_iota(jnp.int32, (cap, pos.shape[1]), 0).astype(f32)
    leaving = []
    for a, peer in enumerate((peer0, peer1)):
        for rel in range(n):
            i = a * n + rel
            at = slice(rel * cap, (rel + 1) * cap)
            gh = share[i * cap : (i + 1) * cap, :] + peer[at, :].astype(f32)
            other, step = chunk[rel]
            own = pl.ds(pl.multiple_of(source(here[0], step, other) * cap, 16), cap)
            gg, gu = kernel_grads(gh, saved[2 * a][own, :].astype(f32), saved[2 * a + 1][own, :].astype(f32))
            gps[a, at, :h] = gg
            gps[a, at, h:] = gu
            if a == 0 or not last:
                to = buffers[a].at[plane_rows(here[0], *chunk[rel], cap), :]
                leaving.append(pltpu.make_async_copy(gps.at[a, at, :], to, out_sems.at[i]))
    for c in leaving:
        c.start()
    if last:
        buffers[1][...] = gps[1]
    sums = [None] * n
    for a, w in enumerate(ws):
        slots = contract_cols(gps[a], w[...]).astype(bf16)
        for rel in range(n):
            i = a * n + rel
            pick = jnp.where(slot == pos[i : i + 1, :], 1.0, 0.0).astype(bf16)
            part = contract_rows(pick, slots[rel * cap : (rel + 1) * cap])
            sums[rel] = part if sums[rel] is None else sums[rel] + part
    if len(backs) > n:
        half = backs[0].shape[1]
        for k, back in enumerate(backs):
            back[...] = sums[0][:, k * half : (k + 1) * half].astype(bf16)
    else:
        for rel in range(n):
            backs[rel][...] = sums[rel].astype(bf16)
    for c in leaving:
        c.wait()


def combine(here, chunk, share, peers, pos, saved0, saved1, w0, w1, cap, rows, old, last=False):
    n = len(chunk)
    h = share.shape[1]
    d = w0.shape[0]
    tok = pos.shape[1]
    old = old[:1] if last else old
    outs = [(rows, 2 * h), (n * cap if last else rows, 2 * h)] + ([(tok, d // 2)] * 2 if last else [(tok, d)] * n)
    first_old = 2 + len(peers) + 1 + 4 + 2
    return pl.pallas_call(
        functools.partial(combine_kernel, chunk, cap, len(old), last),
        out_shape=[jax.ShapeDtypeStruct(s, bf16) for s in outs],
        in_specs=[on_scalar] + [on_chip] * (2 + len(peers) + 6) + [anywhere] * len(old),
        out_specs=[anywhere, on_chip if last else anywhere] + [on_chip] * (len(outs) - 2),
        scratch_shapes=[
            pltpu.VMEM((2, n * cap, 2 * h), bf16),
            pltpu.SemaphoreType.DMA((2 * n,)),
        ],
        input_output_aliases={first_old + k: k for k in range(len(old))},
        cost_estimate=light,
        compiler_params=params(20),
        name="combine",
    )(here, share, *peers, pos, *saved0, *saved1, w0, w1, *old)


def join_kernel(left, right, out):
    out[:, : left.shape[1]] = left[...]
    out[:, left.shape[1] :] = right[...]


def join(left, right):
    rows, h = left.shape
    return pl.pallas_call(
        join_kernel,
        out_shape=jax.ShapeDtypeStruct((rows, 2 * h), left.dtype),
        in_specs=[on_chip] * 2,
        out_specs=on_chip,
        cost_estimate=light,
        compiler_params=params(8),
        name="join",
    )(left, right)


def add_kernel(part, *refs):
    wide = refs[-1].shape[1]
    total = None
    for r in refs[:-1]:
        v = r[...] if part is None or r.shape[1] == wide else r[:, part * wide : (part + 1) * wide]
        total = v.astype(f32) if total is None else total + v.astype(f32)
    refs[-1][...] = total.astype(bf16)


def add(values, part=None):
    rows, wide = values[0].shape
    return pl.pallas_call(
        functools.partial(add_kernel, part),
        out_shape=jax.ShapeDtypeStruct((rows, wide if part is None else wide // 2), bf16),
        in_specs=[on_chip] * len(values),
        out_specs=on_chip,
        cost_estimate=light,
        compiler_params=params(8),
        name="add",
    )(*values)


def add_halves_kernel(a, b, left, right):
    total = (a[...].astype(f32) + b[...].astype(f32)).astype(bf16)
    left[...] = total[:, : left.shape[1]]
    right[...] = total[:, left.shape[1] :]


def add_halves(a, b):
    rows, wide = a.shape
    return pl.pallas_call(
        add_halves_kernel,
        out_shape=[jax.ShapeDtypeStruct((rows, wide // 2), bf16)] * 2,
        in_specs=[on_chip] * 2,
        out_specs=[on_chip] * 2,
        cost_estimate=light,
        compiler_params=params(8),
        name="add_halves",
    )(a, b)


def finish_kernel(a, b, left, right, out):
    half = left.shape[1]
    for at, v in ((0, left), (half, right)):
        total = a[:, at : at + half].astype(f32) + b[:, at : at + half].astype(f32) + v[...].astype(f32)
        out[:, at : at + half] = total.astype(bf16)


def finish(a, b, left, right):
    return pl.pallas_call(
        finish_kernel,
        out_shape=jax.ShapeDtypeStruct(a.shape, bf16),
        in_specs=[on_chip] * 4,
        out_specs=on_chip,
        cost_estimate=light,
        compiler_params=params(8),
        name="finish",
    )(a, b, left, right)


def in_hbm(v):
    return pltpu.with_memory_space_constraint(v, pltpu.HBM)


def hidden_kernel(cap, k, here, gate, up, out, held, sems):
    plane = lax.rem(here[0] + k, 2)
    copies = []
    for i, v in enumerate((gate, up)):
        for q in range(held.shape[1] // cap):
            at = pl.ds(pl.multiple_of((2 * q + plane) * cap, 16), cap)
            to = held.at[i, pl.ds(q * cap, cap), :]
            copies.append(pltpu.make_async_copy(v.at[at, :], to, sems.at[len(copies)]))
    for c in copies:
        c.start()
    for c in copies:
        c.wait()
    gate_pre = held[0].astype(f32)
    out[...] = (gate_pre * sigmoid_of(gate_pre) * held[1].astype(f32)).astype(bf16).T


def hidden(here, gate, up, cap, k):
    slots, h = gate.shape
    return pl.pallas_call(
        functools.partial(hidden_kernel, cap, k),
        out_shape=jax.ShapeDtypeStruct((h, slots // 2), bf16),
        in_specs=[on_scalar, anywhere, anywhere],
        out_specs=on_chip,
        scratch_shapes=[pltpu.VMEM((2, slots // 2, h), bf16), pltpu.SemaphoreType.DMA((slots // cap,))],
        cost_estimate=light,
        compiler_params=params(16),
        name="hidden",
    )(here, in_hbm(gate), in_hbm(up))


def turn_kernel(cap, here, v, out, held):
    rows = held.shape[0]
    for k in range(2):
        plane = lax.rem(here[0] + k, 2)
        for q in range(rows // cap):
            held[q * cap : (q + 1) * cap, :] = v[pl.ds(pl.multiple_of((2 * q + plane) * cap, 16), cap), :]
        out[:, k * rows : (k + 1) * rows] = held[...].T


def turn(here, v, cap):
    slots, d = v.shape
    tile = 256
    return pl.pallas_call(
        functools.partial(turn_kernel, cap),
        out_shape=jax.ShapeDtypeStruct((d, slots), v.dtype),
        grid_spec=pltpu.PrefetchScalarGridSpec(
            num_scalar_prefetch=1,
            grid=(d // tile,),
            in_specs=[pl.BlockSpec((slots, tile), lambda i, here: (0, i))],
            out_specs=pl.BlockSpec((tile, slots), lambda i, here: (i, 0)),
            scratch_shapes=[pltpu.VMEM((slots // 2, tile), v.dtype)],
        ),
        cost_estimate=light,
        compiler_params=params(12),
        name="turn",
    )(here, in_hbm(v))


def pack_kernel(line, tokens, routes, codes, out, named, sems):
    tok = tokens.shape[0]
    copies = [
        pltpu.make_async_copy(tokens, out.at[:tok, :], sems.at[0]),
        pltpu.make_async_copy(routes, named.at[0], sems.at[1]),
        pltpu.make_async_copy(codes, named.at[1], sems.at[2]),
    ]
    for c in copies:
        c.start()
    out[tok:, :] = jnp.zeros((8, out.shape[1]), bf16)
    for k, at in enumerate((0, line)):
        copies[1 + k].wait()
        out[tok:, at : at + tok] = named[k].astype(f32).astype(bf16)
    copies[0].wait()


def pack(tokens, routes, codes, line):
    tok, d = tokens.shape
    return pl.pallas_call(
        functools.partial(pack_kernel, line),
        out_shape=jax.ShapeDtypeStruct((tok + 8, d), bf16),
        in_specs=[anywhere] * 3,
        out_specs=on_chip,
        scratch_shapes=[pltpu.VMEM((2, *routes.shape), jnp.int32), pltpu.SemaphoreType.DMA((3,))],
        cost_estimate=light,
        compiler_params=params(8),
        name="pack",
    )(in_hbm(tokens), in_hbm(routes), in_hbm(codes))


def received_kernel(hid, hid_c, own, other, out):
    part = jnp.dot(hid[...], own[...], preferred_element_type=f32)
    part = part + jnp.dot(hid_c[...], other[...], preferred_element_type=f32)
    out[0] = (part * loss_scale).astype(bf16).T


def received_part(hid, hid_c, own, other):
    h = hid.shape[0]
    rows, d = own.shape
    tile = 256
    return pl.pallas_call(
        received_kernel,
        out_shape=jax.ShapeDtypeStruct((1, d, 3 * h), bf16),
        grid=(d // tile,),
        in_specs=[pl.BlockSpec((h, rows), lambda i: (0, 0))] * 2 + [pl.BlockSpec((rows, tile), lambda i: (0, i))] * 2,
        out_specs=pl.BlockSpec((1, tile, h), lambda i: (0, i, 2)),
        cost_estimate=light,
        compiler_params=params(20),
        name="received_part",
    )(hid, hid_c, own, other)


def inputs_kernel(cap, last, here, old, inputs, own, other, late, out, held):
    rows = own.shape[0]

    @pl.when(pl.program_id(0) == 0)
    def _():
        held[...] = other[...]
        held[plane_rows(here[0], *last, cap), :] = late[...]

    part = jnp.dot(inputs[:, :rows], own[...], preferred_element_type=f32)
    part = part + jnp.dot(inputs[:, rows:], held[...], preferred_element_type=f32)
    out[0] = (part * loss_scale).astype(bf16)


def inputs_part(here, last, old, inputs, own, other, late, cap):
    d, slots = inputs.shape
    rows, wide = own.shape
    tile = 256

    def fixed(v):
        return pl.BlockSpec(v.shape, lambda i, here: (0, 0))

    return pl.pallas_call(
        functools.partial(inputs_kernel, cap, last),
        out_shape=jax.ShapeDtypeStruct(old.shape, bf16),
        grid_spec=pltpu.PrefetchScalarGridSpec(
            num_scalar_prefetch=1,
            grid=(d // tile,),
            in_specs=[anywhere, pl.BlockSpec((tile, slots), lambda i, here: (i, 0)), fixed(own), fixed(other), fixed(late)],
            out_specs=pl.BlockSpec((1, tile, wide), lambda i, here: (0, i, 0)),
            scratch_shapes=[pltpu.VMEM((rows, wide), bf16)],
        ),
        input_output_aliases={1: 0},
        cost_estimate=light,
        compiler_params=params(24),
        name="inputs_part",
    )(here, old, inputs, own, other, late)


def together(*values):
    return lax.optimization_barrier(values)


def body_grid(out_grad, routes, gate_codes, w_gate, w_up, w_down, saved_inputs, saved_gate, saved_up):
    owners = lax.axis_size("expert")
    me = lax.axis_index("expert")
    to_core = [(i, i ^ 1) for i in range(owners)]
    to_x = [(i, i ^ 2) for i in range(owners)]
    tok, d = out_grad.shape
    choices = routes.shape[1]
    slots = saved_gate.shape[1]
    cap = slots // owners

    def send(v, perm):
        return lax.ppermute(v, "expert", perm)

    line = 256 * pl.cdiv(tok, 256)
    block = pack(out_grad, routes.T, gate_codes.T, line)
    here = me.reshape(1).astype(jnp.int32)

    def ring(v, hops=1):
        return send(v, [(i, (i + 4 * hops) % owners) for i in range(owners)])

    wd, sg, su = w_down[0], saved_gate[0], saved_up[0]
    wd_c, sg_c, su_c = [send(v, to_core) for v in (wd, sg, su)]

    half = slots // 2
    recs, gps = [], []

    def first(chunk, toks):
        recs[:], (share, *shares, pos) = (lambda a, b, *rest: ([a, b], rest))(
            *dispatch(here, chunk, toks, wd, wd_c, cap, half, recs)
        )
        return (chunk, share, pos), *shares

    def exchange(v):
        return lax.ppermute(v, "dp", [(0, 1), (1, 0)])

    def second(state, *peers, last=False):
        chunk, share, pos = state
        gps[:], sums = (lambda a, b, *rest: ([a, b], rest))(
            *combine(here, chunk, share, peers, pos, (sg, su), (sg_c, su_c), w, w_c, cap, half, gps, last)
        )
        return sums

    r1, x0 = ring(block), send(block, to_x)
    c0, h0 = first([(0, 0)], [block])
    w = join(w_gate[0], w_up[0])
    inputs = turn(here, saved_inputs[0], cap)
    hid = hidden(here, sg, su, cap, 0)
    r1, x0, h0, w, inputs, hid, sg_c, su_c = together(r1, x0, h0, w, inputs, hid, sg_c, su_c)
    r2, x1 = ring(r1), send(r1, to_x)
    h0, w_c = exchange(h0), send(w, to_core)
    c1, h1, g1 = first([(1, 0), (0, 1)], [x0, r1])
    h1 = exchange(h1)
    (t_r0,) = second(c0, h0)
    hid_c = hidden(here, sg, su, cap, 1)
    r2, x1, h1, g1, t_r0, hid_c = together(r2, x1, h1, g1, t_r0, hid_c)
    r3, x2 = ring(r2), send(r2, to_x)
    g1 = exchange(g1)
    c2, h2, g2 = first([(1, 1), (0, 2)], [x1, r2])
    h2 = exchange(h2)
    t_x0, t_r1 = second(c1, h1, g1)
    r3, x2, h2, g2, t_x0, t_r1 = together(r3, x2, h2, g2, t_x0, t_r1)
    x3, w1 = send(r3, to_x), ring(t_r1)
    g2 = exchange(g2)
    c3, h3, g3 = first([(1, 2), (0, 3)], [x2, r3])
    h3 = exchange(h3)
    t_x1, t_r2 = second(c2, h2, g2)
    x3, w1, h3, g3, t_x0, t_x1, t_r2 = together(x3, w1, h3, g3, t_x0, t_x1, t_r2)
    u1, b0 = ring(t_x1), send(t_x0, to_x)
    g3 = exchange(g3)
    c4, h4 = first([(1, 3)], [x3])
    h4 = exchange(h4)
    t_x2, t_r3 = second(c3, h3, g3)
    u1, b0, h4, t_x2, t_r3, rec_away, gp_away = together(u1, b0, h4, t_x2, t_r3, recs[1], gps[1])
    rec_c, gp_c = send(rec_away, to_core), send(gp_away, to_core)
    a0, a1, h4 = together(*add_halves(t_x2, u1), h4)
    b2 = [send(a0, to_x), send(a1, to_x)]
    left, right = second(c4, h4, last=True)
    left, rec_c = together(left, rec_c)
    b3 = [send(left, to_x), send(right, to_x)]
    late = send(gps[1], to_core)
    w2 = [ring(add([t_r2, w1, b2[k]], k)) for k in range(2)]
    part = received_part(hid, hid_c, recs[0], rec_c)
    w2[0], part = together(w2[0], part)
    w3 = [ring(add([t_r3, b3[k], w2[k]], k)) for k in range(2)]
    weight_grads = inputs_part(here, (1, 3), part, inputs, gps[0], gp_c, late, cap)
    w3[1], weight_grads = together(w3[1], weight_grads)
    return (finish(t_r0, b0, *w3), weight_grads)


def solution(mesh):
    placed = (
        P("expert", "dp"),
        P("expert", None),
        P("expert", None),
        P("expert", "dp", None),
        P("expert", "dp", None),
        P("expert", None, "dp"),
        P("expert", None, "dp"),
        P("expert", None, None),
        P("expert", None, None),
    )
    small = mesh.shape["expert"] == 16 and mesh.shape["dp"] == 2
    return jax.shard_map(
        body_grid if small else body_any,
        mesh=mesh,
        in_specs=placed,
        out_specs=(P("expert", "dp"), P("expert", "dp", None)),
        check_vma=False,
    )
```

```python
import functools

import jax
import jax.numpy as jnp
from jax import lax
from jax.experimental import pallas as pl
from jax.experimental.pallas import tpu as pltpu
from jax.sharding import PartitionSpec as P

gate_unit = 0.00390625
loss_scale = 0.015625
f32 = jnp.float32
bf16 = jnp.bfloat16


def contract_rows(left, right):
    return lax.dot_general(left, right, (((0,), (0,)), ((), ())), preferred_element_type=f32)


def contract_cols(left, right):
    return lax.dot_general(left, right, (((1,), (1,)), ((), ())), preferred_element_type=f32)


def activation_grads(grad_hidden, gate_pre, up_pre):
    sigmoid = jax.nn.sigmoid(gate_pre)
    silu = gate_pre * sigmoid
    dsilu = sigmoid * (1.0 + gate_pre * (1.0 - sigmoid))
    grad_gate_pre = (grad_hidden * up_pre * dsilu).astype(bf16)
    grad_up_pre = (grad_hidden * silu).astype(bf16)
    return (grad_gate_pre, grad_up_pre)


def sigmoid_of(x):
    return 0.5 * jnp.tanh(0.5 * x) + 0.5


def kernel_grads(grad_hidden, gate_pre, up_pre):
    sigmoid = sigmoid_of(gate_pre)
    silu = gate_pre * sigmoid
    dsilu = sigmoid + silu * (1.0 - sigmoid)
    return ((grad_hidden * up_pre * dsilu).astype(bf16), (grad_hidden * silu).astype(bf16))


def body_any(out_grad, routes, gate_codes, w_gate, w_up, w_down, saved_inputs, saved_gate, saved_up):
    owners = lax.axis_size("expert")
    slot_count = saved_gate.shape[1]
    capacity = slot_count // owners
    token_count = routes.shape[0]
    choice_count = routes.shape[1]
    flat_routes = routes.reshape(-1)
    onehot = (flat_routes[:, None] == jnp.arange(owners, dtype=jnp.int32)[None, :]).astype(jnp.int32)
    earlier = jnp.cumsum(onehot, axis=0) - onehot
    position = jnp.sum(earlier * onehot, axis=1)
    slot_index = (flat_routes * capacity + position).reshape(token_count, choice_count)
    gate_values = gate_codes.astype(f32) * gate_unit
    rows_iota = jnp.arange(slot_count, dtype=jnp.int32)[:, None]
    weighted = jnp.zeros((slot_count, token_count), f32)
    picks = jnp.zeros((slot_count, token_count), f32)
    for pick in range(choice_count):
        hit = rows_iota == slot_index[:, pick][None, :]
        weighted = weighted + jnp.where(hit, gate_values[:, pick][None, :], 0.0)
        picks = picks + hit.astype(f32)
    outgoing = jnp.dot(weighted.astype(bf16), out_grad, preferred_element_type=f32).astype(bf16)
    received = lax.all_to_all(outgoing, "expert", split_axis=0, concat_axis=0, tiled=True)
    hidden_share = lax.psum_scatter(
        contract_cols(received, w_down[0]), "dp", scatter_dimension=0, tiled=True
    )
    gate_pre = saved_gate[0].astype(f32)
    up_pre = saved_up[0].astype(f32)
    hidden = (gate_pre * jax.nn.sigmoid(gate_pre) * up_pre).astype(bf16)
    grad_hidden = lax.all_gather(hidden_share, "dp", axis=0, tiled=True)
    grad_gate_pre, grad_up_pre = activation_grads(grad_hidden, gate_pre, up_pre)
    slot_grads = contract_cols(grad_gate_pre, w_gate[0]) + contract_cols(grad_up_pre, w_up[0])
    returned = lax.all_to_all(
        slot_grads.astype(bf16), "expert", split_axis=0, concat_axis=0, tiled=True
    )
    token_grads = contract_rows(picks.astype(bf16), returned).astype(bf16)
    inputs_here = saved_inputs[0]
    part = jnp.concatenate(
        [
            contract_rows(inputs_here, grad_gate_pre),
            contract_rows(inputs_here, grad_up_pre),
            contract_rows(received, hidden),
        ],
        axis=1,
    )
    return (token_grads, (part * loss_scale).astype(bf16)[None])


on_chip = pl.BlockSpec(memory_space=pltpu.VMEM)
on_scalar = pl.BlockSpec(memory_space=pltpu.SMEM)
anywhere = pl.BlockSpec(memory_space=pl.ANY)
light = pl.CostEstimate(flops=1 << 20, bytes_accessed=1 << 14, transcendentals=0)


def source(here, step, other):
    group = lax.rem(here // 4 + (4 - step), 4)
    return jnp.bitwise_xor(group * 4 + lax.rem(here, 4), 2 * other)


def params(mib):
    return pltpu.CompilerParams(vmem_limit_bytes=mib << 20)


def plane_rows(here, other, step, cap):
    return pl.ds(pl.multiple_of((source(here, step, other) // 2) * cap, 16), cap)


def dispatch_kernel(chunk, cap, begun, here, *refs):
    n = len(chunk)
    toks, (wd0, wd1) = refs[:n], refs[n : n + 2]
    buf0, buf1, share, *share_out, pos_out, rec, sems = refs[n + 2 + 2 * begun :]
    tok = toks[0].shape[0] - 8
    line = 256 * pl.cdiv(tok, 256)
    before = lax.broadcasted_iota(jnp.int32, (tok, tok), 0) < lax.broadcasted_iota(jnp.int32, (tok, tok), 1)
    before = jnp.where(before, 1.0, 0.0).astype(bf16)
    slot = lax.broadcasted_iota(jnp.int32, (cap, tok), 0).astype(f32)
    masks, gates = [], []
    for a in range(2):
        expert = jnp.bitwise_xor(here[0], a).astype(f32)
        for t in toks:
            hit = t[tok:, :tok].astype(f32) == expert
            masks.append(jnp.max(jnp.where(hit, 1.0, 0.0), axis=0, keepdims=True))
            gates.append(jnp.sum(jnp.where(hit, t[tok:, line : line + tok].astype(f32), 0.0), axis=0, keepdims=True))
    fill = [jnp.zeros((8 - 2 * n, tok), f32)] if n < 4 else []
    mask = jnp.concatenate(masks + fill, axis=0)
    pos = jnp.dot(mask.astype(bf16), before, preferred_element_type=f32)
    pos = jnp.where(mask > 0.0, pos, -1.0)
    pos_out[...] = pos
    copies = []
    for rel, t in enumerate(toks):
        w = [
            jnp.where(slot == pos[i : i + 1, :], gates[i] * gate_unit, 0.0).astype(bf16)
            for i in (rel, n + rel)
        ]
        rows = jnp.dot(jnp.concatenate(w, axis=0), t[:tok, :], preferred_element_type=f32).astype(bf16)
        at = pl.ds(rel * cap, cap)
        for a, buf in enumerate((buf0, buf1)):
            rec[a, at, :] = rows[a * cap : (a + 1) * cap]
            to = plane_rows(here[0], *chunk[rel], cap)
            copies.append(pltpu.make_async_copy(rec.at[a, at, :], buf.at[to, :], sems.at[len(copies)]))
    for c in copies:
        c.start()
    for a, wd in enumerate((wd0, wd1)):
        gh = contract_cols(rec[a], wd[...])
        share[a * n * cap : (a + 1) * n * cap, :] = gh
        if n == 1:
            share_out[0][a * cap : (a + 1) * cap, :] = gh.astype(bf16)
        else:
            share_out[a][...] = gh.astype(bf16)
    for c in copies:
        c.wait()


def dispatch(here, chunk, toks, wd0, wd1, cap, rows, old):
    n = len(toks)
    tok, d = toks[0].shape
    h = wd0.shape[0]
    outs = [((rows, d), bf16)] * 2 + [((2 * n * cap, h), f32)]
    outs += [((2 * cap, h), bf16)] if n == 1 else [((n * cap, h), bf16)] * 2
    outs += [((8, tok - 8), f32)]
    return pl.pallas_call(
        functools.partial(dispatch_kernel, chunk, cap, len(old) // 2),
        out_shape=[jax.ShapeDtypeStruct(s, t) for s, t in outs],
        in_specs=[on_scalar] + [on_chip] * (n + 2) + [anywhere] * len(old),
        out_specs=[anywhere] * 2 + [on_chip] * (len(outs) - 2),
        scratch_shapes=[pltpu.VMEM((2, n * cap, d), bf16), pltpu.SemaphoreType.DMA((2 * n,))],
        input_output_aliases={n + 3 + k: k for k in range(len(old))},
        cost_estimate=light,
        compiler_params=params(16),
        name="dispatch",
    )(here, *toks, wd0, wd1, *old)


def combine_kernel(chunk, cap, begun, last, here, share, *refs):
    n = len(chunk)
    if n == 1:
        peer0, peer1 = refs[0].at[:cap, :], refs[0].at[cap:, :]
        pos, *refs = refs[1:]
    else:
        peer0, peer1, pos, *refs = refs
    saved, ws, refs = refs[:4], refs[4:6], refs[6 + begun :]
    buffers, backs, (gps, out_sems) = refs[:2], refs[2:-2], refs[-2:]
    h = share.shape[1]
    slot = lax.broadcasted_iota(jnp.int32, (cap, pos.shape[1]), 0).astype(f32)
    leaving = []
    for a, peer in enumerate((peer0, peer1)):
        for rel in range(n):
            i = a * n + rel
            at = slice(rel * cap, (rel + 1) * cap)
            gh = share[i * cap : (i + 1) * cap, :] + peer[at, :].astype(f32)
            other, step = chunk[rel]
            own = pl.ds(pl.multiple_of(source(here[0], step, other) * cap, 16), cap)
            gg, gu = kernel_grads(gh, saved[2 * a][own, :].astype(f32), saved[2 * a + 1][own, :].astype(f32))
            gps[a, at, :h] = gg
            gps[a, at, h:] = gu
            if a == 0 or not last:
                to = buffers[a].at[plane_rows(here[0], *chunk[rel], cap), :]
                leaving.append(pltpu.make_async_copy(gps.at[a, at, :], to, out_sems.at[i]))
    for c in leaving:
        c.start()
    if last:
        buffers[1][...] = gps[1]
    sums = [None] * n
    for a, w in enumerate(ws):
        slots = contract_cols(gps[a], w[...]).astype(bf16)
        for rel in range(n):
            i = a * n + rel
            pick = jnp.where(slot == pos[i : i + 1, :], 1.0, 0.0).astype(bf16)
            part = contract_rows(pick, slots[rel * cap : (rel + 1) * cap])
            sums[rel] = part if sums[rel] is None else sums[rel] + part
    if len(backs) > n:
        half = backs[0].shape[1]
        for k, back in enumerate(backs):
            back[...] = sums[0][:, k * half : (k + 1) * half].astype(bf16)
    else:
        for rel in range(n):
            backs[rel][...] = sums[rel].astype(bf16)
    for c in leaving:
        c.wait()


def combine(here, chunk, share, peers, pos, saved0, saved1, w0, w1, cap, rows, old, last=False):
    n = len(chunk)
    h = share.shape[1]
    d = w0.shape[0]
    tok = pos.shape[1]
    old = old[:1] if last else old
    outs = [(rows, 2 * h), (n * cap if last else rows, 2 * h)] + ([(tok, d // 2)] * 2 if last else [(tok, d)] * n)
    first_old = 2 + len(peers) + 1 + 4 + 2
    return pl.pallas_call(
        functools.partial(combine_kernel, chunk, cap, len(old), last),
        out_shape=[jax.ShapeDtypeStruct(s, bf16) for s in outs],
        in_specs=[on_scalar] + [on_chip] * (2 + len(peers) + 6) + [anywhere] * len(old),
        out_specs=[anywhere, on_chip if last else anywhere] + [on_chip] * (len(outs) - 2),
        scratch_shapes=[
            pltpu.VMEM((2, n * cap, 2 * h), bf16),
            pltpu.SemaphoreType.DMA((2 * n,)),
        ],
        input_output_aliases={first_old + k: k for k in range(len(old))},
        cost_estimate=light,
        compiler_params=params(20),
        name="combine",
    )(here, share, *peers, pos, *saved0, *saved1, w0, w1, *old)


def join_kernel(left, right, out):
    out[:, : left.shape[1]] = left[...]
    out[:, left.shape[1] :] = right[...]


def join(left, right):
    rows, h = left.shape
    return pl.pallas_call(
        join_kernel,
        out_shape=jax.ShapeDtypeStruct((rows, 2 * h), left.dtype),
        in_specs=[on_chip] * 2,
        out_specs=on_chip,
        cost_estimate=light,
        compiler_params=params(8),
        name="join",
    )(left, right)


def add_kernel(part, *refs):
    wide = refs[-1].shape[1]
    total = None
    for r in refs[:-1]:
        v = r[...] if part is None or r.shape[1] == wide else r[:, part * wide : (part + 1) * wide]
        total = v.astype(f32) if total is None else total + v.astype(f32)
    refs[-1][...] = total.astype(bf16)


def add(values, part=None):
    rows, wide = values[0].shape
    return pl.pallas_call(
        functools.partial(add_kernel, part),
        out_shape=jax.ShapeDtypeStruct((rows, wide if part is None else wide // 2), bf16),
        in_specs=[on_chip] * len(values),
        out_specs=on_chip,
        cost_estimate=light,
        compiler_params=params(8),
        name="add",
    )(*values)


def add_halves_kernel(a, b, left, right):
    total = (a[...].astype(f32) + b[...].astype(f32)).astype(bf16)
    left[...] = total[:, : left.shape[1]]
    right[...] = total[:, left.shape[1] :]


def add_halves(a, b):
    rows, wide = a.shape
    return pl.pallas_call(
        add_halves_kernel,
        out_shape=[jax.ShapeDtypeStruct((rows, wide // 2), bf16)] * 2,
        in_specs=[on_chip] * 2,
        out_specs=[on_chip] * 2,
        cost_estimate=light,
        compiler_params=params(8),
        name="add_halves",
    )(a, b)


def finish_kernel(a, b, left, right, out):
    half = left.shape[1]
    for at, v in ((0, left), (half, right)):
        total = a[:, at : at + half].astype(f32) + b[:, at : at + half].astype(f32) + v[...].astype(f32)
        out[:, at : at + half] = total.astype(bf16)


def finish(a, b, left, right):
    return pl.pallas_call(
        finish_kernel,
        out_shape=jax.ShapeDtypeStruct(a.shape, bf16),
        in_specs=[on_chip] * 4,
        out_specs=on_chip,
        cost_estimate=light,
        compiler_params=params(8),
        name="finish",
    )(a, b, left, right)


def in_hbm(v):
    return pltpu.with_memory_space_constraint(v, pltpu.HBM)


def hidden_kernel(cap, k, here, gate, up, out, held, sems):
    plane = lax.rem(here[0] + k, 2)
    copies = []
    for i, v in enumerate((gate, up)):
        for q in range(held.shape[1] // cap):
            at = pl.ds(pl.multiple_of((2 * q + plane) * cap, 16), cap)
            to = held.at[i, pl.ds(q * cap, cap), :]
            copies.append(pltpu.make_async_copy(v.at[at, :], to, sems.at[len(copies)]))
    for c in copies:
        c.start()
    for c in copies:
        c.wait()
    gate_pre = held[0].astype(f32)
    out[...] = (gate_pre * sigmoid_of(gate_pre) * held[1].astype(f32)).astype(bf16).T


def hidden(here, gate, up, cap, k):
    slots, h = gate.shape
    return pl.pallas_call(
        functools.partial(hidden_kernel, cap, k),
        out_shape=jax.ShapeDtypeStruct((h, slots // 2), bf16),
        in_specs=[on_scalar, anywhere, anywhere],
        out_specs=on_chip,
        scratch_shapes=[pltpu.VMEM((2, slots // 2, h), bf16), pltpu.SemaphoreType.DMA((slots // cap,))],
        cost_estimate=light,
        compiler_params=params(16),
        name="hidden",
    )(here, in_hbm(gate), in_hbm(up))


def turn_kernel(cap, here, v, out, held):
    rows = held.shape[0]
    for k in range(2):
        plane = lax.rem(here[0] + k, 2)
        for q in range(rows // cap):
            held[q * cap : (q + 1) * cap, :] = v[pl.ds(pl.multiple_of((2 * q + plane) * cap, 16), cap), :]
        out[:, k * rows : (k + 1) * rows] = held[...].T


def turn(here, v, cap):
    slots, d = v.shape
    tile = 256
    return pl.pallas_call(
        functools.partial(turn_kernel, cap),
        out_shape=jax.ShapeDtypeStruct((d, slots), v.dtype),
        grid_spec=pltpu.PrefetchScalarGridSpec(
            num_scalar_prefetch=1,
            grid=(d // tile,),
            in_specs=[pl.BlockSpec((slots, tile), lambda i, here: (0, i))],
            out_specs=pl.BlockSpec((tile, slots), lambda i, here: (i, 0)),
            scratch_shapes=[pltpu.VMEM((slots // 2, tile), v.dtype)],
        ),
        cost_estimate=light,
        compiler_params=params(12),
        name="turn",
    )(here, in_hbm(v))


def pack_kernel(line, tokens, routes, codes, out, named, sems):
    tok = tokens.shape[0]
    copies = [
        pltpu.make_async_copy(tokens, out.at[:tok, :], sems.at[0]),
        pltpu.make_async_copy(routes, named.at[0], sems.at[1]),
        pltpu.make_async_copy(codes, named.at[1], sems.at[2]),
    ]
    for c in copies:
        c.start()
    out[tok:, :] = jnp.zeros((8, out.shape[1]), bf16)
    for k, at in enumerate((0, line)):
        copies[1 + k].wait()
        out[tok:, at : at + tok] = named[k].astype(f32).astype(bf16)
    copies[0].wait()


def pack(tokens, routes, codes, line):
    tok, d = tokens.shape
    return pl.pallas_call(
        functools.partial(pack_kernel, line),
        out_shape=jax.ShapeDtypeStruct((tok + 8, d), bf16),
        in_specs=[anywhere] * 3,
        out_specs=on_chip,
        scratch_shapes=[pltpu.VMEM((2, *routes.shape), jnp.int32), pltpu.SemaphoreType.DMA((3,))],
        cost_estimate=light,
        compiler_params=params(8),
        name="pack",
    )(in_hbm(tokens), in_hbm(routes), in_hbm(codes))


def received_own_kernel(hid, own, out):
    out[...] = jnp.dot(hid[...], own[...], preferred_element_type=f32)


def received_other_kernel(part, hid, other, out):
    total = part[...] + jnp.dot(hid[...], other[...], preferred_element_type=f32)
    out[0] = (total * loss_scale).astype(bf16).T


def received_own(hid, own):
    h = hid.shape[0]
    rows, d = own.shape
    tile = 256
    return pl.pallas_call(
        received_own_kernel,
        out_shape=jax.ShapeDtypeStruct((h, d), f32),
        grid=(d // tile,),
        in_specs=[pl.BlockSpec((h, rows), lambda i: (0, 0)), pl.BlockSpec((rows, tile), lambda i: (0, i))],
        out_specs=pl.BlockSpec((h, tile), lambda i: (0, i)),
        cost_estimate=light,
        compiler_params=params(16),
        name="received_own",
    )(hid, own)


def received_other(part, hid, other):
    h, d = part.shape
    rows = other.shape[0]
    tile = 256
    return pl.pallas_call(
        received_other_kernel,
        out_shape=jax.ShapeDtypeStruct((1, d, 3 * h), bf16),
        grid=(d // tile,),
        in_specs=[
            pl.BlockSpec((h, tile), lambda i: (0, i)),
            pl.BlockSpec((h, rows), lambda i: (0, 0)),
            pl.BlockSpec((rows, tile), lambda i: (0, i)),
        ],
        out_specs=pl.BlockSpec((1, tile, h), lambda i: (0, i, 2)),
        cost_estimate=light,
        compiler_params=params(16),
        name="received_other",
    )(part, hid, other)


def inputs_kernel(cap, last, here, old, inputs, own, other, late, out, held):
    rows = own.shape[0]

    @pl.when(pl.program_id(0) == 0)
    def _():
        held[...] = other[...]
        held[plane_rows(here[0], *last, cap), :] = late[...]

    part = jnp.dot(inputs[:, :rows], own[...], preferred_element_type=f32)
    part = part + jnp.dot(inputs[:, rows:], held[...], preferred_element_type=f32)
    out[0] = (part * loss_scale).astype(bf16)


def inputs_part(here, last, old, inputs, own, other, late, cap):
    d, slots = inputs.shape
    rows, wide = own.shape
    tile = 256

    def fixed(v):
        return pl.BlockSpec(v.shape, lambda i, here: (0, 0))

    return pl.pallas_call(
        functools.partial(inputs_kernel, cap, last),
        out_shape=jax.ShapeDtypeStruct(old.shape, bf16),
        grid_spec=pltpu.PrefetchScalarGridSpec(
            num_scalar_prefetch=1,
            grid=(d // tile,),
            in_specs=[anywhere, pl.BlockSpec((tile, slots), lambda i, here: (i, 0)), fixed(own), fixed(other), fixed(late)],
            out_specs=pl.BlockSpec((1, tile, wide), lambda i, here: (0, i, 0)),
            scratch_shapes=[pltpu.VMEM((rows, wide), bf16)],
        ),
        input_output_aliases={1: 0},
        cost_estimate=light,
        compiler_params=params(24),
        name="inputs_part",
    )(here, old, inputs, own, other, late)


def together(*values):
    return lax.optimization_barrier(values)


def body_grid(out_grad, routes, gate_codes, w_gate, w_up, w_down, saved_inputs, saved_gate, saved_up):
    owners = lax.axis_size("expert")
    me = lax.axis_index("expert")
    to_core = [(i, i ^ 1) for i in range(owners)]
    to_x = [(i, i ^ 2) for i in range(owners)]
    tok, d = out_grad.shape
    choices = routes.shape[1]
    slots = saved_gate.shape[1]
    cap = slots // owners

    def send(v, perm):
        return lax.ppermute(v, "expert", perm)

    line = 256 * pl.cdiv(tok, 256)
    block = pack(out_grad, routes.T, gate_codes.T, line)
    here = me.reshape(1).astype(jnp.int32)

    def ring(v, hops=1):
        return send(v, [(i, (i + 4 * hops) % owners) for i in range(owners)])

    wd, sg, su = w_down[0], saved_gate[0], saved_up[0]
    wd_c, sg_c, su_c = [send(v, to_core) for v in (wd, sg, su)]

    half = slots // 2
    recs, gps = [], []

    def first(chunk, toks):
        recs[:], (share, *shares, pos) = (lambda a, b, *rest: ([a, b], rest))(
            *dispatch(here, chunk, toks, wd, wd_c, cap, half, recs)
        )
        return (chunk, share, pos), *shares

    def exchange(v):
        return lax.ppermute(v, "dp", [(0, 1), (1, 0)])

    def second(state, *peers, last=False):
        chunk, share, pos = state
        gps[:], sums = (lambda a, b, *rest: ([a, b], rest))(
            *combine(here, chunk, share, peers, pos, (sg, su), (sg_c, su_c), w, w_c, cap, half, gps, last)
        )
        return sums

    r1, x0 = ring(block), send(block, to_x)
    c0, h0 = first([(0, 0)], [block])
    w = join(w_gate[0], w_up[0])
    inputs = turn(here, saved_inputs[0], cap)
    hid = hidden(here, sg, su, cap, 0)
    r1, x0, h0, w, inputs, hid, sg_c, su_c = together(r1, x0, h0, w, inputs, hid, sg_c, su_c)
    r2, x1 = ring(r1), send(r1, to_x)
    h0, w_c = exchange(h0), send(w, to_core)
    c1, h1, g1 = first([(1, 0), (0, 1)], [x0, r1])
    h1 = exchange(h1)
    (t_r0,) = second(c0, h0)
    hid_c = hidden(here, sg, su, cap, 1)
    r2, x1, h1, g1, t_r0, hid_c = together(r2, x1, h1, g1, t_r0, hid_c)
    r3, x2 = ring(r2), send(r2, to_x)
    g1 = exchange(g1)
    c2, h2, g2 = first([(1, 1), (0, 2)], [x1, r2])
    h2 = exchange(h2)
    t_x0, t_r1 = second(c1, h1, g1)
    r3, x2, h2, g2, t_x0, t_r1 = together(r3, x2, h2, g2, t_x0, t_r1)
    x3, w1 = send(r3, to_x), ring(t_r1)
    g2 = exchange(g2)
    c3, h3, g3 = first([(1, 2), (0, 3)], [x2, r3])
    h3 = exchange(h3)
    t_x1, t_r2 = second(c2, h2, g2)
    x3, w1, h3, g3, t_x0, t_x1, t_r2 = together(x3, w1, h3, g3, t_x0, t_x1, t_r2)
    u1, b0 = ring(t_x1), send(t_x0, to_x)
    g3 = exchange(g3)
    c4, h4 = first([(1, 3)], [x3])
    h4 = exchange(h4)
    t_x2, t_r3 = second(c3, h3, g3)
    u1, b0, h4, t_x2, t_r3, rec_away, gp_away = together(u1, b0, h4, t_x2, t_r3, recs[1], gps[1])
    rec_c, gp_c = send(rec_away, to_core), send(gp_away, to_core)
    a0, a1, h4 = together(*add_halves(t_x2, u1), h4)
    b2 = [send(a0, to_x), send(a1, to_x)]
    left, right = second(c4, h4, last=True)
    b3 = [send(left, to_x), send(right, to_x)]
    late = send(gps[1], to_core)
    part = received_own(hid, recs[0])
    b2[1], part, rec_c = together(b2[1], part, rec_c)
    w2 = [ring(add([t_r2, w1, b2[k]], k)) for k in range(2)]
    part = received_other(part, hid_c, rec_c)
    w2[0], part = together(w2[0], part)
    w3 = [ring(add([t_r3, b3[k], w2[k]], k)) for k in range(2)]
    weight_grads = inputs_part(here, (1, 3), part, inputs, gps[0], gp_c, late, cap)
    w3[1], weight_grads = together(w3[1], weight_grads)
    return (finish(t_r0, b0, *w3), weight_grads)


def solution(mesh):
    placed = (
        P("expert", "dp"),
        P("expert", None),
        P("expert", None),
        P("expert", "dp", None),
        P("expert", "dp", None),
        P("expert", None, "dp"),
        P("expert", None, "dp"),
        P("expert", None, None),
        P("expert", None, None),
    )
    small = mesh.shape["expert"] == 16 and mesh.shape["dp"] == 2
    return jax.shard_map(
        body_grid if small else body_any,
        mesh=mesh,
        in_specs=placed,
        out_specs=(P("expert", "dp"), P("expert", "dp", None)),
        check_vma=False,
    )
```

```python
import functools

import jax
import jax.numpy as jnp
from jax import lax
from jax.experimental import pallas as pl
from jax.experimental.pallas import tpu as pltpu
from jax.sharding import PartitionSpec as P

gate_unit = 0.00390625
loss_scale = 0.015625
f32 = jnp.float32
bf16 = jnp.bfloat16


def contract_rows(left, right):
    return lax.dot_general(left, right, (((0,), (0,)), ((), ())), preferred_element_type=f32)


def contract_cols(left, right):
    return lax.dot_general(left, right, (((1,), (1,)), ((), ())), preferred_element_type=f32)


def activation_grads(grad_hidden, gate_pre, up_pre):
    sigmoid = jax.nn.sigmoid(gate_pre)
    silu = gate_pre * sigmoid
    dsilu = sigmoid * (1.0 + gate_pre * (1.0 - sigmoid))
    grad_gate_pre = (grad_hidden * up_pre * dsilu).astype(bf16)
    grad_up_pre = (grad_hidden * silu).astype(bf16)
    return (grad_gate_pre, grad_up_pre)


def sigmoid_of(x):
    return 0.5 * jnp.tanh(0.5 * x) + 0.5


def kernel_grads(grad_hidden, gate_pre, up_pre):
    sigmoid = sigmoid_of(gate_pre)
    silu = gate_pre * sigmoid
    dsilu = sigmoid + silu * (1.0 - sigmoid)
    return ((grad_hidden * up_pre * dsilu).astype(bf16), (grad_hidden * silu).astype(bf16))


def body_any(out_grad, routes, gate_codes, w_gate, w_up, w_down, saved_inputs, saved_gate, saved_up):
    owners = lax.axis_size("expert")
    slot_count = saved_gate.shape[1]
    capacity = slot_count // owners
    token_count = routes.shape[0]
    choice_count = routes.shape[1]
    flat_routes = routes.reshape(-1)
    onehot = (flat_routes[:, None] == jnp.arange(owners, dtype=jnp.int32)[None, :]).astype(jnp.int32)
    earlier = jnp.cumsum(onehot, axis=0) - onehot
    position = jnp.sum(earlier * onehot, axis=1)
    slot_index = (flat_routes * capacity + position).reshape(token_count, choice_count)
    gate_values = gate_codes.astype(f32) * gate_unit
    rows_iota = jnp.arange(slot_count, dtype=jnp.int32)[:, None]
    weighted = jnp.zeros((slot_count, token_count), f32)
    picks = jnp.zeros((slot_count, token_count), f32)
    for pick in range(choice_count):
        hit = rows_iota == slot_index[:, pick][None, :]
        weighted = weighted + jnp.where(hit, gate_values[:, pick][None, :], 0.0)
        picks = picks + hit.astype(f32)
    outgoing = jnp.dot(weighted.astype(bf16), out_grad, preferred_element_type=f32).astype(bf16)
    received = lax.all_to_all(outgoing, "expert", split_axis=0, concat_axis=0, tiled=True)
    hidden_share = lax.psum_scatter(
        contract_cols(received, w_down[0]), "dp", scatter_dimension=0, tiled=True
    )
    gate_pre = saved_gate[0].astype(f32)
    up_pre = saved_up[0].astype(f32)
    hidden = (gate_pre * jax.nn.sigmoid(gate_pre) * up_pre).astype(bf16)
    grad_hidden = lax.all_gather(hidden_share, "dp", axis=0, tiled=True)
    grad_gate_pre, grad_up_pre = activation_grads(grad_hidden, gate_pre, up_pre)
    slot_grads = contract_cols(grad_gate_pre, w_gate[0]) + contract_cols(grad_up_pre, w_up[0])
    returned = lax.all_to_all(
        slot_grads.astype(bf16), "expert", split_axis=0, concat_axis=0, tiled=True
    )
    token_grads = contract_rows(picks.astype(bf16), returned).astype(bf16)
    inputs_here = saved_inputs[0]
    part = jnp.concatenate(
        [
            contract_rows(inputs_here, grad_gate_pre),
            contract_rows(inputs_here, grad_up_pre),
            contract_rows(received, hidden),
        ],
        axis=1,
    )
    return (token_grads, (part * loss_scale).astype(bf16)[None])


on_chip = pl.BlockSpec(memory_space=pltpu.VMEM)
on_scalar = pl.BlockSpec(memory_space=pltpu.SMEM)
anywhere = pl.BlockSpec(memory_space=pl.ANY)
light = pl.CostEstimate(flops=1 << 20, bytes_accessed=1 << 14, transcendentals=0)


def source(here, step, other):
    group = lax.rem(here // 4 + (4 - step), 4)
    return jnp.bitwise_xor(group * 4 + lax.rem(here, 4), 2 * other)


def params(mib):
    return pltpu.CompilerParams(vmem_limit_bytes=mib << 20)


def plane_rows(here, other, step, cap):
    return pl.ds(pl.multiple_of((source(here, step, other) // 2) * cap, 16), cap)


def dispatch_kernel(chunk, cap, begun, here, *refs):
    n = len(chunk)
    toks, (wd0, wd1) = refs[:n], refs[n : n + 2]
    buf0, buf1, share, *share_out, pos_out, rec, sems = refs[n + 2 + 2 * begun :]
    tok = toks[0].shape[0] - 8
    line = 256 * pl.cdiv(tok, 256)
    before = lax.broadcasted_iota(jnp.int32, (tok, tok), 0) < lax.broadcasted_iota(jnp.int32, (tok, tok), 1)
    before = jnp.where(before, 1.0, 0.0).astype(bf16)
    slot = lax.broadcasted_iota(jnp.int32, (cap, tok), 0).astype(f32)
    masks, gates = [], []
    for a in range(2):
        expert = jnp.bitwise_xor(here[0], a).astype(f32)
        for t in toks:
            hit = t[tok:, :tok].astype(f32) == expert
            masks.append(jnp.max(jnp.where(hit, 1.0, 0.0), axis=0, keepdims=True))
            gates.append(jnp.sum(jnp.where(hit, t[tok:, line : line + tok].astype(f32), 0.0), axis=0, keepdims=True))
    fill = [jnp.zeros((8 - 2 * n, tok), f32)] if n < 4 else []
    mask = jnp.concatenate(masks + fill, axis=0)
    pos = jnp.dot(mask.astype(bf16), before, preferred_element_type=f32)
    pos = jnp.where(mask > 0.0, pos, -1.0)
    pos_out[...] = pos
    copies = []
    for rel, t in enumerate(toks):
        w = [
            jnp.where(slot == pos[i : i + 1, :], gates[i] * gate_unit, 0.0).astype(bf16)
            for i in (rel, n + rel)
        ]
        rows = jnp.dot(jnp.concatenate(w, axis=0), t[:tok, :], preferred_element_type=f32).astype(bf16)
        at = pl.ds(rel * cap, cap)
        for a, buf in enumerate((buf0, buf1)):
            rec[a, at, :] = rows[a * cap : (a + 1) * cap]
            to = plane_rows(here[0], *chunk[rel], cap)
            copies.append(pltpu.make_async_copy(rec.at[a, at, :], buf.at[to, :], sems.at[len(copies)]))
    for c in copies:
        c.start()
    for a, wd in enumerate((wd0, wd1)):
        gh = contract_cols(rec[a], wd[...])
        share[a * n * cap : (a + 1) * n * cap, :] = gh
        if n == 1:
            share_out[0][a * cap : (a + 1) * cap, :] = gh.astype(bf16)
        else:
            share_out[a][...] = gh.astype(bf16)
    for c in copies:
        c.wait()


def dispatch(here, chunk, toks, wd0, wd1, cap, rows, old):
    n = len(toks)
    tok, d = toks[0].shape
    h = wd0.shape[0]
    outs = [((rows, d), bf16)] * 2 + [((2 * n * cap, h), f32)]
    outs += [((2 * cap, h), bf16)] if n == 1 else [((n * cap, h), bf16)] * 2
    outs += [((8, tok - 8), f32)]
    return pl.pallas_call(
        functools.partial(dispatch_kernel, chunk, cap, len(old) // 2),
        out_shape=[jax.ShapeDtypeStruct(s, t) for s, t in outs],
        in_specs=[on_scalar] + [on_chip] * (n + 2) + [anywhere] * len(old),
        out_specs=[anywhere] * 2 + [on_chip] * (len(outs) - 2),
        scratch_shapes=[pltpu.VMEM((2, n * cap, d), bf16), pltpu.SemaphoreType.DMA((2 * n,))],
        input_output_aliases={n + 3 + k: k for k in range(len(old))},
        cost_estimate=light,
        compiler_params=params(16),
        name="dispatch",
    )(here, *toks, wd0, wd1, *old)


def combine_kernel(chunk, cap, begun, last, here, share, *refs):
    n = len(chunk)
    if n == 1:
        peer0, peer1 = refs[0].at[:cap, :], refs[0].at[cap:, :]
        pos, *refs = refs[1:]
    else:
        peer0, peer1, pos, *refs = refs
    saved, ws, refs = refs[:4], refs[4:6], refs[6 + begun :]
    buffers, backs, (gps, out_sems) = refs[:2], refs[2:-2], refs[-2:]
    h = share.shape[1]
    slot = lax.broadcasted_iota(jnp.int32, (cap, pos.shape[1]), 0).astype(f32)
    leaving = []
    for a, peer in enumerate((peer0, peer1)):
        for rel in range(n):
            i = a * n + rel
            at = slice(rel * cap, (rel + 1) * cap)
            gh = share[i * cap : (i + 1) * cap, :] + peer[at, :].astype(f32)
            other, step = chunk[rel]
            own = pl.ds(pl.multiple_of(source(here[0], step, other) * cap, 16), cap)
            gg, gu = kernel_grads(gh, saved[2 * a][own, :].astype(f32), saved[2 * a + 1][own, :].astype(f32))
            gps[a, at, :h] = gg
            gps[a, at, h:] = gu
            if a == 0 or not last:
                to = buffers[a].at[plane_rows(here[0], *chunk[rel], cap), :]
                leaving.append(pltpu.make_async_copy(gps.at[a, at, :], to, out_sems.at[i]))
    for c in leaving:
        c.start()
    if last:
        buffers[1][...] = gps[1]
    sums = [None] * n
    for a, w in enumerate(ws):
        slots = contract_cols(gps[a], w[...]).astype(bf16)
        for rel in range(n):
            i = a * n + rel
            pick = jnp.where(slot == pos[i : i + 1, :], 1.0, 0.0).astype(bf16)
            part = contract_rows(pick, slots[rel * cap : (rel + 1) * cap])
            sums[rel] = part if sums[rel] is None else sums[rel] + part
    if len(backs) > n:
        half = backs[0].shape[1]
        for k, back in enumerate(backs):
            back[...] = sums[0][:, k * half : (k + 1) * half].astype(bf16)
    else:
        for rel in range(n):
            backs[rel][...] = sums[rel].astype(bf16)
    for c in leaving:
        c.wait()


def combine(here, chunk, share, peers, pos, saved0, saved1, w0, w1, cap, rows, old, last=False):
    n = len(chunk)
    h = share.shape[1]
    d = w0.shape[0]
    tok = pos.shape[1]
    old = old[:1] if last else old
    outs = [(rows, 2 * h), (n * cap if last else rows, 2 * h)] + ([(tok, d // 2)] * 2 if last else [(tok, d)] * n)
    first_old = 2 + len(peers) + 1 + 4 + 2
    return pl.pallas_call(
        functools.partial(combine_kernel, chunk, cap, len(old), last),
        out_shape=[jax.ShapeDtypeStruct(s, bf16) for s in outs],
        in_specs=[on_scalar] + [on_chip] * (2 + len(peers) + 6) + [anywhere] * len(old),
        out_specs=[anywhere, on_chip if last else anywhere] + [on_chip] * (len(outs) - 2),
        scratch_shapes=[
            pltpu.VMEM((2, n * cap, 2 * h), bf16),
            pltpu.SemaphoreType.DMA((2 * n,)),
        ],
        input_output_aliases={first_old + k: k for k in range(len(old))},
        cost_estimate=light,
        compiler_params=params(20),
        name="combine",
    )(here, share, *peers, pos, *saved0, *saved1, w0, w1, *old)


def join_kernel(left, right, out):
    out[:, : left.shape[1]] = left[...]
    out[:, left.shape[1] :] = right[...]


def join(left, right):
    rows, h = left.shape
    return pl.pallas_call(
        join_kernel,
        out_shape=jax.ShapeDtypeStruct((rows, 2 * h), left.dtype),
        in_specs=[on_chip] * 2,
        out_specs=on_chip,
        cost_estimate=light,
        compiler_params=params(8),
        name="join",
    )(left, right)


def add_kernel(part, *refs):
    wide = refs[-1].shape[1]
    total = None
    for r in refs[:-1]:
        v = r[...] if part is None or r.shape[1] == wide else r[:, part * wide : (part + 1) * wide]
        total = v.astype(f32) if total is None else total + v.astype(f32)
    refs[-1][...] = total.astype(bf16)


def add(values, part=None):
    rows, wide = values[0].shape
    return pl.pallas_call(
        functools.partial(add_kernel, part),
        out_shape=jax.ShapeDtypeStruct((rows, wide if part is None else wide // 2), bf16),
        in_specs=[on_chip] * len(values),
        out_specs=on_chip,
        cost_estimate=light,
        compiler_params=params(8),
        name="add",
    )(*values)


def add_halves_kernel(a, b, left, right):
    total = (a[...].astype(f32) + b[...].astype(f32)).astype(bf16)
    left[...] = total[:, : left.shape[1]]
    right[...] = total[:, left.shape[1] :]


def add_halves(a, b):
    rows, wide = a.shape
    return pl.pallas_call(
        add_halves_kernel,
        out_shape=[jax.ShapeDtypeStruct((rows, wide // 2), bf16)] * 2,
        in_specs=[on_chip] * 2,
        out_specs=[on_chip] * 2,
        cost_estimate=light,
        compiler_params=params(8),
        name="add_halves",
    )(a, b)


def finish_kernel(a, b, left, right, out):
    half = left.shape[1]
    for at, v in ((0, left), (half, right)):
        total = a[:, at : at + half].astype(f32) + b[:, at : at + half].astype(f32) + v[...].astype(f32)
        out[:, at : at + half] = total.astype(bf16)


def finish(a, b, left, right):
    return pl.pallas_call(
        finish_kernel,
        out_shape=jax.ShapeDtypeStruct(a.shape, bf16),
        in_specs=[on_chip] * 4,
        out_specs=on_chip,
        cost_estimate=light,
        compiler_params=params(8),
        name="finish",
    )(a, b, left, right)


def in_hbm(v):
    return pltpu.with_memory_space_constraint(v, pltpu.HBM)


def hidden_kernel(cap, k, here, gate, up, out, held, sems):
    plane = lax.rem(here[0] + k, 2)
    copies = []
    for i, v in enumerate((gate, up)):
        for q in range(held.shape[1] // cap):
            at = pl.ds(pl.multiple_of((2 * q + plane) * cap, 16), cap)
            to = held.at[i, pl.ds(q * cap, cap), :]
            copies.append(pltpu.make_async_copy(v.at[at, :], to, sems.at[len(copies)]))
    for c in copies:
        c.start()
    for c in copies:
        c.wait()
    gate_pre = held[0].astype(f32)
    out[...] = (gate_pre * sigmoid_of(gate_pre) * held[1].astype(f32)).astype(bf16).T


def hidden(here, gate, up, cap, k):
    slots, h = gate.shape
    return pl.pallas_call(
        functools.partial(hidden_kernel, cap, k),
        out_shape=jax.ShapeDtypeStruct((h, slots // 2), bf16),
        in_specs=[on_scalar, anywhere, anywhere],
        out_specs=on_chip,
        scratch_shapes=[pltpu.VMEM((2, slots // 2, h), bf16), pltpu.SemaphoreType.DMA((slots // cap,))],
        cost_estimate=light,
        compiler_params=params(16),
        name="hidden",
    )(here, in_hbm(gate), in_hbm(up))


def turn_kernel(cap, here, v, out, held):
    rows = held.shape[0]
    for k in range(2):
        plane = lax.rem(here[0] + k, 2)
        for q in range(rows // cap):
            held[q * cap : (q + 1) * cap, :] = v[pl.ds(pl.multiple_of((2 * q + plane) * cap, 16), cap), :]
        out[:, k * rows : (k + 1) * rows] = held[...].T


def turn(here, v, cap):
    slots, d = v.shape
    tile = 256
    return pl.pallas_call(
        functools.partial(turn_kernel, cap),
        out_shape=jax.ShapeDtypeStruct((d, slots), v.dtype),
        grid_spec=pltpu.PrefetchScalarGridSpec(
            num_scalar_prefetch=1,
            grid=(d // tile,),
            in_specs=[pl.BlockSpec((slots, tile), lambda i, here: (0, i))],
            out_specs=pl.BlockSpec((tile, slots), lambda i, here: (i, 0)),
            scratch_shapes=[pltpu.VMEM((slots // 2, tile), v.dtype)],
        ),
        cost_estimate=light,
        compiler_params=params(12),
        name="turn",
    )(here, in_hbm(v))


def pack_kernel(line, tokens, routes, codes, out, named, sems):
    tok = tokens.shape[0]
    copies = [
        pltpu.make_async_copy(tokens, out.at[:tok, :], sems.at[0]),
        pltpu.make_async_copy(routes, named.at[0], sems.at[1]),
        pltpu.make_async_copy(codes, named.at[1], sems.at[2]),
    ]
    for c in copies:
        c.start()
    out[tok:, :] = jnp.zeros((8, out.shape[1]), bf16)
    for k, at in enumerate((0, line)):
        copies[1 + k].wait()
        out[tok:, at : at + tok] = named[k].astype(f32).astype(bf16)
    copies[0].wait()


def pack(tokens, routes, codes, line):
    tok, d = tokens.shape
    return pl.pallas_call(
        functools.partial(pack_kernel, line),
        out_shape=jax.ShapeDtypeStruct((tok + 8, d), bf16),
        in_specs=[anywhere] * 3,
        out_specs=on_chip,
        scratch_shapes=[pltpu.VMEM((2, *routes.shape), jnp.int32), pltpu.SemaphoreType.DMA((3,))],
        cost_estimate=light,
        compiler_params=params(8),
        name="pack",
    )(in_hbm(tokens), in_hbm(routes), in_hbm(codes))


def received_own_kernel(hid, own, out):
    out[...] = jnp.dot(hid[...], own[...], preferred_element_type=f32)


def received_other_kernel(part, hid, other, out):
    total = part[...] + jnp.dot(hid[...], other[...], preferred_element_type=f32)
    out[0] = (total * loss_scale).astype(bf16).T


def received_own(hid, own):
    h = hid.shape[0]
    rows, d = own.shape
    tile = 256
    return pl.pallas_call(
        received_own_kernel,
        out_shape=jax.ShapeDtypeStruct((h, d), f32),
        grid=(d // tile,),
        in_specs=[pl.BlockSpec((h, rows), lambda i: (0, 0)), pl.BlockSpec((rows, tile), lambda i: (0, i))],
        out_specs=pl.BlockSpec((h, tile), lambda i: (0, i)),
        cost_estimate=light,
        compiler_params=params(16),
        name="received_own",
    )(hid, own)


def received_other(part, hid, other):
    h, d = part.shape
    rows = other.shape[0]
    tile = 256
    return pl.pallas_call(
        received_other_kernel,
        out_shape=jax.ShapeDtypeStruct((1, d, 3 * h), bf16),
        grid=(d // tile,),
        in_specs=[
            pl.BlockSpec((h, tile), lambda i: (0, i)),
            pl.BlockSpec((h, rows), lambda i: (0, 0)),
            pl.BlockSpec((rows, tile), lambda i: (0, i)),
        ],
        out_specs=pl.BlockSpec((1, tile, h), lambda i: (0, i, 2)),
        cost_estimate=light,
        compiler_params=params(16),
        name="received_other",
    )(part, hid, other)


def inputs_kernel(cap, last, here, old, inputs, own, other, late, out, held):
    rows = own.shape[0]

    @pl.when(pl.program_id(0) == 0)
    def _():
        held[...] = other[...]
        held[plane_rows(here[0], *last, cap), :] = late[...]

    part = jnp.dot(inputs[:, :rows], own[...], preferred_element_type=f32)
    part = part + jnp.dot(inputs[:, rows:], held[...], preferred_element_type=f32)
    out[0] = (part * loss_scale).astype(bf16)


def inputs_part(here, last, old, inputs, own, other, late, cap):
    d, slots = inputs.shape
    rows, wide = own.shape
    tile = 256

    def fixed(v):
        return pl.BlockSpec(v.shape, lambda i, here: (0, 0))

    return pl.pallas_call(
        functools.partial(inputs_kernel, cap, last),
        out_shape=jax.ShapeDtypeStruct(old.shape, bf16),
        grid_spec=pltpu.PrefetchScalarGridSpec(
            num_scalar_prefetch=1,
            grid=(d // tile,),
            in_specs=[anywhere, pl.BlockSpec((tile, slots), lambda i, here: (i, 0)), fixed(own), fixed(other), fixed(late)],
            out_specs=pl.BlockSpec((1, tile, wide), lambda i, here: (0, i, 0)),
            scratch_shapes=[pltpu.VMEM((rows, wide), bf16)],
        ),
        input_output_aliases={1: 0},
        cost_estimate=light,
        compiler_params=params(24),
        name="inputs_part",
    )(here, old, inputs, own, other, late)


def together(*values):
    return lax.optimization_barrier(values)


def body_grid(out_grad, routes, gate_codes, w_gate, w_up, w_down, saved_inputs, saved_gate, saved_up):
    owners = lax.axis_size("expert")
    me = lax.axis_index("expert")
    to_core = [(i, i ^ 1) for i in range(owners)]
    to_x = [(i, i ^ 2) for i in range(owners)]
    tok, d = out_grad.shape
    choices = routes.shape[1]
    slots = saved_gate.shape[1]
    cap = slots // owners

    def send(v, perm):
        return lax.ppermute(v, "expert", perm)

    line = 256 * pl.cdiv(tok, 256)
    block = pack(out_grad, routes.T, gate_codes.T, line)
    here = me.reshape(1).astype(jnp.int32)

    def ring(v, hops=1):
        return send(v, [(i, (i + 4 * hops) % owners) for i in range(owners)])

    wd, sg, su = w_down[0], saved_gate[0], saved_up[0]
    wd_c, sg_c, su_c = [send(v, to_core) for v in (wd, sg, su)]

    half = slots // 2
    recs, gps = [], []

    def first(chunk, toks):
        recs[:], (share, *shares, pos) = (lambda a, b, *rest: ([a, b], rest))(
            *dispatch(here, chunk, toks, wd, wd_c, cap, half, recs)
        )
        return (chunk, share, pos), *shares

    def exchange(v):
        return lax.ppermute(v, "dp", [(0, 1), (1, 0)])

    def second(state, *peers, last=False):
        chunk, share, pos = state
        gps[:], sums = (lambda a, b, *rest: ([a, b], rest))(
            *combine(here, chunk, share, peers, pos, (sg, su), (sg_c, su_c), w, w_c, cap, half, gps, last)
        )
        return sums

    r1, x0 = ring(block), send(block, to_x)
    c0, h0 = first([(0, 0)], [block])
    w = join(w_gate[0], w_up[0])
    inputs = turn(here, saved_inputs[0], cap)
    hid = hidden(here, sg, su, cap, 0)
    r1, x0, h0, w, inputs, hid, sg_c, su_c = together(r1, x0, h0, w, inputs, hid, sg_c, su_c)
    r2, x1 = ring(r1), send(r1, to_x)
    h0, w_c = exchange(h0), send(w, to_core)
    c1, h1, g1 = first([(1, 0), (0, 1)], [x0, r1])
    h1 = exchange(h1)
    (t_r0,) = second(c0, h0)
    hid_c = hidden(here, sg, su, cap, 1)
    r2, x1, h1, g1, t_r0, hid_c = together(r2, x1, h1, g1, t_r0, hid_c)
    r3, x2 = ring(r2), send(r2, to_x)
    g1 = exchange(g1)
    c2, h2, g2 = first([(1, 1), (0, 2)], [x1, r2])
    h2 = exchange(h2)
    t_x0, t_r1 = second(c1, h1, g1)
    r3, x2, h2, g2, t_x0, t_r1 = together(r3, x2, h2, g2, t_x0, t_r1)
    x3, w1 = send(r3, to_x), ring(t_r1)
    g2 = exchange(g2)
    c3, h3, g3 = first([(1, 2), (0, 3)], [x2, r3])
    h3 = exchange(h3)
    t_x1, t_r2 = second(c2, h2, g2)
    x3, w1, h3, g3, t_x0, t_x1, t_r2 = together(x3, w1, h3, g3, t_x0, t_x1, t_r2)
    u1, b0 = ring(t_x1), send(t_x0, to_x)
    g3 = exchange(g3)
    c4, h4 = first([(1, 3)], [x3])
    h4 = exchange(h4)
    t_x2, t_r3 = second(c3, h3, g3)
    u1, b0, h4, t_x2, t_r3, rec_away, gp_away = together(u1, b0, h4, t_x2, t_r3, recs[1], gps[1])
    rec_c, gp_c = send(rec_away, to_core), send(gp_away, to_core)
    a0, a1, h4 = together(*add_halves(t_x2, u1), h4)
    b2 = [send(a0, to_x), send(a1, to_x)]
    left, right = second(c4, h4, last=True)
    b3 = [send(left, to_x), send(right, to_x)]
    late = send(gps[1], to_core)
    part = received_own(hid, recs[0])
    b2[0], _, part, rec_c = together(b2[0], left, part, rec_c)
    w2 = [ring(add([t_r2, w1, b2[k]], k)) for k in range(2)]
    part = received_other(part, hid_c, rec_c)
    w2[0], part = together(w2[0], part)
    w3 = [ring(add([t_r3, b3[k], w2[k]], k)) for k in range(2)]
    weight_grads = inputs_part(here, (1, 3), part, inputs, gps[0], gp_c, late, cap)
    w3[1], weight_grads = together(w3[1], weight_grads)
    return (finish(t_r0, b0, *w3), weight_grads)


def solution(mesh):
    placed = (
        P("expert", "dp"),
        P("expert", None),
        P("expert", None),
        P("expert", "dp", None),
        P("expert", "dp", None),
        P("expert", None, "dp"),
        P("expert", None, "dp"),
        P("expert", None, None),
        P("expert", None, None),
    )
    small = mesh.shape["expert"] == 16 and mesh.shape["dp"] == 2
    return jax.shard_map(
        body_grid if small else body_any,
        mesh=mesh,
        in_specs=placed,
        out_specs=(P("expert", "dp"), P("expert", "dp", None)),
        check_vma=False,
    )
```

```python
import functools

import jax
import jax.numpy as jnp
from jax import lax
from jax.experimental import pallas as pl
from jax.experimental.pallas import tpu as pltpu
from jax.sharding import PartitionSpec as P

gate_unit = 0.00390625
loss_scale = 0.015625
f32 = jnp.float32
bf16 = jnp.bfloat16


def contract_rows(left, right):
    return lax.dot_general(left, right, (((0,), (0,)), ((), ())), preferred_element_type=f32)


def contract_cols(left, right):
    return lax.dot_general(left, right, (((1,), (1,)), ((), ())), preferred_element_type=f32)


def activation_grads(grad_hidden, gate_pre, up_pre):
    sigmoid = jax.nn.sigmoid(gate_pre)
    silu = gate_pre * sigmoid
    dsilu = sigmoid * (1.0 + gate_pre * (1.0 - sigmoid))
    grad_gate_pre = (grad_hidden * up_pre * dsilu).astype(bf16)
    grad_up_pre = (grad_hidden * silu).astype(bf16)
    return (grad_gate_pre, grad_up_pre)


def sigmoid_of(x):
    return 0.5 * jnp.tanh(0.5 * x) + 0.5


def kernel_grads(grad_hidden, gate_pre, up_pre):
    sigmoid = sigmoid_of(gate_pre)
    silu = gate_pre * sigmoid
    dsilu = sigmoid + silu * (1.0 - sigmoid)
    return ((grad_hidden * up_pre * dsilu).astype(bf16), (grad_hidden * silu).astype(bf16))


def body_any(out_grad, routes, gate_codes, w_gate, w_up, w_down, saved_inputs, saved_gate, saved_up):
    owners = lax.axis_size("expert")
    slot_count = saved_gate.shape[1]
    capacity = slot_count // owners
    token_count = routes.shape[0]
    choice_count = routes.shape[1]
    flat_routes = routes.reshape(-1)
    onehot = (flat_routes[:, None] == jnp.arange(owners, dtype=jnp.int32)[None, :]).astype(jnp.int32)
    earlier = jnp.cumsum(onehot, axis=0) - onehot
    position = jnp.sum(earlier * onehot, axis=1)
    slot_index = (flat_routes * capacity + position).reshape(token_count, choice_count)
    gate_values = gate_codes.astype(f32) * gate_unit
    rows_iota = jnp.arange(slot_count, dtype=jnp.int32)[:, None]
    weighted = jnp.zeros((slot_count, token_count), f32)
    picks = jnp.zeros((slot_count, token_count), f32)
    for pick in range(choice_count):
        hit = rows_iota == slot_index[:, pick][None, :]
        weighted = weighted + jnp.where(hit, gate_values[:, pick][None, :], 0.0)
        picks = picks + hit.astype(f32)
    outgoing = jnp.dot(weighted.astype(bf16), out_grad, preferred_element_type=f32).astype(bf16)
    received = lax.all_to_all(outgoing, "expert", split_axis=0, concat_axis=0, tiled=True)
    hidden_share = lax.psum_scatter(
        contract_cols(received, w_down[0]), "dp", scatter_dimension=0, tiled=True
    )
    gate_pre = saved_gate[0].astype(f32)
    up_pre = saved_up[0].astype(f32)
    hidden = (gate_pre * jax.nn.sigmoid(gate_pre) * up_pre).astype(bf16)
    grad_hidden = lax.all_gather(hidden_share, "dp", axis=0, tiled=True)
    grad_gate_pre, grad_up_pre = activation_grads(grad_hidden, gate_pre, up_pre)
    slot_grads = contract_cols(grad_gate_pre, w_gate[0]) + contract_cols(grad_up_pre, w_up[0])
    returned = lax.all_to_all(
        slot_grads.astype(bf16), "expert", split_axis=0, concat_axis=0, tiled=True
    )
    token_grads = contract_rows(picks.astype(bf16), returned).astype(bf16)
    inputs_here = saved_inputs[0]
    part = jnp.concatenate(
        [
            contract_rows(inputs_here, grad_gate_pre),
            contract_rows(inputs_here, grad_up_pre),
            contract_rows(received, hidden),
        ],
        axis=1,
    )
    return (token_grads, (part * loss_scale).astype(bf16)[None])


on_chip = pl.BlockSpec(memory_space=pltpu.VMEM)
on_scalar = pl.BlockSpec(memory_space=pltpu.SMEM)
anywhere = pl.BlockSpec(memory_space=pl.ANY)
light = pl.CostEstimate(flops=1 << 20, bytes_accessed=1 << 14, transcendentals=0)


def source(here, step, other):
    group = lax.rem(here // 4 + (4 - step), 4)
    return jnp.bitwise_xor(group * 4 + lax.rem(here, 4), 2 * other)


def params(mib):
    return pltpu.CompilerParams(vmem_limit_bytes=mib << 20)


def plane_rows(here, other, step, cap):
    return pl.ds(pl.multiple_of((source(here, step, other) // 2) * cap, 16), cap)


def dispatch_kernel(chunk, cap, begun, here, *refs):
    n = len(chunk)
    toks, (wd0, wd1) = refs[:n], refs[n : n + 2]
    buf0, buf1, share, *share_out, pos_out, rec, sems = refs[n + 2 + 2 * begun :]
    tok = toks[0].shape[0] - 8
    line = 256 * pl.cdiv(tok, 256)
    before = lax.broadcasted_iota(jnp.int32, (tok, tok), 0) < lax.broadcasted_iota(jnp.int32, (tok, tok), 1)
    before = jnp.where(before, 1.0, 0.0).astype(bf16)
    slot = lax.broadcasted_iota(jnp.int32, (cap, tok), 0).astype(f32)
    masks, gates = [], []
    for a in range(2):
        expert = jnp.bitwise_xor(here[0], a).astype(f32)
        for t in toks:
            hit = t[tok:, :tok].astype(f32) == expert
            masks.append(jnp.max(jnp.where(hit, 1.0, 0.0), axis=0, keepdims=True))
            gates.append(jnp.sum(jnp.where(hit, t[tok:, line : line + tok].astype(f32), 0.0), axis=0, keepdims=True))
    fill = [jnp.zeros((8 - 2 * n, tok), f32)] if n < 4 else []
    mask = jnp.concatenate(masks + fill, axis=0)
    pos = jnp.dot(mask.astype(bf16), before, preferred_element_type=f32)
    pos = jnp.where(mask > 0.0, pos, -1.0)
    pos_out[...] = pos
    copies = []
    for rel, t in enumerate(toks):
        w = [
            jnp.where(slot == pos[i : i + 1, :], gates[i] * gate_unit, 0.0).astype(bf16)
            for i in (rel, n + rel)
        ]
        rows = jnp.dot(jnp.concatenate(w, axis=0), t[:tok, :], preferred_element_type=f32).astype(bf16)
        at = pl.ds(rel * cap, cap)
        for a, buf in enumerate((buf0, buf1)):
            rec[a, at, :] = rows[a * cap : (a + 1) * cap]
            to = plane_rows(here[0], *chunk[rel], cap)
            copies.append(pltpu.make_async_copy(rec.at[a, at, :], buf.at[to, :], sems.at[len(copies)]))
    for c in copies:
        c.start()
    for a, wd in enumerate((wd0, wd1)):
        gh = contract_cols(rec[a], wd[...])
        share[a * n * cap : (a + 1) * n * cap, :] = gh
        if n == 1:
            share_out[0][a * cap : (a + 1) * cap, :] = gh.astype(bf16)
        else:
            share_out[a][...] = gh.astype(bf16)
    for c in copies:
        c.wait()


def dispatch(here, chunk, toks, wd0, wd1, cap, rows, old):
    n = len(toks)
    tok, d = toks[0].shape
    h = wd0.shape[0]
    outs = [((rows, d), bf16)] * 2 + [((2 * n * cap, h), f32)]
    outs += [((2 * cap, h), bf16)] if n == 1 else [((n * cap, h), bf16)] * 2
    outs += [((8, tok - 8), f32)]
    return pl.pallas_call(
        functools.partial(dispatch_kernel, chunk, cap, len(old) // 2),
        out_shape=[jax.ShapeDtypeStruct(s, t) for s, t in outs],
        in_specs=[on_scalar] + [on_chip] * (n + 2) + [anywhere] * len(old),
        out_specs=[anywhere] * 2 + [on_chip] * (len(outs) - 2),
        scratch_shapes=[pltpu.VMEM((2, n * cap, d), bf16), pltpu.SemaphoreType.DMA((2 * n,))],
        input_output_aliases={n + 3 + k: k for k in range(len(old))},
        cost_estimate=light,
        compiler_params=params(16),
        name="dispatch",
    )(here, *toks, wd0, wd1, *old)


def combine_kernel(chunk, cap, begun, last, here, share, *refs):
    n = len(chunk)
    if n == 1:
        peer0, peer1 = refs[0].at[:cap, :], refs[0].at[cap:, :]
        pos, *refs = refs[1:]
    else:
        peer0, peer1, pos, *refs = refs
    saved, ws, refs = refs[:4], refs[4:6], refs[6 + begun :]
    buffers, backs, (gps, out_sems) = refs[:2], refs[2:-2], refs[-2:]
    h = share.shape[1]
    slot = lax.broadcasted_iota(jnp.int32, (cap, pos.shape[1]), 0).astype(f32)
    leaving = []
    for a, peer in enumerate((peer0, peer1)):
        for rel in range(n):
            i = a * n + rel
            at = slice(rel * cap, (rel + 1) * cap)
            gh = share[i * cap : (i + 1) * cap, :] + peer[at, :].astype(f32)
            other, step = chunk[rel]
            own = pl.ds(pl.multiple_of(source(here[0], step, other) * cap, 16), cap)
            gg, gu = kernel_grads(gh, saved[2 * a][own, :].astype(f32), saved[2 * a + 1][own, :].astype(f32))
            gps[a, at, :h] = gg
            gps[a, at, h:] = gu
            if a == 0 or not last:
                to = buffers[a].at[plane_rows(here[0], *chunk[rel], cap), :]
                leaving.append(pltpu.make_async_copy(gps.at[a, at, :], to, out_sems.at[i]))
    for c in leaving:
        c.start()
    if last:
        buffers[1][...] = gps[1]
    sums = [None] * n
    for a, w in enumerate(ws):
        slots = contract_cols(gps[a], w[...]).astype(bf16)
        for rel in range(n):
            i = a * n + rel
            pick = jnp.where(slot == pos[i : i + 1, :], 1.0, 0.0).astype(bf16)
            part = contract_rows(pick, slots[rel * cap : (rel + 1) * cap])
            sums[rel] = part if sums[rel] is None else sums[rel] + part
    if len(backs) > n:
        half = backs[0].shape[1]
        for k, back in enumerate(backs):
            back[...] = sums[0][:, k * half : (k + 1) * half].astype(bf16)
    else:
        for rel in range(n):
            backs[rel][...] = sums[rel].astype(bf16)
    for c in leaving:
        c.wait()


def combine(here, chunk, share, peers, pos, saved0, saved1, w0, w1, cap, rows, old, last=False):
    n = len(chunk)
    h = share.shape[1]
    d = w0.shape[0]
    tok = pos.shape[1]
    old = old[:1] if last else old
    outs = [(rows, 2 * h), (n * cap if last else rows, 2 * h)] + ([(tok, d // 2)] * 2 if last else [(tok, d)] * n)
    first_old = 2 + len(peers) + 1 + 4 + 2
    return pl.pallas_call(
        functools.partial(combine_kernel, chunk, cap, len(old), last),
        out_shape=[jax.ShapeDtypeStruct(s, bf16) for s in outs],
        in_specs=[on_scalar] + [on_chip] * (2 + len(peers) + 6) + [anywhere] * len(old),
        out_specs=[anywhere, on_chip if last else anywhere] + [on_chip] * (len(outs) - 2),
        scratch_shapes=[
            pltpu.VMEM((2, n * cap, 2 * h), bf16),
            pltpu.SemaphoreType.DMA((2 * n,)),
        ],
        input_output_aliases={first_old + k: k for k in range(len(old))},
        cost_estimate=light,
        compiler_params=params(20),
        name="combine",
    )(here, share, *peers, pos, *saved0, *saved1, w0, w1, *old)


def join_kernel(left, right, out):
    out[:, : left.shape[1]] = left[...]
    out[:, left.shape[1] :] = right[...]


def join(left, right):
    rows, h = left.shape
    return pl.pallas_call(
        join_kernel,
        out_shape=jax.ShapeDtypeStruct((rows, 2 * h), left.dtype),
        in_specs=[on_chip] * 2,
        out_specs=on_chip,
        cost_estimate=light,
        compiler_params=params(8),
        name="join",
    )(left, right)


def add_kernel(part, *refs):
    wide = refs[-1].shape[1]
    total = None
    for r in refs[:-1]:
        v = r[...] if part is None or r.shape[1] == wide else r[:, part * wide : (part + 1) * wide]
        total = v.astype(f32) if total is None else total + v.astype(f32)
    refs[-1][...] = total.astype(bf16)


def add(values, part=None):
    rows, wide = values[0].shape
    return pl.pallas_call(
        functools.partial(add_kernel, part),
        out_shape=jax.ShapeDtypeStruct((rows, wide if part is None else wide // 2), bf16),
        in_specs=[on_chip] * len(values),
        out_specs=on_chip,
        cost_estimate=light,
        compiler_params=params(8),
        name="add",
    )(*values)


def add_halves_kernel(a, b, left, right):
    total = (a[...].astype(f32) + b[...].astype(f32)).astype(bf16)
    left[...] = total[:, : left.shape[1]]
    right[...] = total[:, left.shape[1] :]


def add_halves(a, b):
    rows, wide = a.shape
    return pl.pallas_call(
        add_halves_kernel,
        out_shape=[jax.ShapeDtypeStruct((rows, wide // 2), bf16)] * 2,
        in_specs=[on_chip] * 2,
        out_specs=[on_chip] * 2,
        cost_estimate=light,
        compiler_params=params(8),
        name="add_halves",
    )(a, b)


def finish_kernel(a, b, left, right, out):
    half = left.shape[1]
    for at, v in ((0, left), (half, right)):
        total = a[:, at : at + half].astype(f32) + b[:, at : at + half].astype(f32) + v[...].astype(f32)
        out[:, at : at + half] = total.astype(bf16)


def finish(a, b, left, right):
    return pl.pallas_call(
        finish_kernel,
        out_shape=jax.ShapeDtypeStruct(a.shape, bf16),
        in_specs=[on_chip] * 4,
        out_specs=on_chip,
        cost_estimate=light,
        compiler_params=params(8),
        name="finish",
    )(a, b, left, right)


def in_hbm(v):
    return pltpu.with_memory_space_constraint(v, pltpu.HBM)


def hidden_kernel(cap, k, here, gate, up, out, held, sems):
    plane = lax.rem(here[0] + k, 2)
    copies = []
    for i, v in enumerate((gate, up)):
        for q in range(held.shape[1] // cap):
            at = pl.ds(pl.multiple_of((2 * q + plane) * cap, 16), cap)
            to = held.at[i, pl.ds(q * cap, cap), :]
            copies.append(pltpu.make_async_copy(v.at[at, :], to, sems.at[len(copies)]))
    for c in copies:
        c.start()
    for c in copies:
        c.wait()
    gate_pre = held[0].astype(f32)
    out[...] = (gate_pre * sigmoid_of(gate_pre) * held[1].astype(f32)).astype(bf16).T


def hidden(here, gate, up, cap, k):
    slots, h = gate.shape
    return pl.pallas_call(
        functools.partial(hidden_kernel, cap, k),
        out_shape=jax.ShapeDtypeStruct((h, slots // 2), bf16),
        in_specs=[on_scalar, anywhere, anywhere],
        out_specs=on_chip,
        scratch_shapes=[pltpu.VMEM((2, slots // 2, h), bf16), pltpu.SemaphoreType.DMA((slots // cap,))],
        cost_estimate=light,
        compiler_params=params(16),
        name="hidden",
    )(here, in_hbm(gate), in_hbm(up))


def turn_kernel(cap, here, v, out, held):
    rows = held.shape[0]
    for k in range(2):
        plane = lax.rem(here[0] + k, 2)
        for q in range(rows // cap):
            held[q * cap : (q + 1) * cap, :] = v[pl.ds(pl.multiple_of((2 * q + plane) * cap, 16), cap), :]
        out[:, k * rows : (k + 1) * rows] = held[...].T


def turn(here, v, cap):
    slots, d = v.shape
    tile = 256
    return pl.pallas_call(
        functools.partial(turn_kernel, cap),
        out_shape=jax.ShapeDtypeStruct((d, slots), v.dtype),
        grid_spec=pltpu.PrefetchScalarGridSpec(
            num_scalar_prefetch=1,
            grid=(d // tile,),
            in_specs=[pl.BlockSpec((slots, tile), lambda i, here: (0, i))],
            out_specs=pl.BlockSpec((tile, slots), lambda i, here: (i, 0)),
            scratch_shapes=[pltpu.VMEM((slots // 2, tile), v.dtype)],
        ),
        cost_estimate=light,
        compiler_params=params(12),
        name="turn",
    )(here, in_hbm(v))


def pack_kernel(line, tokens, routes, codes, out, named, sems):
    tok = tokens.shape[0]
    copies = [
        pltpu.make_async_copy(tokens, out.at[:tok, :], sems.at[0]),
        pltpu.make_async_copy(routes, named.at[0], sems.at[1]),
        pltpu.make_async_copy(codes, named.at[1], sems.at[2]),
    ]
    for c in copies:
        c.start()
    out[tok:, :] = jnp.zeros((8, out.shape[1]), bf16)
    for k, at in enumerate((0, line)):
        copies[1 + k].wait()
        out[tok:, at : at + tok] = named[k].astype(f32).astype(bf16)
    copies[0].wait()


def pack(tokens, routes, codes, line):
    tok, d = tokens.shape
    return pl.pallas_call(
        functools.partial(pack_kernel, line),
        out_shape=jax.ShapeDtypeStruct((tok + 8, d), bf16),
        in_specs=[anywhere] * 3,
        out_specs=on_chip,
        scratch_shapes=[pltpu.VMEM((2, *routes.shape), jnp.int32), pltpu.SemaphoreType.DMA((3,))],
        cost_estimate=light,
        compiler_params=params(8),
        name="pack",
    )(in_hbm(tokens), in_hbm(routes), in_hbm(codes))


def received_own_kernel(hid, own, out):
    out[...] = jnp.dot(hid[...], own[...], preferred_element_type=f32)


def received_own(hid, own):
    return pl.pallas_call(
        received_own_kernel,
        out_shape=jax.ShapeDtypeStruct((hid.shape[0], own.shape[1]), f32),
        in_specs=[on_chip] * 2,
        out_specs=on_chip,
        cost_estimate=light,
        compiler_params=params(16),
        name="received_own",
    )(hid, own)


def received_other_kernel(part, hid, other, out, tiles, sems):
    count, tile, h = tiles.shape
    copies = []
    for i in range(count):
        at = slice(i * tile, (i + 1) * tile)
        total = part[:, at] + jnp.dot(hid[...], other[:, at], preferred_element_type=f32)
        tiles[i] = (total * loss_scale).astype(bf16).T
        copies.append(pltpu.make_async_copy(tiles.at[i], out.at[0, at, pl.ds(2 * h, h)], sems.at[i]))
        copies[-1].start()
    for c in copies:
        c.wait()


def received_other(part, hid, other):
    h, d = part.shape
    tile = 256
    return pl.pallas_call(
        received_other_kernel,
        out_shape=jax.ShapeDtypeStruct((1, d, 3 * h), bf16),
        in_specs=[on_chip] * 3,
        out_specs=anywhere,
        scratch_shapes=[pltpu.VMEM((d // tile, tile, h), bf16), pltpu.SemaphoreType.DMA((d // tile,))],
        cost_estimate=light,
        compiler_params=params(16),
        name="received_other",
    )(part, hid, other)


def inputs_kernel(cap, last, here, old, inputs, own, other, late, out, held, tiles, sems):
    rows, wide = own.shape
    count, tile, _ = tiles.shape
    held[...] = other[...]
    held[plane_rows(here[0], *last, cap), :] = late[...]
    copies = []
    for i in range(count):
        at = slice(i * tile, (i + 1) * tile)
        part = jnp.dot(inputs[at, :rows], own[...], preferred_element_type=f32)
        part = part + jnp.dot(inputs[at, rows:], held[...], preferred_element_type=f32)
        tiles[i] = (part * loss_scale).astype(bf16)
        copies.append(pltpu.make_async_copy(tiles.at[i], out.at[0, at, pl.ds(0, wide)], sems.at[i]))
        copies[-1].start()
    for c in copies:
        c.wait()


def inputs_part(here, last, old, inputs, own, other, late, cap):
    d = inputs.shape[0]
    rows, wide = own.shape
    tile = 256
    return pl.pallas_call(
        functools.partial(inputs_kernel, cap, last),
        out_shape=jax.ShapeDtypeStruct(old.shape, bf16),
        in_specs=[on_scalar, anywhere] + [on_chip] * 4,
        out_specs=anywhere,
        scratch_shapes=[
            pltpu.VMEM((rows, wide), bf16),
            pltpu.VMEM((d // tile, tile, wide), bf16),
            pltpu.SemaphoreType.DMA((d // tile,)),
        ],
        input_output_aliases={1: 0},
        cost_estimate=light,
        compiler_params=params(20),
        name="inputs_part",
    )(here, old, inputs, own, other, late)


def together(*values):
    return lax.optimization_barrier(values)


def body_grid(out_grad, routes, gate_codes, w_gate, w_up, w_down, saved_inputs, saved_gate, saved_up):
    owners = lax.axis_size("expert")
    me = lax.axis_index("expert")
    to_core = [(i, i ^ 1) for i in range(owners)]
    to_x = [(i, i ^ 2) for i in range(owners)]
    tok, d = out_grad.shape
    choices = routes.shape[1]
    slots = saved_gate.shape[1]
    cap = slots // owners

    def send(v, perm):
        return lax.ppermute(v, "expert", perm)

    line = 256 * pl.cdiv(tok, 256)
    block = pack(out_grad, routes.T, gate_codes.T, line)
    here = me.reshape(1).astype(jnp.int32)

    def ring(v, hops=1):
        return send(v, [(i, (i + 4 * hops) % owners) for i in range(owners)])

    wd, sg, su = w_down[0], saved_gate[0], saved_up[0]
    wd_c, sg_c, su_c = [send(v, to_core) for v in (wd, sg, su)]

    half = slots // 2
    recs, gps = [], []

    def first(chunk, toks):
        recs[:], (share, *shares, pos) = (lambda a, b, *rest: ([a, b], rest))(
            *dispatch(here, chunk, toks, wd, wd_c, cap, half, recs)
        )
        return (chunk, share, pos), *shares

    def exchange(v):
        return lax.ppermute(v, "dp", [(0, 1), (1, 0)])

    def second(state, *peers, last=False):
        chunk, share, pos = state
        gps[:], sums = (lambda a, b, *rest: ([a, b], rest))(
            *combine(here, chunk, share, peers, pos, (sg, su), (sg_c, su_c), w, w_c, cap, half, gps, last)
        )
        return sums

    r1, x0 = ring(block), send(block, to_x)
    c0, h0 = first([(0, 0)], [block])
    w = join(w_gate[0], w_up[0])
    inputs = turn(here, saved_inputs[0], cap)
    hid = hidden(here, sg, su, cap, 0)
    r1, x0, h0, w, inputs, hid, sg_c, su_c = together(r1, x0, h0, w, inputs, hid, sg_c, su_c)
    r2, x1 = ring(r1), send(r1, to_x)
    h0, w_c = exchange(h0), send(w, to_core)
    c1, h1, g1 = first([(1, 0), (0, 1)], [x0, r1])
    h1 = exchange(h1)
    (t_r0,) = second(c0, h0)
    hid_c = hidden(here, sg, su, cap, 1)
    r2, x1, h1, g1, t_r0, hid_c = together(r2, x1, h1, g1, t_r0, hid_c)
    r3, x2 = ring(r2), send(r2, to_x)
    g1 = exchange(g1)
    c2, h2, g2 = first([(1, 1), (0, 2)], [x1, r2])
    h2 = exchange(h2)
    t_x0, t_r1 = second(c1, h1, g1)
    r3, x2, h2, g2, t_x0, t_r1 = together(r3, x2, h2, g2, t_x0, t_r1)
    x3, w1 = send(r3, to_x), ring(t_r1)
    g2 = exchange(g2)
    c3, h3, g3 = first([(1, 2), (0, 3)], [x2, r3])
    h3 = exchange(h3)
    t_x1, t_r2 = second(c2, h2, g2)
    x3, w1, h3, g3, t_x0, t_x1, t_r2 = together(x3, w1, h3, g3, t_x0, t_x1, t_r2)
    u1, b0 = ring(t_x1), send(t_x0, to_x)
    g3 = exchange(g3)
    c4, h4 = first([(1, 3)], [x3])
    h4 = exchange(h4)
    t_x2, t_r3 = second(c3, h3, g3)
    u1, b0, h4, t_x2, t_r3, rec_away, gp_away = together(u1, b0, h4, t_x2, t_r3, recs[1], gps[1])
    rec_c, gp_c = send(rec_away, to_core), send(gp_away, to_core)
    a0, a1, h4 = together(*add_halves(t_x2, u1), h4)
    b2 = [send(a0, to_x), send(a1, to_x)]
    left, right = second(c4, h4, last=True)
    b3 = [send(left, to_x), send(right, to_x)]
    late = send(gps[1], to_core)
    part = received_own(hid, recs[0])
    b2[0], _, part, rec_c = together(b2[0], left, part, rec_c)
    w2 = [ring(add([t_r2, w1, b2[k]], k)) for k in range(2)]
    part = received_other(part, hid_c, rec_c)
    w2[0], part = together(w2[0], part)
    w3 = [ring(add([t_r3, b3[k], w2[k]], k)) for k in range(2)]
    weight_grads = inputs_part(here, (1, 3), part, inputs, gps[0], gp_c, late, cap)
    w3[1], weight_grads = together(w3[1], weight_grads)
    return (finish(t_r0, b0, *w3), weight_grads)


def solution(mesh):
    placed = (
        P("expert", "dp"),
        P("expert", None),
        P("expert", None),
        P("expert", "dp", None),
        P("expert", "dp", None),
        P("expert", None, "dp"),
        P("expert", None, "dp"),
        P("expert", None, None),
        P("expert", None, None),
    )
    small = mesh.shape["expert"] == 16 and mesh.shape["dp"] == 2
    return jax.shard_map(
        body_grid if small else body_any,
        mesh=mesh,
        in_specs=placed,
        out_specs=(P("expert", "dp"), P("expert", "dp", None)),
        check_vma=False,
    )
```

```python
import functools

import jax
import jax.numpy as jnp
from jax import lax
from jax.experimental import pallas as pl
from jax.experimental.pallas import tpu as pltpu
from jax.sharding import PartitionSpec as P

gate_unit = 0.00390625
loss_scale = 0.015625
f32 = jnp.float32
bf16 = jnp.bfloat16


def contract_rows(left, right):
    return lax.dot_general(left, right, (((0,), (0,)), ((), ())), preferred_element_type=f32)


def contract_cols(left, right):
    return lax.dot_general(left, right, (((1,), (1,)), ((), ())), preferred_element_type=f32)


def activation_grads(grad_hidden, gate_pre, up_pre):
    sigmoid = jax.nn.sigmoid(gate_pre)
    silu = gate_pre * sigmoid
    dsilu = sigmoid * (1.0 + gate_pre * (1.0 - sigmoid))
    grad_gate_pre = (grad_hidden * up_pre * dsilu).astype(bf16)
    grad_up_pre = (grad_hidden * silu).astype(bf16)
    return (grad_gate_pre, grad_up_pre)


def sigmoid_of(x):
    return 0.5 * jnp.tanh(0.5 * x) + 0.5


def kernel_grads(grad_hidden, gate_pre, up_pre):
    sigmoid = sigmoid_of(gate_pre)
    silu = gate_pre * sigmoid
    dsilu = sigmoid + silu * (1.0 - sigmoid)
    return ((grad_hidden * up_pre * dsilu).astype(bf16), (grad_hidden * silu).astype(bf16))


def body_any(out_grad, routes, gate_codes, w_gate, w_up, w_down, saved_inputs, saved_gate, saved_up):
    owners = lax.axis_size("expert")
    slot_count = saved_gate.shape[1]
    capacity = slot_count // owners
    token_count = routes.shape[0]
    choice_count = routes.shape[1]
    flat_routes = routes.reshape(-1)
    onehot = (flat_routes[:, None] == jnp.arange(owners, dtype=jnp.int32)[None, :]).astype(jnp.int32)
    earlier = jnp.cumsum(onehot, axis=0) - onehot
    position = jnp.sum(earlier * onehot, axis=1)
    slot_index = (flat_routes * capacity + position).reshape(token_count, choice_count)
    gate_values = gate_codes.astype(f32) * gate_unit
    rows_iota = jnp.arange(slot_count, dtype=jnp.int32)[:, None]
    weighted = jnp.zeros((slot_count, token_count), f32)
    picks = jnp.zeros((slot_count, token_count), f32)
    for pick in range(choice_count):
        hit = rows_iota == slot_index[:, pick][None, :]
        weighted = weighted + jnp.where(hit, gate_values[:, pick][None, :], 0.0)
        picks = picks + hit.astype(f32)
    outgoing = jnp.dot(weighted.astype(bf16), out_grad, preferred_element_type=f32).astype(bf16)
    received = lax.all_to_all(outgoing, "expert", split_axis=0, concat_axis=0, tiled=True)
    hidden_share = lax.psum_scatter(
        contract_cols(received, w_down[0]), "dp", scatter_dimension=0, tiled=True
    )
    gate_pre = saved_gate[0].astype(f32)
    up_pre = saved_up[0].astype(f32)
    hidden = (gate_pre * jax.nn.sigmoid(gate_pre) * up_pre).astype(bf16)
    grad_hidden = lax.all_gather(hidden_share, "dp", axis=0, tiled=True)
    grad_gate_pre, grad_up_pre = activation_grads(grad_hidden, gate_pre, up_pre)
    slot_grads = contract_cols(grad_gate_pre, w_gate[0]) + contract_cols(grad_up_pre, w_up[0])
    returned = lax.all_to_all(
        slot_grads.astype(bf16), "expert", split_axis=0, concat_axis=0, tiled=True
    )
    token_grads = contract_rows(picks.astype(bf16), returned).astype(bf16)
    inputs_here = saved_inputs[0]
    part = jnp.concatenate(
        [
            contract_rows(inputs_here, grad_gate_pre),
            contract_rows(inputs_here, grad_up_pre),
            contract_rows(received, hidden),
        ],
        axis=1,
    )
    return (token_grads, (part * loss_scale).astype(bf16)[None])


on_chip = pl.BlockSpec(memory_space=pltpu.VMEM)
on_scalar = pl.BlockSpec(memory_space=pltpu.SMEM)
anywhere = pl.BlockSpec(memory_space=pl.ANY)
light = pl.CostEstimate(flops=1 << 20, bytes_accessed=1 << 14, transcendentals=0)


def source(here, step, other):
    group = lax.rem(here // 4 + (4 - step), 4)
    return jnp.bitwise_xor(group * 4 + lax.rem(here, 4), 2 * other)


def params(mib):
    return pltpu.CompilerParams(vmem_limit_bytes=mib << 20)


def plane_rows(here, other, step, cap):
    return pl.ds(pl.multiple_of((source(here, step, other) // 2) * cap, 16), cap)


def dispatch_kernel(chunk, cap, begun, here, *refs):
    n = len(chunk)
    toks, (wd0, wd1) = refs[:n], refs[n : n + 2]
    buf0, buf1, share, *share_out, pos_out, rec, sems = refs[n + 2 + 2 * begun :]
    tok = toks[0].shape[0] - 8
    line = 256 * pl.cdiv(tok, 256)
    before = lax.broadcasted_iota(jnp.int32, (tok, tok), 0) < lax.broadcasted_iota(jnp.int32, (tok, tok), 1)
    before = jnp.where(before, 1.0, 0.0).astype(bf16)
    slot = lax.broadcasted_iota(jnp.int32, (cap, tok), 0).astype(f32)
    masks, gates = [], []
    for a in range(2):
        expert = jnp.bitwise_xor(here[0], a).astype(f32)
        for t in toks:
            hit = t[tok:, :tok].astype(f32) == expert
            masks.append(jnp.max(jnp.where(hit, 1.0, 0.0), axis=0, keepdims=True))
            gates.append(jnp.sum(jnp.where(hit, t[tok:, line : line + tok].astype(f32), 0.0), axis=0, keepdims=True))
    fill = [jnp.zeros((8 - 2 * n, tok), f32)] if n < 4 else []
    mask = jnp.concatenate(masks + fill, axis=0)
    pos = jnp.dot(mask.astype(bf16), before, preferred_element_type=f32)
    pos = jnp.where(mask > 0.0, pos, -1.0)
    pos_out[...] = pos
    copies = []
    for rel, t in enumerate(toks):
        w = [
            jnp.where(slot == pos[i : i + 1, :], gates[i] * gate_unit, 0.0).astype(bf16)
            for i in (rel, n + rel)
        ]
        rows = jnp.dot(jnp.concatenate(w, axis=0), t[:tok, :], preferred_element_type=f32).astype(bf16)
        at = pl.ds(rel * cap, cap)
        for a, buf in enumerate((buf0, buf1)):
            rec[a, at, :] = rows[a * cap : (a + 1) * cap]
            to = plane_rows(here[0], *chunk[rel], cap)
            copies.append(pltpu.make_async_copy(rec.at[a, at, :], buf.at[to, :], sems.at[len(copies)]))
    for c in copies:
        c.start()
    for a, wd in enumerate((wd0, wd1)):
        gh = contract_cols(rec[a], wd[...])
        share[a * n * cap : (a + 1) * n * cap, :] = gh
        if n == 1:
            share_out[0][a * cap : (a + 1) * cap, :] = gh.astype(bf16)
        else:
            share_out[a][...] = gh.astype(bf16)
    for c in copies:
        c.wait()


def dispatch(here, chunk, toks, wd0, wd1, cap, rows, old):
    n = len(toks)
    tok, d = toks[0].shape
    h = wd0.shape[0]
    outs = [((rows, d), bf16)] * 2 + [((2 * n * cap, h), f32)]
    outs += [((2 * cap, h), bf16)] if n == 1 else [((n * cap, h), bf16)] * 2
    outs += [((8, tok - 8), f32)]
    return pl.pallas_call(
        functools.partial(dispatch_kernel, chunk, cap, len(old) // 2),
        out_shape=[jax.ShapeDtypeStruct(s, t) for s, t in outs],
        in_specs=[on_scalar] + [on_chip] * (n + 2) + [anywhere] * len(old),
        out_specs=[anywhere] * 2 + [on_chip] * (len(outs) - 2),
        scratch_shapes=[pltpu.VMEM((2, n * cap, d), bf16), pltpu.SemaphoreType.DMA((2 * n,))],
        input_output_aliases={n + 3 + k: k for k in range(len(old))},
        cost_estimate=light,
        compiler_params=params(16),
        name="dispatch",
    )(here, *toks, wd0, wd1, *old)


def combine_kernel(chunk, cap, begun, last, here, share, *refs):
    n = len(chunk)
    if n == 1:
        peer0, peer1 = refs[0].at[:cap, :], refs[0].at[cap:, :]
        pos, *refs = refs[1:]
    else:
        peer0, peer1, pos, *refs = refs
    saved, ws, refs = refs[:4], refs[4:6], refs[6 + begun :]
    buffers, backs, (gps, out_sems) = refs[:2], refs[2:-2], refs[-2:]
    h = share.shape[1]
    slot = lax.broadcasted_iota(jnp.int32, (cap, pos.shape[1]), 0).astype(f32)
    leaving = []
    for a, peer in enumerate((peer0, peer1)):
        for rel in range(n):
            i = a * n + rel
            at = slice(rel * cap, (rel + 1) * cap)
            gh = share[i * cap : (i + 1) * cap, :] + peer[at, :].astype(f32)
            other, step = chunk[rel]
            own = pl.ds(pl.multiple_of(source(here[0], step, other) * cap, 16), cap)
            gg, gu = kernel_grads(gh, saved[2 * a][own, :].astype(f32), saved[2 * a + 1][own, :].astype(f32))
            gps[a, at, :h] = gg
            gps[a, at, h:] = gu
            if a == 0 or not last:
                to = buffers[a].at[plane_rows(here[0], *chunk[rel], cap), :]
                leaving.append(pltpu.make_async_copy(gps.at[a, at, :], to, out_sems.at[i]))
    for c in leaving:
        c.start()
    if last:
        buffers[1][...] = gps[1]
    sums = [None] * n
    for a, w in enumerate(ws):
        slots = contract_cols(gps[a], w[...]).astype(bf16)
        for rel in range(n):
            i = a * n + rel
            pick = jnp.where(slot == pos[i : i + 1, :], 1.0, 0.0).astype(bf16)
            part = contract_rows(pick, slots[rel * cap : (rel + 1) * cap])
            sums[rel] = part if sums[rel] is None else sums[rel] + part
    if len(backs) > n:
        half = backs[0].shape[1]
        for k, back in enumerate(backs):
            back[...] = sums[0][:, k * half : (k + 1) * half].astype(bf16)
    else:
        for rel in range(n):
            backs[rel][...] = sums[rel].astype(bf16)
    for c in leaving:
        c.wait()


def combine(here, chunk, share, peers, pos, saved0, saved1, w0, w1, cap, rows, old, last=False):
    n = len(chunk)
    h = share.shape[1]
    d = w0.shape[0]
    tok = pos.shape[1]
    old = old[:1] if last else old
    outs = [(rows, 2 * h), (n * cap if last else rows, 2 * h)] + ([(tok, d // 2)] * 2 if last else [(tok, d)] * n)
    first_old = 2 + len(peers) + 1 + 4 + 2
    return pl.pallas_call(
        functools.partial(combine_kernel, chunk, cap, len(old), last),
        out_shape=[jax.ShapeDtypeStruct(s, bf16) for s in outs],
        in_specs=[on_scalar] + [on_chip] * (2 + len(peers) + 6) + [anywhere] * len(old),
        out_specs=[anywhere, on_chip if last else anywhere] + [on_chip] * (len(outs) - 2),
        scratch_shapes=[
            pltpu.VMEM((2, n * cap, 2 * h), bf16),
            pltpu.SemaphoreType.DMA((2 * n,)),
        ],
        input_output_aliases={first_old + k: k for k in range(len(old))},
        cost_estimate=light,
        compiler_params=params(20),
        name="combine",
    )(here, share, *peers, pos, *saved0, *saved1, w0, w1, *old)


def join_kernel(left, right, out):
    out[:, : left.shape[1]] = left[...]
    out[:, left.shape[1] :] = right[...]


def join(left, right):
    rows, h = left.shape
    return pl.pallas_call(
        join_kernel,
        out_shape=jax.ShapeDtypeStruct((rows, 2 * h), left.dtype),
        in_specs=[on_chip] * 2,
        out_specs=on_chip,
        cost_estimate=light,
        compiler_params=params(8),
        name="join",
    )(left, right)


def add_kernel(part, *refs):
    wide = refs[-1].shape[1]
    total = None
    for r in refs[:-1]:
        v = r[...] if part is None or r.shape[1] == wide else r[:, part * wide : (part + 1) * wide]
        total = v.astype(f32) if total is None else total + v.astype(f32)
    refs[-1][...] = total.astype(bf16)


def add(values, part=None):
    rows, wide = values[0].shape
    return pl.pallas_call(
        functools.partial(add_kernel, part),
        out_shape=jax.ShapeDtypeStruct((rows, wide if part is None else wide // 2), bf16),
        in_specs=[on_chip] * len(values),
        out_specs=on_chip,
        cost_estimate=light,
        compiler_params=params(8),
        name="add",
    )(*values)


def add_halves_kernel(a, b, left, right):
    total = (a[...].astype(f32) + b[...].astype(f32)).astype(bf16)
    left[...] = total[:, : left.shape[1]]
    right[...] = total[:, left.shape[1] :]


def add_halves(a, b):
    rows, wide = a.shape
    return pl.pallas_call(
        add_halves_kernel,
        out_shape=[jax.ShapeDtypeStruct((rows, wide // 2), bf16)] * 2,
        in_specs=[on_chip] * 2,
        out_specs=[on_chip] * 2,
        cost_estimate=light,
        compiler_params=params(8),
        name="add_halves",
    )(a, b)


def finish_kernel(a, b, left, right, out):
    half = left.shape[1]
    for at, v in ((0, left), (half, right)):
        total = a[:, at : at + half].astype(f32) + b[:, at : at + half].astype(f32) + v[...].astype(f32)
        out[:, at : at + half] = total.astype(bf16)


def finish(a, b, left, right):
    return pl.pallas_call(
        finish_kernel,
        out_shape=jax.ShapeDtypeStruct(a.shape, bf16),
        in_specs=[on_chip] * 4,
        out_specs=on_chip,
        cost_estimate=light,
        compiler_params=params(8),
        name="finish",
    )(a, b, left, right)


def in_hbm(v):
    return pltpu.with_memory_space_constraint(v, pltpu.HBM)


def hidden_kernel(cap, k, here, gate, up, out, held, sems):
    plane = lax.rem(here[0] + k, 2)
    copies = []
    for i, v in enumerate((gate, up)):
        for q in range(held.shape[1] // cap):
            at = pl.ds(pl.multiple_of((2 * q + plane) * cap, 16), cap)
            to = held.at[i, pl.ds(q * cap, cap), :]
            copies.append(pltpu.make_async_copy(v.at[at, :], to, sems.at[len(copies)]))
    for c in copies:
        c.start()
    for c in copies:
        c.wait()
    gate_pre = held[0].astype(f32)
    out[...] = (gate_pre * sigmoid_of(gate_pre) * held[1].astype(f32)).astype(bf16).T


def hidden(here, gate, up, cap, k):
    slots, h = gate.shape
    return pl.pallas_call(
        functools.partial(hidden_kernel, cap, k),
        out_shape=jax.ShapeDtypeStruct((h, slots // 2), bf16),
        in_specs=[on_scalar, anywhere, anywhere],
        out_specs=on_chip,
        scratch_shapes=[pltpu.VMEM((2, slots // 2, h), bf16), pltpu.SemaphoreType.DMA((slots // cap,))],
        cost_estimate=light,
        compiler_params=params(16),
        name="hidden",
    )(here, in_hbm(gate), in_hbm(up))


def turn_kernel(cap, here, v, out, held):
    rows = held.shape[0]
    for k in range(2):
        plane = lax.rem(here[0] + k, 2)
        for q in range(rows // cap):
            held[q * cap : (q + 1) * cap, :] = v[pl.ds(pl.multiple_of((2 * q + plane) * cap, 16), cap), :]
        out[:, k * rows : (k + 1) * rows] = held[...].T


def turn(here, v, cap):
    slots, d = v.shape
    tile = 256
    return pl.pallas_call(
        functools.partial(turn_kernel, cap),
        out_shape=jax.ShapeDtypeStruct((d, slots), v.dtype),
        grid_spec=pltpu.PrefetchScalarGridSpec(
            num_scalar_prefetch=1,
            grid=(d // tile,),
            in_specs=[pl.BlockSpec((slots, tile), lambda i, here: (0, i))],
            out_specs=pl.BlockSpec((tile, slots), lambda i, here: (i, 0)),
            scratch_shapes=[pltpu.VMEM((slots // 2, tile), v.dtype)],
        ),
        cost_estimate=light,
        compiler_params=params(12),
        name="turn",
    )(here, in_hbm(v))


def pack_kernel(line, tokens, routes, codes, out, named, sems):
    tok = tokens.shape[0]
    copies = [
        pltpu.make_async_copy(tokens, out.at[:tok, :], sems.at[0]),
        pltpu.make_async_copy(routes, named.at[0], sems.at[1]),
        pltpu.make_async_copy(codes, named.at[1], sems.at[2]),
    ]
    for c in copies:
        c.start()
    out[tok:, :] = jnp.zeros((8, out.shape[1]), bf16)
    for k, at in enumerate((0, line)):
        copies[1 + k].wait()
        out[tok:, at : at + tok] = named[k].astype(f32).astype(bf16)
    copies[0].wait()


def pack(tokens, routes, codes, line):
    tok, d = tokens.shape
    return pl.pallas_call(
        functools.partial(pack_kernel, line),
        out_shape=jax.ShapeDtypeStruct((tok + 8, d), bf16),
        in_specs=[anywhere] * 3,
        out_specs=on_chip,
        scratch_shapes=[pltpu.VMEM((2, *routes.shape), jnp.int32), pltpu.SemaphoreType.DMA((3,))],
        cost_estimate=light,
        compiler_params=params(8),
        name="pack",
    )(in_hbm(tokens), in_hbm(routes), in_hbm(codes))


def received_own_kernel(hid, own, out):
    out[...] = jnp.dot(hid[...], own[...], preferred_element_type=f32)


def received_own(hid, own):
    return pl.pallas_call(
        received_own_kernel,
        out_shape=jax.ShapeDtypeStruct((hid.shape[0], own.shape[1]), f32),
        in_specs=[on_chip] * 2,
        out_specs=on_chip,
        cost_estimate=light,
        compiler_params=params(16),
        name="received_own",
    )(hid, own)


def received_other_kernel(part, hid, other, out, tiles, sems):
    count, tile, h = tiles.shape
    copies = []
    for i in range(count):
        at = slice(i * tile, (i + 1) * tile)
        total = part[:, at] + jnp.dot(hid[...], other[:, at], preferred_element_type=f32)
        tiles[i] = (total * loss_scale).astype(bf16).T
        copies.append(pltpu.make_async_copy(tiles.at[i], out.at[0, at, pl.ds(2 * h, h)], sems.at[i]))
        copies[-1].start()
    for c in copies:
        c.wait()


def received_other(part, hid, other):
    h, d = part.shape
    tile = 256
    return pl.pallas_call(
        received_other_kernel,
        out_shape=jax.ShapeDtypeStruct((1, d, 3 * h), bf16),
        in_specs=[on_chip] * 3,
        out_specs=anywhere,
        scratch_shapes=[pltpu.VMEM((d // tile, tile, h), bf16), pltpu.SemaphoreType.DMA((d // tile,))],
        cost_estimate=light,
        compiler_params=params(16),
        name="received_other",
    )(part, hid, other)


def inputs_kernel(cap, last, here, old, inputs, own, other, late, out, held, tiles, sems):
    rows, wide = own.shape
    count, tile, _ = tiles.shape
    held[...] = other[...]
    held[plane_rows(here[0], *last, cap), :] = late[...]
    copies = []
    for i in range(count):
        at = slice(i * tile, (i + 1) * tile)
        part = jnp.dot(inputs[at, :rows], own[...], preferred_element_type=f32)
        part = part + jnp.dot(inputs[at, rows:], held[...], preferred_element_type=f32)
        tiles[i] = (part * loss_scale).astype(bf16)
        copies.append(pltpu.make_async_copy(tiles.at[i], out.at[0, at, pl.ds(0, wide)], sems.at[i]))
        copies[-1].start()
    for c in copies:
        c.wait()


def inputs_part(here, last, old, inputs, own, other, late, cap):
    d = inputs.shape[0]
    rows, wide = own.shape
    tile = 256
    return pl.pallas_call(
        functools.partial(inputs_kernel, cap, last),
        out_shape=jax.ShapeDtypeStruct(old.shape, bf16),
        in_specs=[on_scalar, anywhere] + [on_chip] * 4,
        out_specs=anywhere,
        scratch_shapes=[
            pltpu.VMEM((rows, wide), bf16),
            pltpu.VMEM((d // tile, tile, wide), bf16),
            pltpu.SemaphoreType.DMA((d // tile,)),
        ],
        input_output_aliases={1: 0},
        cost_estimate=light,
        compiler_params=params(20),
        name="inputs_part",
    )(here, old, inputs, own, other, late)


def together(*values):
    return lax.optimization_barrier(values)


def body_grid(out_grad, routes, gate_codes, w_gate, w_up, w_down, saved_inputs, saved_gate, saved_up):
    owners = lax.axis_size("expert")
    me = lax.axis_index("expert")
    to_core = [(i, i ^ 1) for i in range(owners)]
    to_x = [(i, i ^ 2) for i in range(owners)]
    tok, d = out_grad.shape
    choices = routes.shape[1]
    slots = saved_gate.shape[1]
    cap = slots // owners

    def send(v, perm):
        return lax.ppermute(v, "expert", perm)

    line = 256 * pl.cdiv(tok, 256)
    block = pack(out_grad, routes.T, gate_codes.T, line)
    here = me.reshape(1).astype(jnp.int32)

    def ring(v, hops=1):
        return send(v, [(i, (i + 4 * hops) % owners) for i in range(owners)])

    wd, sg, su = w_down[0], saved_gate[0], saved_up[0]
    wd_c, sg_c, su_c = [send(v, to_core) for v in (wd, sg, su)]

    half = slots // 2
    recs, gps = [], []

    def first(chunk, toks):
        recs[:], (share, *shares, pos) = (lambda a, b, *rest: ([a, b], rest))(
            *dispatch(here, chunk, toks, wd, wd_c, cap, half, recs)
        )
        return (chunk, share, pos), *shares

    def exchange(v):
        return lax.ppermute(v, "dp", [(0, 1), (1, 0)])

    def second(state, *peers, last=False):
        chunk, share, pos = state
        gps[:], sums = (lambda a, b, *rest: ([a, b], rest))(
            *combine(here, chunk, share, peers, pos, (sg, su), (sg_c, su_c), w, w_c, cap, half, gps, last)
        )
        return sums

    r1, x0 = ring(block), send(block, to_x)
    c0, h0 = first([(0, 0)], [block])
    w = join(w_gate[0], w_up[0])
    inputs = turn(here, saved_inputs[0], cap)
    hid = hidden(here, sg, su, cap, 0)
    r1, x0, h0, w, inputs, hid, sg_c, su_c = together(r1, x0, h0, w, inputs, hid, sg_c, su_c)
    r2, x1 = ring(r1), send(r1, to_x)
    h0, w_c = exchange(h0), send(w, to_core)
    c1, h1, g1 = first([(1, 0), (0, 1)], [x0, r1])
    h1 = exchange(h1)
    (t_r0,) = second(c0, h0)
    hid_c = hidden(here, sg, su, cap, 1)
    r2, x1, h1, g1, t_r0, hid_c = together(r2, x1, h1, g1, t_r0, hid_c)
    r3, x2 = ring(r2), send(r2, to_x)
    g1 = exchange(g1)
    c2, h2, g2 = first([(1, 1), (0, 2)], [x1, r2])
    h2 = exchange(h2)
    t_x0, t_r1 = second(c1, h1, g1)
    r3, x2, h2, g2, t_x0, t_r1 = together(r3, x2, h2, g2, t_x0, t_r1)
    x3, w1 = send(r3, to_x), ring(t_r1)
    g2 = exchange(g2)
    c3, h3, g3 = first([(1, 2), (0, 3)], [x2, r3])
    h3 = exchange(h3)
    t_x1, t_r2 = second(c2, h2, g2)
    x3, w1, h3, g3, t_x0, t_x1, t_r2 = together(x3, w1, h3, g3, t_x0, t_x1, t_r2)
    u1, b0 = ring(t_x1), send(t_x0, to_x)
    g3 = exchange(g3)
    c4, h4 = first([(1, 3)], [x3])
    h4 = exchange(h4)
    t_x2, t_r3 = second(c3, h3, g3)
    u1, b0, h4, t_x2, t_r3, rec_away, gp_away = together(u1, b0, h4, t_x2, t_r3, recs[1], gps[1])
    rec_c, gp_c = send(rec_away, to_core), send(gp_away, to_core)
    a0, a1, h4 = together(*add_halves(t_x2, u1), h4)
    b2 = [send(a0, to_x), send(a1, to_x)]
    left, right = second(c4, h4, last=True)
    b3 = [send(left, to_x), send(right, to_x)]
    late = send(gps[1], to_core)
    part = received_own(hid, recs[0])
    b2[0], _, part, rec_c = together(b2[0], left, part, rec_c)
    w2 = [ring(add([t_r2, w1, b2[k]], k)) for k in range(2)]
    w2[0], _ = together(w2[0], b3[1])
    w3 = [ring(add([t_r3, b3[k], w2[k]], k)) for k in range(2)]
    part = received_other(part, hid_c, rec_c)
    weight_grads = inputs_part(here, (1, 3), part, inputs, gps[0], gp_c, late, cap)
    w3[1], weight_grads = together(w3[1], weight_grads)
    return (finish(t_r0, b0, *w3), weight_grads)


def solution(mesh):
    placed = (
        P("expert", "dp"),
        P("expert", None),
        P("expert", None),
        P("expert", "dp", None),
        P("expert", "dp", None),
        P("expert", None, "dp"),
        P("expert", None, "dp"),
        P("expert", None, None),
        P("expert", None, None),
    )
    small = mesh.shape["expert"] == 16 and mesh.shape["dp"] == 2
    return jax.shard_map(
        body_grid if small else body_any,
        mesh=mesh,
        in_specs=placed,
        out_specs=(P("expert", "dp"), P("expert", "dp", None)),
        check_vma=False,
    )
```

```python
import functools

import jax
import jax.numpy as jnp
from jax import lax
from jax.experimental import pallas as pl
from jax.experimental.pallas import tpu as pltpu
from jax.sharding import PartitionSpec as P

gate_unit = 0.00390625
loss_scale = 0.015625
f32 = jnp.float32
bf16 = jnp.bfloat16


def contract_rows(left, right):
    return lax.dot_general(left, right, (((0,), (0,)), ((), ())), preferred_element_type=f32)


def contract_cols(left, right):
    return lax.dot_general(left, right, (((1,), (1,)), ((), ())), preferred_element_type=f32)


def activation_grads(grad_hidden, gate_pre, up_pre):
    sigmoid = jax.nn.sigmoid(gate_pre)
    silu = gate_pre * sigmoid
    dsilu = sigmoid * (1.0 + gate_pre * (1.0 - sigmoid))
    grad_gate_pre = (grad_hidden * up_pre * dsilu).astype(bf16)
    grad_up_pre = (grad_hidden * silu).astype(bf16)
    return (grad_gate_pre, grad_up_pre)


def sigmoid_of(x):
    return 0.5 * jnp.tanh(0.5 * x) + 0.5


def kernel_grads(grad_hidden, gate_pre, up_pre):
    sigmoid = sigmoid_of(gate_pre)
    silu = gate_pre * sigmoid
    dsilu = sigmoid + silu * (1.0 - sigmoid)
    return ((grad_hidden * up_pre * dsilu).astype(bf16), (grad_hidden * silu).astype(bf16))


def body_any(out_grad, routes, gate_codes, w_gate, w_up, w_down, saved_inputs, saved_gate, saved_up):
    owners = lax.axis_size("expert")
    slot_count = saved_gate.shape[1]
    capacity = slot_count // owners
    token_count = routes.shape[0]
    choice_count = routes.shape[1]
    flat_routes = routes.reshape(-1)
    onehot = (flat_routes[:, None] == jnp.arange(owners, dtype=jnp.int32)[None, :]).astype(jnp.int32)
    earlier = jnp.cumsum(onehot, axis=0) - onehot
    position = jnp.sum(earlier * onehot, axis=1)
    slot_index = (flat_routes * capacity + position).reshape(token_count, choice_count)
    gate_values = gate_codes.astype(f32) * gate_unit
    rows_iota = jnp.arange(slot_count, dtype=jnp.int32)[:, None]
    weighted = jnp.zeros((slot_count, token_count), f32)
    picks = jnp.zeros((slot_count, token_count), f32)
    for pick in range(choice_count):
        hit = rows_iota == slot_index[:, pick][None, :]
        weighted = weighted + jnp.where(hit, gate_values[:, pick][None, :], 0.0)
        picks = picks + hit.astype(f32)
    outgoing = jnp.dot(weighted.astype(bf16), out_grad, preferred_element_type=f32).astype(bf16)
    received = lax.all_to_all(outgoing, "expert", split_axis=0, concat_axis=0, tiled=True)
    hidden_share = lax.psum_scatter(
        contract_cols(received, w_down[0]), "dp", scatter_dimension=0, tiled=True
    )
    gate_pre = saved_gate[0].astype(f32)
    up_pre = saved_up[0].astype(f32)
    hidden = (gate_pre * jax.nn.sigmoid(gate_pre) * up_pre).astype(bf16)
    grad_hidden = lax.all_gather(hidden_share, "dp", axis=0, tiled=True)
    grad_gate_pre, grad_up_pre = activation_grads(grad_hidden, gate_pre, up_pre)
    slot_grads = contract_cols(grad_gate_pre, w_gate[0]) + contract_cols(grad_up_pre, w_up[0])
    returned = lax.all_to_all(
        slot_grads.astype(bf16), "expert", split_axis=0, concat_axis=0, tiled=True
    )
    token_grads = contract_rows(picks.astype(bf16), returned).astype(bf16)
    inputs_here = saved_inputs[0]
    part = jnp.concatenate(
        [
            contract_rows(inputs_here, grad_gate_pre),
            contract_rows(inputs_here, grad_up_pre),
            contract_rows(received, hidden),
        ],
        axis=1,
    )
    return (token_grads, (part * loss_scale).astype(bf16)[None])


on_chip = pl.BlockSpec(memory_space=pltpu.VMEM)
on_scalar = pl.BlockSpec(memory_space=pltpu.SMEM)
anywhere = pl.BlockSpec(memory_space=pl.ANY)
light = pl.CostEstimate(flops=1 << 20, bytes_accessed=1 << 14, transcendentals=0)


def source(here, step, other):
    group = lax.rem(here // 4 + (4 - step), 4)
    return jnp.bitwise_xor(group * 4 + lax.rem(here, 4), 2 * other)


def params(mib):
    return pltpu.CompilerParams(vmem_limit_bytes=mib << 20)


def plane_rows(here, other, step, cap):
    return pl.ds(pl.multiple_of((source(here, step, other) // 2) * cap, 16), cap)


def dispatch_kernel(chunk, cap, begun, here, *refs):
    n = len(chunk)
    toks, (wd0, wd1) = refs[:n], refs[n : n + 2]
    buf0, buf1, share, *share_out, pos_out, rec, sems = refs[n + 2 + 2 * begun :]
    tok = toks[0].shape[0] - 8
    line = 256 * pl.cdiv(tok, 256)
    before = lax.broadcasted_iota(jnp.int32, (tok, tok), 0) < lax.broadcasted_iota(jnp.int32, (tok, tok), 1)
    before = jnp.where(before, 1.0, 0.0).astype(bf16)
    slot = lax.broadcasted_iota(jnp.int32, (cap, tok), 0).astype(f32)
    masks, gates = [], []
    for a in range(2):
        expert = jnp.bitwise_xor(here[0], a).astype(f32)
        for t in toks:
            hit = t[tok:, :tok].astype(f32) == expert
            masks.append(jnp.max(jnp.where(hit, 1.0, 0.0), axis=0, keepdims=True))
            gates.append(jnp.sum(jnp.where(hit, t[tok:, line : line + tok].astype(f32), 0.0), axis=0, keepdims=True))
    fill = [jnp.zeros((8 - 2 * n, tok), f32)] if n < 4 else []
    mask = jnp.concatenate(masks + fill, axis=0)
    pos = jnp.dot(mask.astype(bf16), before, preferred_element_type=f32)
    pos = jnp.where(mask > 0.0, pos, -1.0)
    pos_out[...] = pos
    copies = []
    for rel, t in enumerate(toks):
        w = [
            jnp.where(slot == pos[i : i + 1, :], gates[i] * gate_unit, 0.0).astype(bf16)
            for i in (rel, n + rel)
        ]
        rows = jnp.dot(jnp.concatenate(w, axis=0), t[:tok, :], preferred_element_type=f32).astype(bf16)
        at = pl.ds(rel * cap, cap)
        for a, buf in enumerate((buf0, buf1)):
            rec[a, at, :] = rows[a * cap : (a + 1) * cap]
            to = plane_rows(here[0], *chunk[rel], cap)
            copies.append(pltpu.make_async_copy(rec.at[a, at, :], buf.at[to, :], sems.at[len(copies)]))
    for c in copies:
        c.start()
    for a, wd in enumerate((wd0, wd1)):
        gh = contract_cols(rec[a], wd[...])
        share[a * n * cap : (a + 1) * n * cap, :] = gh
        if n == 1:
            share_out[0][a * cap : (a + 1) * cap, :] = gh.astype(bf16)
        else:
            share_out[a][...] = gh.astype(bf16)
    for c in copies:
        c.wait()


def dispatch(here, chunk, toks, wd0, wd1, cap, rows, old):
    n = len(toks)
    tok, d = toks[0].shape
    h = wd0.shape[0]
    outs = [((rows, d), bf16)] * 2 + [((2 * n * cap, h), f32)]
    outs += [((2 * cap, h), bf16)] if n == 1 else [((n * cap, h), bf16)] * 2
    outs += [((8, tok - 8), f32)]
    return pl.pallas_call(
        functools.partial(dispatch_kernel, chunk, cap, len(old) // 2),
        out_shape=[jax.ShapeDtypeStruct(s, t) for s, t in outs],
        in_specs=[on_scalar] + [on_chip] * (n + 2) + [anywhere] * len(old),
        out_specs=[anywhere] * 2 + [on_chip] * (len(outs) - 2),
        scratch_shapes=[pltpu.VMEM((2, n * cap, d), bf16), pltpu.SemaphoreType.DMA((2 * n,))],
        input_output_aliases={n + 3 + k: k for k in range(len(old))},
        cost_estimate=light,
        compiler_params=params(16),
        name="dispatch",
    )(here, *toks, wd0, wd1, *old)


def combine_kernel(chunk, cap, begun, last, here, share, *refs):
    n = len(chunk)
    if n == 1:
        peer0, peer1 = refs[0].at[:cap, :], refs[0].at[cap:, :]
        pos, *refs = refs[1:]
    else:
        peer0, peer1, pos, *refs = refs
    saved, ws, refs = refs[:4], refs[4:6], refs[6 + begun :]
    count = 3 if last else 2
    buffers, backs, (gps, out_sems) = refs[:count], refs[count:-2], refs[-2:]
    h = share.shape[1]
    slot = lax.broadcasted_iota(jnp.int32, (cap, pos.shape[1]), 0).astype(f32)
    leaving = []
    for a, peer in enumerate((peer0, peer1)):
        for rel in range(n):
            i = a * n + rel
            at = slice(rel * cap, (rel + 1) * cap)
            gh = share[i * cap : (i + 1) * cap, :] + peer[at, :].astype(f32)
            other, step = chunk[rel]
            own = pl.ds(pl.multiple_of(source(here[0], step, other) * cap, 16), cap)
            gg, gu = kernel_grads(gh, saved[2 * a][own, :].astype(f32), saved[2 * a + 1][own, :].astype(f32))
            gps[a, at, :h] = gg
            gps[a, at, h:] = gu
            if a == 0 or not last:
                to = buffers[a].at[plane_rows(here[0], *chunk[rel], cap), :]
                leaving.append(pltpu.make_async_copy(gps.at[a, at, :], to, out_sems.at[i]))
    for c in leaving:
        c.start()
    if last:
        buffers[1][...] = gps[1, :, :h]
        buffers[2][...] = gps[1, :, h:]
    sums = [None] * n
    for a, w in enumerate(ws):
        slots = contract_cols(gps[a], w[...]).astype(bf16)
        for rel in range(n):
            i = a * n + rel
            pick = jnp.where(slot == pos[i : i + 1, :], 1.0, 0.0).astype(bf16)
            part = contract_rows(pick, slots[rel * cap : (rel + 1) * cap])
            sums[rel] = part if sums[rel] is None else sums[rel] + part
    if len(backs) > n:
        half = backs[0].shape[1]
        for k, back in enumerate(backs):
            back[...] = sums[0][:, k * half : (k + 1) * half].astype(bf16)
    else:
        for rel in range(n):
            backs[rel][...] = sums[rel].astype(bf16)
    for c in leaving:
        c.wait()


def combine(here, chunk, share, peers, pos, saved0, saved1, w0, w1, cap, rows, old, last=False):
    n = len(chunk)
    h = share.shape[1]
    d = w0.shape[0]
    tok = pos.shape[1]
    old = old[:1] if last else old
    outs = [(rows, 2 * h)] + ([(n * cap, h)] * 2 if last else [(rows, 2 * h)]) + ([(tok, d // 2)] * 2 if last else [(tok, d)] * n)
    first_old = 2 + len(peers) + 1 + 4 + 2
    return pl.pallas_call(
        functools.partial(combine_kernel, chunk, cap, len(old), last),
        out_shape=[jax.ShapeDtypeStruct(s, bf16) for s in outs],
        in_specs=[on_scalar] + [on_chip] * (2 + len(peers) + 6) + [anywhere] * len(old),
        out_specs=[anywhere] * (1 if last else 2) + [on_chip] * (len(outs) - (1 if last else 2)),
        scratch_shapes=[
            pltpu.VMEM((2, n * cap, 2 * h), bf16),
            pltpu.SemaphoreType.DMA((2 * n,)),
        ],
        input_output_aliases={first_old + k: k for k in range(len(old))},
        cost_estimate=light,
        compiler_params=params(20),
        name="combine",
    )(here, share, *peers, pos, *saved0, *saved1, w0, w1, *old)


def join_kernel(left, right, out):
    out[:, : left.shape[1]] = left[...]
    out[:, left.shape[1] :] = right[...]


def join(left, right):
    rows, h = left.shape
    return pl.pallas_call(
        join_kernel,
        out_shape=jax.ShapeDtypeStruct((rows, 2 * h), left.dtype),
        in_specs=[on_chip] * 2,
        out_specs=on_chip,
        cost_estimate=light,
        compiler_params=params(8),
        name="join",
    )(left, right)


def add_kernel(part, *refs):
    wide = refs[-1].shape[1]
    total = None
    for r in refs[:-1]:
        v = r[...] if part is None or r.shape[1] == wide else r[:, part * wide : (part + 1) * wide]
        total = v.astype(f32) if total is None else total + v.astype(f32)
    refs[-1][...] = total.astype(bf16)


def add(values, part=None):
    rows, wide = values[0].shape
    return pl.pallas_call(
        functools.partial(add_kernel, part),
        out_shape=jax.ShapeDtypeStruct((rows, wide if part is None else wide // 2), bf16),
        in_specs=[on_chip] * len(values),
        out_specs=on_chip,
        cost_estimate=light,
        compiler_params=params(8),
        name="add",
    )(*values)


def add_halves_kernel(a, b, left, right):
    total = (a[...].astype(f32) + b[...].astype(f32)).astype(bf16)
    left[...] = total[:, : left.shape[1]]
    right[...] = total[:, left.shape[1] :]


def add_halves(a, b):
    rows, wide = a.shape
    return pl.pallas_call(
        add_halves_kernel,
        out_shape=[jax.ShapeDtypeStruct((rows, wide // 2), bf16)] * 2,
        in_specs=[on_chip] * 2,
        out_specs=[on_chip] * 2,
        cost_estimate=light,
        compiler_params=params(8),
        name="add_halves",
    )(a, b)


def finish_kernel(a, b, left, right, out):
    half = left.shape[1]
    for at, v in ((0, left), (half, right)):
        total = a[:, at : at + half].astype(f32) + b[:, at : at + half].astype(f32) + v[...].astype(f32)
        out[:, at : at + half] = total.astype(bf16)


def finish(a, b, left, right):
    return pl.pallas_call(
        finish_kernel,
        out_shape=jax.ShapeDtypeStruct(a.shape, bf16),
        in_specs=[on_chip] * 4,
        out_specs=on_chip,
        cost_estimate=light,
        compiler_params=params(8),
        name="finish",
    )(a, b, left, right)


def in_hbm(v):
    return pltpu.with_memory_space_constraint(v, pltpu.HBM)


def hidden_kernel(cap, k, here, gate, up, out, held, sems):
    plane = lax.rem(here[0] + k, 2)
    copies = []
    for i, v in enumerate((gate, up)):
        for q in range(held.shape[1] // cap):
            at = pl.ds(pl.multiple_of((2 * q + plane) * cap, 16), cap)
            to = held.at[i, pl.ds(q * cap, cap), :]
            copies.append(pltpu.make_async_copy(v.at[at, :], to, sems.at[len(copies)]))
    for c in copies:
        c.start()
    for c in copies:
        c.wait()
    gate_pre = held[0].astype(f32)
    out[...] = (gate_pre * sigmoid_of(gate_pre) * held[1].astype(f32)).astype(bf16).T


def hidden(here, gate, up, cap, k):
    slots, h = gate.shape
    return pl.pallas_call(
        functools.partial(hidden_kernel, cap, k),
        out_shape=jax.ShapeDtypeStruct((h, slots // 2), bf16),
        in_specs=[on_scalar, anywhere, anywhere],
        out_specs=on_chip,
        scratch_shapes=[pltpu.VMEM((2, slots // 2, h), bf16), pltpu.SemaphoreType.DMA((slots // cap,))],
        cost_estimate=light,
        compiler_params=params(16),
        name="hidden",
    )(here, in_hbm(gate), in_hbm(up))


def turn_kernel(cap, here, v, out, held):
    rows = held.shape[0]
    for k in range(2):
        plane = lax.rem(here[0] + k, 2)
        for q in range(rows // cap):
            held[q * cap : (q + 1) * cap, :] = v[pl.ds(pl.multiple_of((2 * q + plane) * cap, 16), cap), :]
        out[:, k * rows : (k + 1) * rows] = held[...].T


def turn(here, v, cap):
    slots, d = v.shape
    tile = 256
    return pl.pallas_call(
        functools.partial(turn_kernel, cap),
        out_shape=jax.ShapeDtypeStruct((d, slots), v.dtype),
        grid_spec=pltpu.PrefetchScalarGridSpec(
            num_scalar_prefetch=1,
            grid=(d // tile,),
            in_specs=[pl.BlockSpec((slots, tile), lambda i, here: (0, i))],
            out_specs=pl.BlockSpec((tile, slots), lambda i, here: (i, 0)),
            scratch_shapes=[pltpu.VMEM((slots // 2, tile), v.dtype)],
        ),
        cost_estimate=light,
        compiler_params=params(12),
        name="turn",
    )(here, in_hbm(v))


def pack_kernel(line, tokens, routes, codes, out, named, sems):
    tok = tokens.shape[0]
    copies = [
        pltpu.make_async_copy(tokens, out.at[:tok, :], sems.at[0]),
        pltpu.make_async_copy(routes, named.at[0], sems.at[1]),
        pltpu.make_async_copy(codes, named.at[1], sems.at[2]),
    ]
    for c in copies:
        c.start()
    out[tok:, :] = jnp.zeros((8, out.shape[1]), bf16)
    for k, at in enumerate((0, line)):
        copies[1 + k].wait()
        out[tok:, at : at + tok] = named[k].astype(f32).astype(bf16)
    copies[0].wait()


def pack(tokens, routes, codes, line):
    tok, d = tokens.shape
    return pl.pallas_call(
        functools.partial(pack_kernel, line),
        out_shape=jax.ShapeDtypeStruct((tok + 8, d), bf16),
        in_specs=[anywhere] * 3,
        out_specs=on_chip,
        scratch_shapes=[pltpu.VMEM((2, *routes.shape), jnp.int32), pltpu.SemaphoreType.DMA((3,))],
        cost_estimate=light,
        compiler_params=params(8),
        name="pack",
    )(in_hbm(tokens), in_hbm(routes), in_hbm(codes))


def received_own_kernel(hid, own, out):
    out[...] = jnp.dot(hid[...], own[...], preferred_element_type=f32)


def received_own(hid, own):
    return pl.pallas_call(
        received_own_kernel,
        out_shape=jax.ShapeDtypeStruct((hid.shape[0], own.shape[1]), f32),
        in_specs=[on_chip] * 2,
        out_specs=on_chip,
        cost_estimate=light,
        compiler_params=params(16),
        name="received_own",
    )(hid, own)


def received_other_kernel(part, hid, other, out, tiles, sems):
    count, tile, h = tiles.shape
    copies = []
    for i in range(count):
        at = slice(i * tile, (i + 1) * tile)
        total = part[:, at] + jnp.dot(hid[...], other[:, at], preferred_element_type=f32)
        tiles[i] = (total * loss_scale).astype(bf16).T
        copies.append(pltpu.make_async_copy(tiles.at[i], out.at[0, at, pl.ds(2 * h, h)], sems.at[i]))
        copies[-1].start()
    for c in copies:
        c.wait()


def received_other(part, hid, other):
    h, d = part.shape
    tile = 256
    return pl.pallas_call(
        received_other_kernel,
        out_shape=jax.ShapeDtypeStruct((1, d, 3 * h), bf16),
        in_specs=[on_chip] * 3,
        out_specs=anywhere,
        scratch_shapes=[pltpu.VMEM((d // tile, tile, h), bf16), pltpu.SemaphoreType.DMA((d // tile,))],
        cost_estimate=light,
        compiler_params=params(16),
        name="received_other",
    )(part, hid, other)


def inputs_kernel(cap, last, here, old, inputs, own, other, late0, late1, out, held, tiles, sems):
    rows, wide = own.shape
    count, tile, _ = tiles.shape
    held[...] = other[...]
    at = plane_rows(here[0], *last, cap)
    held[at, : wide // 2] = late0[...]
    held[at, wide // 2 :] = late1[...]
    copies = []
    for i in range(count):
        at = slice(i * tile, (i + 1) * tile)
        part = jnp.dot(inputs[at, :rows], own[...], preferred_element_type=f32)
        part = part + jnp.dot(inputs[at, rows:], held[...], preferred_element_type=f32)
        tiles[i] = (part * loss_scale).astype(bf16)
        copies.append(pltpu.make_async_copy(tiles.at[i], out.at[0, at, pl.ds(0, wide)], sems.at[i]))
        copies[-1].start()
    for c in copies:
        c.wait()


def inputs_part(here, last, old, inputs, own, other, late0, late1, cap):
    d = inputs.shape[0]
    rows, wide = own.shape
    tile = 256
    return pl.pallas_call(
        functools.partial(inputs_kernel, cap, last),
        out_shape=jax.ShapeDtypeStruct(old.shape, bf16),
        in_specs=[on_scalar, anywhere] + [on_chip] * 5,
        out_specs=anywhere,
        scratch_shapes=[
            pltpu.VMEM((rows, wide), bf16),
            pltpu.VMEM((d // tile, tile, wide), bf16),
            pltpu.SemaphoreType.DMA((d // tile,)),
        ],
        input_output_aliases={1: 0},
        cost_estimate=light,
        compiler_params=params(20),
        name="inputs_part",
    )(here, old, inputs, own, other, late0, late1)


def together(*values):
    return lax.optimization_barrier(values)


def body_grid(out_grad, routes, gate_codes, w_gate, w_up, w_down, saved_inputs, saved_gate, saved_up):
    owners = lax.axis_size("expert")
    me = lax.axis_index("expert")
    to_core = [(i, i ^ 1) for i in range(owners)]
    to_x = [(i, i ^ 2) for i in range(owners)]
    tok, d = out_grad.shape
    choices = routes.shape[1]
    slots = saved_gate.shape[1]
    cap = slots // owners

    def send(v, perm):
        return lax.ppermute(v, "expert", perm)

    line = 256 * pl.cdiv(tok, 256)
    block = pack(out_grad, routes.T, gate_codes.T, line)
    here = me.reshape(1).astype(jnp.int32)

    def ring(v, hops=1):
        return send(v, [(i, (i + 4 * hops) % owners) for i in range(owners)])

    wd, sg, su = w_down[0], saved_gate[0], saved_up[0]
    wd_c, sg_c, su_c = [send(v, to_core) for v in (wd, sg, su)]

    half = slots // 2
    recs, gps = [], []

    def first(chunk, toks):
        recs[:], (share, *shares, pos) = (lambda a, b, *rest: ([a, b], rest))(
            *dispatch(here, chunk, toks, wd, wd_c, cap, half, recs)
        )
        return (chunk, share, pos), *shares

    def exchange(v):
        return lax.ppermute(v, "dp", [(0, 1), (1, 0)])

    def second(state, *peers, last=False):
        chunk, share, pos = state
        gps[:], sums = (lambda a, b, *rest: ([a, b], rest))(
            *combine(here, chunk, share, peers, pos, (sg, su), (sg_c, su_c), w, w_c, cap, half, gps, last)
        )
        return sums

    r1, x0 = ring(block), send(block, to_x)
    c0, h0 = first([(0, 0)], [block])
    w = join(w_gate[0], w_up[0])
    inputs = turn(here, saved_inputs[0], cap)
    hid = hidden(here, sg, su, cap, 0)
    r1, x0, h0, w, inputs, hid, sg_c, su_c = together(r1, x0, h0, w, inputs, hid, sg_c, su_c)
    r2, x1 = ring(r1), send(r1, to_x)
    h0, w_c = exchange(h0), send(w, to_core)
    c1, h1, g1 = first([(1, 0), (0, 1)], [x0, r1])
    h1 = exchange(h1)
    (t_r0,) = second(c0, h0)
    hid_c = hidden(here, sg, su, cap, 1)
    r2, x1, h1, g1, t_r0, hid_c = together(r2, x1, h1, g1, t_r0, hid_c)
    r3, x2 = ring(r2), send(r2, to_x)
    g1 = exchange(g1)
    c2, h2, g2 = first([(1, 1), (0, 2)], [x1, r2])
    h2 = exchange(h2)
    t_x0, t_r1 = second(c1, h1, g1)
    r3, x2, h2, g2, t_x0, t_r1 = together(r3, x2, h2, g2, t_x0, t_r1)
    x3, w1 = send(r3, to_x), ring(t_r1)
    g2 = exchange(g2)
    c3, h3, g3 = first([(1, 2), (0, 3)], [x2, r3])
    h3 = exchange(h3)
    t_x1, t_r2 = second(c2, h2, g2)
    x3, w1, h3, g3, t_x0, t_x1, t_r2 = together(x3, w1, h3, g3, t_x0, t_x1, t_r2)
    u1, b0 = ring(t_x1), send(t_x0, to_x)
    g3 = exchange(g3)
    c4, h4 = first([(1, 3)], [x3])
    h4 = exchange(h4)
    t_x2, t_r3 = second(c3, h3, g3)
    u1, b0, h4, t_x2, t_r3, rec_away, gp_away = together(u1, b0, h4, t_x2, t_r3, recs[1], gps[1])
    rec_c, gp_c = send(rec_away, to_core), send(gp_away, to_core)
    a0, a1, h4 = together(*add_halves(t_x2, u1), h4)
    b2 = [send(a0, to_x), send(a1, to_x)]
    late, left, right = second(c4, h4, last=True)
    b3 = [send(left, to_x), send(right, to_x)]
    late = [send(gps[1], to_core), send(late, to_core)]
    part = received_own(hid, recs[0])
    b2[0], _, part, rec_c = together(b2[0], left, part, rec_c)
    w2 = [ring(add([t_r2, w1, b2[k]], k)) for k in range(2)]
    w2[0], _ = together(w2[0], b3[1])
    w3 = [ring(add([t_r3, b3[k], w2[k]], k)) for k in range(2)]
    part = received_other(part, hid_c, rec_c)
    weight_grads = inputs_part(here, (1, 3), part, inputs, gps[0], gp_c, *late, cap)
    w3[1], weight_grads = together(w3[1], weight_grads)
    return (finish(t_r0, b0, *w3), weight_grads)


def solution(mesh):
    placed = (
        P("expert", "dp"),
        P("expert", None),
        P("expert", None),
        P("expert", "dp", None),
        P("expert", "dp", None),
        P("expert", None, "dp"),
        P("expert", None, "dp"),
        P("expert", None, None),
        P("expert", None, None),
    )
    small = mesh.shape["expert"] == 16 and mesh.shape["dp"] == 2
    return jax.shard_map(
        body_grid if small else body_any,
        mesh=mesh,
        in_specs=placed,
        out_specs=(P("expert", "dp"), P("expert", "dp", None)),
        check_vma=False,
    )
```
